32 devices in a mesh: seq: 8 (over y, x, core), tp: 4 (over z).
Axes of the slice: x: 2, y: 2, z: 4, core: 2. Of those that a mesh axis runs over, the one named last changes fastest.
Arguments:
- hidden: bfloat16 [4096, 4096], P('seq', 'tp'), may hold values from -6 to 6
- norm_gain: bfloat16 [4096], replicated, may hold values from 0.25 to 1.75
- gate_x_weight: bfloat16 [4096, 2, 4096], P(None, None, 'tp'), may hold values from -0.09375 to 0.09375
- state_weight: bfloat16 [4096, 2, 1024], P(None, None, 'tp'), may hold values from -0.09375 to 0.09375
- step_weight: bfloat16 [4096, 64], P(None, 'tp'), may hold values from -0.09375 to 0.09375
- conv_inner: bfloat16 [4, 4096], P(None, 'tp'), may hold values from -0.75 to 0.75
- conv_state: bfloat16 [4, 2, 1024], P(None, None, 'tp'), may hold values from -0.75 to 0.75
- step_bias: float32 [64], P('tp'), may hold values from -6 to -1.5
- decay_log: float32 [64], P('tp'), may hold values from -12 to 1
- skip_gain: float32 [64], P('tp'), may hold values from 0.1 to 0.5
- inner_gain: bfloat16 [4096], P('tp'), may hold values from 0.25 to 1.75
- out_weight: bfloat16 [4096, 4096], P('tp'), may hold values from -0.09375 to 0.09375
- initial_state: float32 [64, 64, 128], P('tp'), may hold values from -0.3 to 0.3
Outputs:
- new_hidden: bfloat16 [4096, 4096], P('seq', 'tp')
The draws below stay inside these ranges and needn't reach their ends.
All inputs are finite; a program needn't handle non-finite values.
Results may differ from the reference program's by a relative error of at most 0.009.
Values may be sent and summed in bfloat16 or wider, within the bound.
No kernel may reach another device: no remote copies, remote signals or barrier semaphores. Data moves between devices by JAX's collectives and lax.ppermute only.
A program may use at most 128 MiB of HBM per device.

```python
import math
import jax
import jax.numpy as jnp
from jax import lax

MODEL = 4096
HEADS = 64
HEAD_DIM = 64
GROUPS = 8
STATE = 128
CONV = 4
SPAN = 128
INNER = 4096
LENGTH = 4096


def head_rates(key):
    base = jax.random.fold_in(key, 7)
    pick_key, step_key, rate_key = jax.random.split(base, 3)
    picked = jax.random.uniform(pick_key, (HEADS,), jnp.float32)
    slow_heads = picked < 0.5
    step_draw = jax.random.uniform(step_key, (HEADS,), jnp.float32)
    rate_draw = jax.random.uniform(rate_key, (HEADS,), jnp.float32)
    slow_step = 0.003 * jnp.exp(step_draw * math.log(0.01 / 0.003))
    fast_step = 0.05 * jnp.exp(step_draw * math.log(4.0))
    step_base = jnp.where(slow_heads, slow_step, fast_step)
    slow_rate = 0.12 * jnp.exp(rate_draw * math.log(6.0)) / (LENGTH * step_base)
    fast_rate = 0.012 * jnp.exp(rate_draw * math.log(0.02 / 0.012)) / step_base
    coefficient = jnp.where(slow_heads, slow_rate, fast_rate)
    return (jnp.log(jnp.expm1(step_base)), jnp.log(coefficient))


def draw_step_bias(key, part):
    return head_rates(key)[0].astype(jnp.float32)


def draw_decay_log(key, part):
    return head_rates(key)[1].astype(jnp.float32)


def levels(own_key, dims, shards, smallest, largest):
    gain = 1.0
    for dim, shards_of in shards:
        steps = jax.random.uniform(jax.random.fold_in(jax.random.fold_in(own_key, 6), dim), (shards_of,), jnp.float32, smallest / len(shards), largest / len(shards))
        gain = gain * jnp.repeat(jnp.exp(steps), dims[dim] // shards_of).reshape((-1,) + (1,) * (len(dims) - 1 - dim))
    return gain


def scatter_about(stream_key, dims, scale, limit, cuts=(), kind=jnp.bfloat16):
    entries = jax.random.normal(stream_key, dims, jnp.float32) * scale
    if len(cuts) > 0:
        entries = levels(stream_key, dims, cuts, -0.22, 0.18) * entries
    return jnp.clip(entries, min=-limit, max=limit).astype(kind)


def setup_inputs(seed: int = 0) -> dict:
    key_of = jax.random.split(jax.random.key(seed), 14)
    hidden = scatter_about(key_of[0], (LENGTH, MODEL), 1.0, 6.0, ((0, 8), (1, 4)))
    norm_gain = jnp.clip(1.0 + 0.15 * jax.random.normal(key_of[1], (MODEL,), jnp.float32), 0.25, 1.75).astype(jnp.bfloat16)
    gate_x_weight = scatter_about(key_of[2], (MODEL, 2, INNER), MODEL ** -0.5, 0.09375, ((2, 4),))
    state_weight = scatter_about(key_of[3], (MODEL, 2, GROUPS * STATE), MODEL ** -0.5, 0.09375, ((2, 4),))
    step_weight = scatter_about(key_of[4], (MODEL, HEADS), MODEL ** -0.5, 0.09375, ((1, 4),))
    conv_inner = scatter_about(key_of[5], (CONV, INNER), (16 * CONV) ** -0.5, 0.75, ((1, 4),))
    conv_state = scatter_about(key_of[6], (CONV, 2, GROUPS * STATE), (16 * CONV) ** -0.5, 0.75, ((2, 4),))
    step_bias = draw_step_bias(jax.random.fold_in(key_of[13], 71), 0)
    decay_log = draw_decay_log(jax.random.fold_in(key_of[13], 71), 0)
    skip_gain = jnp.clip(0.1 + 0.4 * jax.random.uniform(key_of[9], (HEADS,), jnp.float32) ** levels(key_of[9], (HEADS,), ((0, 4),), -0.2, 0.2), 0.1, 0.5)
    inner_gain = jnp.clip(1.0 + 0.15 * jax.random.normal(key_of[10], (INNER,), jnp.float32), 0.25, 1.75).astype(jnp.bfloat16)
    out_weight = scatter_about(key_of[11], (INNER, MODEL), INNER ** -0.5, 0.09375, ((0, 4),))
    initial_state = scatter_about(key_of[12], (HEADS, HEAD_DIM, STATE), 0.05, 0.3, ((0, 4),), jnp.float32)
    return dict(hidden=hidden, norm_gain=norm_gain, gate_x_weight=gate_x_weight, state_weight=state_weight, step_weight=step_weight, conv_inner=conv_inner, conv_state=conv_state, step_bias=step_bias, decay_log=decay_log, skip_gain=skip_gain, inner_gain=inner_gain, out_weight=out_weight, initial_state=initial_state)


EPSILON = 1e-05
PRECISE = lax.Precision.HIGHEST

def causal_filter(padded, kernel, length):
    summed = kernel[0].astype(jnp.float32) * padded[0:length].astype(jnp.float32)
    for offset in range(1, kernel.shape[0]):
        summed = summed + kernel[offset].astype(jnp.float32) * padded[offset:offset + length].astype(jnp.float32)
    return jax.nn.silu(summed).astype(jnp.bfloat16)

def block_step(carried, inputs):
    memory, log_total = carried
    values, in_map, out_map, step_size, log_decay = inputs
    head_count = values.shape[1]
    group_count = in_map.shape[1]
    ratio_heads = head_count // group_count
    length = values.shape[0]
    row_pos = lax.broadcasted_iota(jnp.int32, (length, length), 0)
    col_pos = lax.broadcasted_iota(jnp.int32, (length, length), 1)
    causal = row_pos >= col_pos
    cumulative = jnp.cumsum(log_decay, axis=0)
    across = cumulative.T
    spread = across[:, :, None] - across[:, None, :]
    weights = jnp.where(causal[None], jnp.exp(jnp.where(causal[None], spread, 0.0)), 0.0)
    group_scores = jnp.einsum('tgn,sgn->gts', out_map, in_map, preferred_element_type=jnp.float32)
    scores = (weights.reshape(group_count, ratio_heads, length, length) * group_scores[:, None]).reshape(head_count, length, length)
    scaled = values * step_size[:, :, None]
    within = jnp.einsum('hts,shp->thp', scores, scaled, precision=PRECISE)
    in_heads = jnp.repeat(in_map.astype(jnp.float32), ratio_heads, axis=1)
    out_heads = jnp.repeat(out_map.astype(jnp.float32), ratio_heads, axis=1)
    from_memory = jnp.einsum('thn,hpn->thp', out_heads * jnp.exp(cumulative)[:, :, None], memory, precision=PRECISE)
    final_log = cumulative[-1]
    remaining = jnp.exp(final_log[None, :] - cumulative)
    update = jnp.einsum('shp,shn->hpn', scaled * remaining[:, :, None], in_heads, precision=PRECISE)
    new_memory = jnp.exp(final_log)[:, None, None] * memory + update
    return ((new_memory, log_total + final_log), (within + from_memory, cumulative + log_total[None, :]))

def run_blocks(values, in_map, out_map, step_size, log_decay, memory):
    blocks = values.shape[0] // SPAN

    def in_blocks(tensor):
        return tensor.reshape((blocks, SPAN) + tensor.shape[1:])
    start_total = jnp.zeros((values.shape[1],), jnp.float32)
    finals, traced = lax.scan(block_step, (memory, start_total), (in_blocks(values), in_blocks(in_map), in_blocks(out_map), in_blocks(step_size), in_blocks(log_decay)))
    outputs = traced[0].reshape(values.shape)
    cumulative = traced[1].reshape(step_size.shape)
    return (finals[0], finals[1], outputs, cumulative)

def reference(hidden, norm_gain, gate_x_weight, state_weight, step_weight, conv_inner, conv_state, step_bias, decay_log, skip_gain, inner_gain, out_weight, initial_state):
    hidden_wide = hidden.astype(jnp.float32)
    moments = lax.optimization_barrier(jnp.mean(hidden_wide * hidden_wide, axis=-1, keepdims=True))
    normed = (hidden_wide * lax.rsqrt(moments + EPSILON) * norm_gain.astype(jnp.float32)).astype(jnp.bfloat16)
    gate_and_x = jnp.dot(normed, gate_x_weight.reshape(MODEL, 2 * INNER), preferred_element_type=jnp.float32).astype(jnp.bfloat16).reshape(LENGTH, 2, INNER)
    state_raw = jnp.dot(normed, state_weight.reshape(MODEL, 2 * GROUPS * STATE), preferred_element_type=jnp.float32).astype(jnp.bfloat16).reshape(LENGTH, 2, GROUPS * STATE)
    step_raw = jnp.dot(normed, step_weight, preferred_element_type=jnp.float32).astype(jnp.bfloat16)
    rim_rows = CONV - 1
    inner_pad = jnp.concatenate([jnp.zeros((rim_rows, INNER), jnp.bfloat16), gate_and_x[:, 1]], axis=0)
    inner_conv = causal_filter(inner_pad, conv_inner, LENGTH)
    state_pad = jnp.concatenate([jnp.zeros((rim_rows, 2, GROUPS * STATE), jnp.bfloat16), state_raw], axis=0)
    state_conv = causal_filter(state_pad, conv_state, LENGTH)
    step_size = jax.nn.softplus(step_raw.astype(jnp.float32) + step_bias[None, :])
    log_decay = -step_size * jnp.exp(decay_log)[None, :]
    values = inner_conv.astype(jnp.float32).reshape(LENGTH, HEADS, HEAD_DIM)
    in_map = state_conv[:, 0].reshape(LENGTH, GROUPS, STATE)
    out_map = state_conv[:, 1].reshape(LENGTH, GROUPS, STATE)
    memory_end, total_end, outputs, cumulative = run_blocks(values, in_map, out_map, step_size, log_decay, initial_state)
    mixer_out = outputs + skip_gain[None, :, None] * values
    gated_out = mixer_out.reshape(LENGTH, INNER) * jax.nn.silu(gate_and_x[:, 0].astype(jnp.float32))
    grouped = gated_out.reshape(LENGTH, GROUPS, INNER // GROUPS)
    scale_rows = lax.rsqrt(lax.optimization_barrier(jnp.mean(grouped * grouped, axis=-1, keepdims=True)) + EPSILON)
    mixed_rows = ((grouped * scale_rows).reshape(LENGTH, INNER) * inner_gain.astype(jnp.float32)).astype(jnp.bfloat16)
    projected = jnp.dot(mixed_rows, out_weight, preferred_element_type=jnp.float32)
    return (projected + hidden_wide).astype(jnp.bfloat16)
```

```python
import jax
import jax.numpy as jnp
from jax import lax
from jax.experimental import pallas as pl
from jax.experimental.pallas import tpu as pltpu
from jax.sharding import PartitionSpec as P

SPAN = 128
EPSILON = 1e-05
TAIL = 16
LANES = 128
F32 = jnp.float32
BF16 = jnp.bfloat16


def shifted(block, axis, distance):
    count = lax.axis_size(axis)
    route = [(i, i + distance) for i in range(count) if 0 <= i + distance < count]
    return lax.ppermute(block, axis, route)


def swapped(block, axis, bit):
    return lax.ppermute(block, axis, [(i, i ^ bit) for i in range(lax.axis_size(axis))])


def line_gather(block, axis):
    count = lax.axis_size(axis)
    pieces = [(block, 0)]
    behind = ahead = block
    for step in range(1, count):
        behind = lax.ppermute(behind, axis, [(i, i + 1) for i in range(step - 1, count - 1)])
        ahead = lax.ppermute(ahead, axis, [(i, i - 1) for i in range(1, count - step + 1)])
        pieces += [(behind, -step), (ahead, step)]
    return pieces


def whole_spec(array):
    rank = len(array.shape)
    return pl.BlockSpec(array.shape, lambda *_: (0,) * rank)


def call(body, outs, *arrays, scratch=(), scalars=0, name=None):
    return pl.pallas_call(
        body,
        out_shape=outs,
        in_specs=[pl.BlockSpec(memory_space=pltpu.SMEM)] * scalars
        + [whole_spec(a) for a in arrays[scalars:]],
        out_specs=jax.tree.map(whole_spec, outs),
        scratch_shapes=list(scratch),
        name=name,
    )(*arrays)


def dot(a, b, contract=((1,), (0,))):
    return lax.dot_general(a, b, (contract, ((), ())), preferred_element_type=F32)


def parts_of(x, count):
    parts = []
    for _ in range(count):
        part = x.astype(BF16)
        parts.append(part)
        x = x - part.astype(F32)
    return parts


def spread(x, expand, count=2):
    total = None
    for part in parts_of(x, count):
        term = dot(part, expand)
        total = term if total is None else total + term
    return total


def expander(heads, width):
    head = lax.broadcasted_iota(jnp.int32, (heads, heads * width), 0)
    lane = lax.broadcasted_iota(jnp.int32, (heads, heads * width), 1)
    inside = jnp.logical_and(lane >= head * width, lane < (head + 1) * width)
    return jnp.where(inside, 1.0, 0.0).astype(BF16)


def silu(v):
    return v * (1.0 / (1.0 + jnp.exp(-v)))


def conv_block(padded_ref, start, taps_ref, columns):
    summed = None
    for k in range(taps_ref.shape[0]):
        row = 8 + start - (taps_ref.shape[0] - 1) + k
        term = taps_ref[k : k + 1, columns].astype(F32) * padded_ref[row : row + SPAN, columns]
        summed = term if summed is None else summed + term
    return silu(summed).astype(BF16)


def project_first(pieces, index, gain, wide_weight, narrow_weight, step_weight, inner, state):
    rows, width = pieces[0][0].shape
    model, heads = step_weight.shape[1], step_weight.shape[0]
    count = model // width
    wide_blocks = inner // state
    offsets = [offset for _, offset in pieces]

    def body(index_ref, gain_ref, *refs):
        parts = refs[: len(offsets)]
        wide_ref, narrow_ref, steps_ref, out_ref, step_ref, scaled_ref, scale_ref, square_ref = refs[
            len(offsets) :
        ]
        turn = pl.program_id(0)

        @pl.when(turn == 0)
        def _():
            square_ref[...] = jnp.zeros_like(square_ref)
            for part, offset in zip(parts, offsets):
                target = index_ref[0] + offset

                @pl.when(jnp.logical_and(target >= 0, target < count))
                def _():
                    def columns(k, carry):
                        here = pl.ds(pl.multiple_of(k * LANES, LANES), LANES)
                        there = pl.ds(pl.multiple_of(target * width + k * LANES, LANES), LANES)
                        value = part[:, here].astype(F32)
                        square_ref[...] += value * value
                        scaled_ref[:, there] = (value * gain_ref[:, there]).astype(BF16)
                        return carry

                    lax.fori_loop(0, width // LANES, columns, 0)

            moment = jnp.sum(square_ref[...], axis=-1, keepdims=True) * (1.0 / model)
            scale_ref[...] = jnp.broadcast_to(lax.rsqrt(moment + EPSILON), scale_ref.shape)
            raw = dot(scaled_ref[...], steps_ref[...], ((1,), (1,)))
            step_ref[...] = (raw * scale_ref[:, 0:heads]).astype(BF16)

        @pl.when(turn < wide_blocks)
        def _():
            raw = dot(scaled_ref[...], wide_ref[...])
            out_ref[...] = (raw * scale_ref[:, 0:1]).astype(BF16)

        @pl.when(turn == wide_blocks)
        def _():
            raw = dot(scaled_ref[...], narrow_ref[...])
            out_ref[...] = (raw * scale_ref[:, 0:1]).astype(BF16)

    shape = jax.ShapeDtypeStruct
    return pl.pallas_call(
        body,
        grid=(wide_blocks + 1,),
        out_shape=[
            shape((rows, inner + state), BF16),
            shape((rows, heads), BF16),
            shape((rows, model), BF16),
            shape((rows, LANES), F32),
        ],
        in_specs=[pl.BlockSpec(memory_space=pltpu.SMEM), whole_spec(gain)]
        + [whole_spec(piece) for piece, _ in pieces]
        + [
            pl.BlockSpec(
                (model, state),
                lambda j: (0, wide_blocks + jnp.minimum(j, wide_blocks - 1)),
            ),
            pl.BlockSpec((model, state), lambda j: (0, 0)),
            whole_spec(step_weight),
        ],
        out_specs=[
            pl.BlockSpec((rows, state), lambda j: (0, j)),
            pl.BlockSpec((rows, heads), lambda j: (0, 0)),
            pl.BlockSpec((rows, model), lambda j: (0, 0)),
            pl.BlockSpec((rows, LANES), lambda j: (0, 0)),
        ],
        scratch_shapes=[pltpu.VMEM((rows, LANES), F32)],
        name="project_first",
    )(index, gain, *[piece for piece, _ in pieces], wide_weight, narrow_weight, step_weight)


def project_second(scaled, scale, wide_weight, narrow_weight, inner, state):
    rows, model = scaled.shape
    wide_blocks = inner // state

    def body(scaled_ref, scale_ref, wide_ref, narrow_ref, out_ref):
        turn = pl.program_id(0)

        @pl.when(turn < wide_blocks)
        def _():
            raw = dot(scaled_ref[...], wide_ref[...])
            out_ref[...] = (raw * scale_ref[:, 0:1]).astype(BF16)

        @pl.when(turn == wide_blocks)
        def _():
            raw = dot(scaled_ref[...], narrow_ref[...])
            out_ref[...] = (raw * scale_ref[:, 0:1]).astype(BF16)

    return pl.pallas_call(
        body,
        grid=(wide_blocks + 1,),
        out_shape=jax.ShapeDtypeStruct((rows, inner + state), BF16),
        in_specs=[
            whole_spec(scaled),
            whole_spec(scale),
            pl.BlockSpec((model, state), lambda j: (0, jnp.minimum(j, wide_blocks - 1))),
            pl.BlockSpec((model, state), lambda j: (0, 1)),
        ],
        out_specs=pl.BlockSpec((rows, state), lambda j: (0, j)),
        name="project_second",
    )(scaled, scale, wide_weight, narrow_weight)


def state_body(inner, state, heads, groups):
    size = state // groups
    width = inner // heads

    def body(
        early_ref, late_ref, early_step_ref, late_step_ref, rim_ref, taps_ref, bias_ref, decay_ref,
        conv_ref, step_ref, cum_ref, update_ref, block_log_ref, message_ref,
        padded_ref,
    ):
        half = early_ref.shape[0]
        rows = 2 * half
        columns = inner + state
        padded_ref[0:8, :] = rim_ref[TAIL - 8 : TAIL, 0:columns].astype(F32)
        padded_ref[8 : 8 + half, :] = early_ref[:, 0:columns].astype(F32)
        padded_ref[8 + half : 8 + rows, :] = late_ref[:, 0:columns].astype(F32)
        expand = expander(heads, width)
        row = lax.broadcasted_iota(jnp.int32, (SPAN, SPAN), 0)
        col = lax.broadcasted_iota(jnp.int32, (SPAN, SPAN), 1)
        lower = jnp.where(row >= col, 1.0, 0.0).astype(BF16)
        rate = jnp.exp(decay_ref[...])
        total_log = jnp.zeros((1, heads), F32)
        block_log_ref[...] = jnp.zeros_like(block_log_ref)
        total = None
        for b in range(rows // SPAN):
            start = b * SPAN
            source = early_step_ref if start < half else late_step_ref
            raw = source[start % half : start % half + SPAN, :]
            pre = raw.astype(F32) + bias_ref[...]
            step = jnp.maximum(pre, 0.0) + jnp.log1p(jnp.exp(-jnp.abs(pre)))
            log_decay = -step * rate
            cum = None
            for part in parts_of(log_decay, 3):
                term = dot(lower, part)
                cum = term if cum is None else cum + term
            last = cum[SPAN - 1 : SPAN, :]
            step_ref[start : start + SPAN, :] = step
            cum_ref[start : start + SPAN, :] = cum
            block_log_ref[b : b + 1, :] = last
            factor = spread(step * jnp.exp(last - cum), expand)
            final = spread(jnp.broadcast_to(last, (8, heads)), expand, 3)[0:1, :]
            keep = jnp.exp(final)
            updates = []
            for g in range(groups):
                x_cols = slice(g * inner // groups, (g + 1) * inner // groups)
                b_cols = slice(inner + g * size, inner + (g + 1) * size)
                x = conv_block(padded_ref, start, taps_ref, x_cols)
                maps = conv_block(padded_ref, start, taps_ref, b_cols)
                conv_ref[start : start + SPAN, x_cols] = x
                conv_ref[start : start + SPAN, b_cols] = maps
                scaled = (x.astype(F32) * factor[:, x_cols]).astype(BF16)
                update = dot(maps, scaled, ((0,), (0,)))
                update_ref[b, :, x_cols] = update
                updates.append(update)
            update = jnp.concatenate(updates, axis=1)
            total = update if total is None else keep * total + update
            total_log = total_log + last
        message_ref[0:size, :] = total.astype(BF16)
        message_ref[size : size + TAIL, :] = log_rows(
            spread(jnp.broadcast_to(total_log, (8, heads)), expand, 3)[0:1, :]
        )

    return body


def log_rows(log):
    row = lax.broadcasted_iota(jnp.int32, (TAIL, log.shape[1]), 0)
    block = jnp.zeros((TAIL, log.shape[1]), F32)
    for k, part in enumerate(parts_of(log, 3)):
        block = jnp.where(row == k, part.astype(F32), block)
    return block.astype(BF16)


def log_of(message_ref, size):
    rows = message_ref[size : size + TAIL, :].astype(F32)
    return rows[0:1, :] + rows[1:2, :] + rows[2:3, :]


def combine_body(size, first):
    def body(later_ref, mine_ref, came_ref, *refs):
        if first:
            out_ref, before_ref, before_log_ref = refs
        else:
            prior_ref, prior_log_ref, out_ref, before_ref, before_log_ref = refs
        mine = mine_ref[0:size, :].astype(F32)
        came = came_ref[0:size, :].astype(F32)
        my_log, came_log = log_of(mine_ref, size), log_of(came_ref, size)

        @pl.when(later_ref[0] == 1)
        def _():
            out_ref[0:size, :] = (jnp.exp(my_log) * came + mine).astype(BF16)
            if first:
                before_ref[...] = came
                before_log_ref[0:1, :] = came_log
            else:
                before_ref[...] = jnp.exp(prior_log_ref[0:1, :]) * came + prior_ref[...]
                before_log_ref[0:1, :] = prior_log_ref[0:1, :] + came_log

        @pl.when(later_ref[0] == 0)
        def _():
            out_ref[0:size, :] = (jnp.exp(came_log) * mine + came).astype(BF16)
            if first:
                before_ref[...] = jnp.zeros_like(before_ref)
                before_log_ref[0:1, :] = jnp.zeros_like(came_log)
            else:
                before_ref[...] = prior_ref[...]
                before_log_ref[0:1, :] = prior_log_ref[0:1, :]

        out_ref[size : size + TAIL, :] = log_rows(my_log + came_log)

    return body


def within_body(inner, state, heads, groups):
    size = state // groups
    width = inner // heads
    per_group = heads // groups

    def body(
        conv_ref, step_ref, cum_ref, early_ref, late_ref, rim_ref, taps_ref, skip_ref,
        out_ref, maps_ref,
        padded_ref,
    ):
        half = early_ref.shape[0]
        rows = 2 * half
        padded_ref[0:8, :] = rim_ref[TAIL - 8 : TAIL, :].astype(F32)
        padded_ref[8 : 8 + half, :] = early_ref[:, inner : inner + state].astype(F32)
        padded_ref[8 + half : 8 + rows, :] = late_ref[:, inner : inner + state].astype(F32)
        expand = expander(heads, width)
        row = lax.broadcasted_iota(jnp.int32, (SPAN, SPAN), 0)
        col = lax.broadcasted_iota(jnp.int32, (SPAN, SPAN), 1)
        causal = row >= col
        lane = lax.broadcasted_iota(jnp.int32, (SPAN, 2 * width), 1)
        skip = spread(jnp.broadcast_to(skip_ref[...], (8, heads)), expand, 3)[0:1, :]
        for b in range(rows // SPAN):
            here = slice(b * SPAN, (b + 1) * SPAN)
            cum = cum_ref[here, :]
            padded_cum = jnp.concatenate([cum, jnp.zeros((SPAN, SPAN - heads), F32)], axis=1)
            cum_rows = padded_cum.T
            step = spread(step_ref[here, :], expand)
            for g in range(groups):
                maps = conv_block(
                    padded_ref, b * SPAN, taps_ref, slice(g * size, (g + 1) * size)
                )
                maps_ref[here, g * size : (g + 1) * size] = maps
                in_map = conv_ref[here, inner + g * size : inner + (g + 1) * size]
                scores = dot(maps, in_map, ((1,), (1,)))
                for pair in range(per_group // 2):
                    head = g * per_group + 2 * pair
                    cols = slice(head * width, (head + 2) * width)
                    x = conv_ref[here, cols].astype(F32)
                    scaled = x * step[:, cols]
                    weighted = []
                    for h in (head, head + 1):
                        gap = cum[:, h : h + 1] - cum_rows[h : h + 1, :]
                        decay = jnp.exp(jnp.where(causal, gap, -1e30))
                        weighted.append((scores * decay).astype(BF16))
                    stacked = jnp.concatenate(
                        [
                            jnp.where(lane < width, scaled, 0.0).astype(BF16),
                            jnp.where(lane < width, 0.0, scaled).astype(BF16),
                        ],
                        axis=0,
                    )
                    out = dot(jnp.concatenate(weighted, axis=1), stacked)
                    out_ref[here, cols] = out + skip[:, cols] * x

    return body


def finish(
    part, parts, index, later, entering, update, block_log, cum, maps, within, second, gain,
    out_weight, inner, state, heads, groups, count,
):
    size = state // groups
    width = inner // heads
    rows = second.shape[0]
    blocks = rows // SPAN
    model = out_weight.shape[1]
    turn_width = model // count
    first = part == 0

    def body(index_ref, later_ref, *refs):
        entering_refs, refs = refs[: len(entering)], refs[len(entering) :]
        (
            update_ref, block_log_ref, cum_ref, maps_ref, within_ref, second_ref, gain_ref,
            weight_ref, out_ref, *memory_out, mixed_ref,
        ) = refs

        @pl.when(pl.program_id(0) == 0)
        def _():
            expand = expander(heads, width)
            if first:
                came_ref, before_ref, before_log_ref, start_ref = entering_refs
                is_later = later_ref[0] == 1
                prior_log = before_log_ref[0:1, :]
                prior = before_ref[...]
                came = came_ref[0:size, :].astype(F32)
                came_log = log_of(came_ref, size)
                memory = jnp.where(is_later, jnp.exp(prior_log) * came + prior, prior)
                memory_log = jnp.where(is_later, prior_log + came_log, prior_log)
                memory = jnp.exp(memory_log) * start_ref[...] + memory
            else:
                memory = entering_refs[0][...]
            keep = jnp.exp(spread(block_log_ref[...], expand, 3))
            for b in range(blocks):
                here = slice(b * SPAN, (b + 1) * SPAN)
                reach = spread(jnp.exp(cum_ref[here, :]), expand)
                for g in range(groups):
                    cols = slice(g * inner // groups, (g + 1) * inner // groups)
                    carried = dot(
                        maps_ref[here, g * size : (g + 1) * size], memory[:, cols].astype(BF16)
                    )
                    scan = within_ref[here, cols] + reach[:, cols] * carried
                    gated = scan * silu(second_ref[here, cols].astype(F32))
                    moment = jnp.mean(gated * gated, axis=-1, keepdims=True)
                    mixed_ref[here, cols] = (
                        gated * lax.rsqrt(moment + EPSILON) * gain_ref[:, cols].astype(F32)
                    ).astype(BF16)
                if part < parts - 1 or b < blocks - 1:
                    step = part * blocks + b
                    memory = keep[step : step + 1, :] * memory + update_ref[b]
            if memory_out:
                memory_out[0][...] = memory

        out_ref[...] = dot(mixed_ref[...], weight_ref[...]).astype(BF16)

    def rows_of(array):
        return pl.BlockSpec((rows, array.shape[1]), lambda *_: (part, 0))

    def farthest(j, index_ref):
        index = index_ref[0]
        low, high = jnp.int32(0), jnp.int32(count - 1)
        chosen = low
        for k in range(count):
            up = high - index >= index - low
            pick = jnp.where(up, high, low)
            chosen = jnp.where(j == k, pick, chosen)
            high = jnp.where(up, high - 1, high)
            low = jnp.where(up, low, low + 1)
        return chosen

    shape = jax.ShapeDtypeStruct
    memory_shape = [shape((size, inner), F32)] if part < parts - 1 else []

    def fixed(array):
        rank = len(array.shape)
        return pl.BlockSpec(array.shape, lambda *_: (0,) * rank)

    return pl.pallas_call(
        body,
        out_shape=[shape((rows, model), BF16)] + memory_shape,
        grid_spec=pltpu.PrefetchScalarGridSpec(
            num_scalar_prefetch=2,
            grid=(count,),
            in_specs=[fixed(a) for a in entering]
            + [
                pl.BlockSpec((blocks, size, inner), lambda *_: (part, 0, 0)),
                fixed(block_log),
                rows_of(cum),
                rows_of(maps),
                rows_of(within),
                fixed(second),
                fixed(gain),
                pl.BlockSpec((inner, turn_width), lambda j, i, _: (0, farthest(j, i))),
            ],
            out_specs=[pl.BlockSpec((rows, turn_width), lambda j, i, _: (0, farthest(j, i)))]
            + [fixed(a) for a in memory_shape],
            scratch_shapes=[pltpu.VMEM((rows, inner), BF16)],
        ),
        name="finish",
    )(
        index, later, *entering, update, block_log, cum, maps, within, second, gain, out_weight
    )


def relay(index, distance, partial, received, count):
    rows, model = partial.shape
    width = model // count

    def body(index_ref, ahead_ref, behind_ref, *refs):
        for own, came, out in zip((ahead_ref, behind_ref), refs[:-2], refs[-2:]):
            out[...] = (own[...].astype(F32) + came[...].astype(F32)).astype(BF16)

    def place(sign):
        return lambda j, i: (0, jnp.clip(i[0] + sign * distance, 0, count - 1))

    whole = pl.BlockSpec((rows, width), lambda *_: (0, 0))
    shape = jax.ShapeDtypeStruct((rows, width), BF16)
    return pl.pallas_call(
        body,
        out_shape=[shape, shape],
        grid_spec=pltpu.PrefetchScalarGridSpec(
            num_scalar_prefetch=1,
            grid=(1,),
            in_specs=[
                pl.BlockSpec((rows, width), place(1)),
                pl.BlockSpec((rows, width), place(-1)),
                whole,
                whole,
            ],
            out_specs=[whole, whole],
        ),
        name="relay",
    )(index, partial, partial, *received)


def outermost(index, partial, count):
    width = partial.shape[1] // count
    return partial[:, (count - 1) * width :], partial[:, :width]


def send_on(ahead, behind, distance, axis):
    count = lax.axis_size(axis)
    return (
        lax.ppermute(ahead, axis, [(i, i + 1) for i in range(count - distance)]),
        lax.ppermute(behind, axis, [(i, i - 1) for i in range(distance, count)]),
    )


def total(index, partial, received, hidden, row_block, count):
    rows, model = partial.shape
    width = model // count

    def body(index_ref, own_ref, ahead_ref, behind_ref, hidden_ref, out_ref):
        summed = own_ref[...].astype(F32) + ahead_ref[...].astype(F32)
        summed = summed + behind_ref[...].astype(F32)
        out_ref[...] = (summed + hidden_ref[...].astype(F32)).astype(BF16)

    whole = pl.BlockSpec((rows, width), lambda *_: (0, 0))
    return pl.pallas_call(
        body,
        out_shape=jax.ShapeDtypeStruct((rows, width), BF16),
        grid_spec=pltpu.PrefetchScalarGridSpec(
            num_scalar_prefetch=1,
            grid=(1,),
            in_specs=[
                pl.BlockSpec((rows, width), lambda j, i: (0, i[0])),
                whole,
                whole,
                pl.BlockSpec((rows, width), lambda *_: (row_block, 0)),
            ],
            out_specs=whole,
        ),
        name="total",
    )(index, partial, *received, hidden)


def on_device(
    hidden, norm_gain, gate_x_weight, state_weight, step_weight, conv_inner, conv_state,
    step_bias, decay_log, skip_gain, inner_gain, out_weight, initial_state,
):
    rows = hidden.shape[0]
    half = rows // 2
    inner = gate_x_weight.shape[2]
    state = state_weight.shape[2]
    heads = step_weight.shape[1]
    size = initial_state.shape[2]
    groups = state // size
    blocks = rows // SPAN
    feature_index = lax.axis_index("tp").reshape(1)
    range_index = lax.axis_index("seq")
    ranges = lax.axis_size("seq")

    model = step_weight.shape[0]
    parts_count = lax.axis_size("tp")
    wide_weight = gate_x_weight.reshape(model, 2 * inner)
    narrow_weight = state_weight.reshape(model, 2 * state)
    step_rows = step_weight.T
    taps = jnp.concatenate([conv_inner, conv_state[:, 0]], axis=1)
    start_state = initial_state.transpose(2, 0, 1).reshape(size, inner)

    late_pieces = line_gather(hidden[half:], "tp")
    early_pieces = line_gather(hidden[:half], "tp")
    gain = norm_gain.astype(F32)[None, :]
    weights = (wide_weight, narrow_weight)
    late_first, late_step, late, late_scale = project_first(
        late_pieces, feature_index, gain, *weights, step_rows, inner, state
    )
    late_second = project_second(late, late_scale, *weights, inner, state)
    rim = jnp.concatenate(
        [late_first[half - TAIL :], late_second[half - TAIL :, inner:]], axis=1
    )
    rim = shifted(rim, "seq", 1)
    rim_first, rim_second = rim[:, : inner + state], rim[:, inner + state :]

    early_first, early_step, early, early_scale = project_first(
        early_pieces, feature_index, gain, *weights, step_rows, inner, state
    )
    shape = jax.ShapeDtypeStruct
    conv, step, cum, update, block_log, message = call(
        state_body(inner, state, heads, groups),
        [
            shape((rows, inner + state), BF16),
            shape((rows, heads), F32),
            shape((rows, heads), F32),
            shape((blocks, size, inner), F32),
            shape((8 * ((blocks + 7) // 8), heads), F32),
            shape((size + TAIL, inner), BF16),
        ],
        early_first,
        late_first,
        early_step,
        late_step,
        rim_first,
        taps,
        step_bias[None, :],
        decay_log[None, :],
        scratch=[pltpu.VMEM((rows + 8, inner + state), F32)],
        name="states",
    )
    early_second = project_second(early, early_scale, *weights, inner, state)
    within, maps = call(
        within_body(inner, state, heads, groups),
        [shape((rows, inner), F32), shape((rows, state), BF16)],
        conv,
        step,
        cum,
        early_second,
        late_second,
        rim_second,
        conv_state[:, 1],
        skip_gain[None, :],
        scratch=[pltpu.VMEM((rows + 8, state), F32)],
        name="within",
    )
    before = ()
    bit = 1
    while True:
        came = swapped(message, "seq", bit)
        later = ((range_index // bit) % 2).astype(jnp.int32).reshape(1)
        bit *= 2
        if bit == ranges:
            break
        message, *before = call(
            combine_body(size, not before),
            [
                shape((size + TAIL, inner), BF16),
                shape((size, inner), F32),
                shape((8, inner), F32),
            ],
            later,
            message,
            came,
            *before,
            scalars=1,
            name="combine",
        )
    entering = (came, *before, start_state)
    partials = []
    for part, second in enumerate((early_second, late_second)):
        partial, *entering = finish(
            part, 2, feature_index, later, entering, update, block_log, cum, maps, within,
            second, inner_gain[None, :], out_weight, inner, state, heads, groups, parts_count,
        )
        partials.append(partial)
    received = [
        send_on(*outermost(feature_index, partial, parts_count), parts_count - 1, "tp")
        for partial in partials
    ]
    for distance in range(parts_count - 2, 0, -1):
        for k, partial in enumerate(partials):
            onward = relay(feature_index, distance, partial, received[k], parts_count)
            received[k] = send_on(*onward, distance, "tp")
    outs = [
        total(feature_index, partial, received[k], hidden, k, parts_count)
        for k, partial in enumerate(partials)
    ]
    return jnp.concatenate(outs, axis=0)


def solution(mesh):
    return jax.shard_map(
        on_device,
        mesh=mesh,
        in_specs=(
            P("seq", "tp"),
            P(),
            P(None, None, "tp"),
            P(None, None, "tp"),
            P(None, "tp"),
            P(None, "tp"),
            P(None, None, "tp"),
            P("tp"),
            P("tp"),
            P("tp"),
            P("tp"),
            P("tp", None),
            P("tp", None, None),
        ),
        out_specs=P("seq", "tp"),
        check_vma=False,
    )
```

```python
import jax
import jax.numpy as jnp
from jax import lax
from jax.experimental import pallas as pl
from jax.experimental.pallas import tpu as pltpu
from jax.sharding import PartitionSpec as P

SPAN = 128
EPSILON = 1e-05
TAIL = 16
LANES = 128
F32 = jnp.float32
BF16 = jnp.bfloat16


def shifted(block, axis, distance):
    count = lax.axis_size(axis)
    route = [(i, i + distance) for i in range(count) if 0 <= i + distance < count]
    return lax.ppermute(block, axis, route)


def swapped(block, axis, bit):
    return lax.ppermute(block, axis, [(i, i ^ bit) for i in range(lax.axis_size(axis))])


def line_step(pieces, step, axis):
    count = lax.axis_size(axis)
    behind, ahead = pieces[-2], pieces[-1]
    behind = lax.ppermute(behind, axis, [(i, i + 1) for i in range(step - 1, count - 1)])
    ahead = lax.ppermute(ahead, axis, [(i, i - 1) for i in range(1, count - step + 1)])
    return pieces + [behind, ahead]


def whole_spec(array):
    rank = len(array.shape)
    return pl.BlockSpec(array.shape, lambda *_: (0,) * rank)


def call(body, outs, *arrays, scratch=(), scalars=0, name=None, limit=16):
    pairs = [a if isinstance(a, tuple) else (a, whole_spec(a)) for a in arrays[scalars:]]
    return pl.pallas_call(
        body,
        out_shape=outs,
        grid=(1,),
        in_specs=[pl.BlockSpec(memory_space=pltpu.SMEM)] * scalars + [spec for _, spec in pairs],
        out_specs=jax.tree.map(whole_spec, outs),
        scratch_shapes=list(scratch),
        compiler_params=granted(limit),
        name=name,
    )(*arrays[:scalars], *[a for a, _ in pairs])


def granted(mebibytes):
    return pltpu.CompilerParams(vmem_limit_bytes=mebibytes * 2**20)


def rim_of(raw):
    place = raw.shape[0] // TAIL - 1
    return raw, pl.BlockSpec((TAIL, raw.shape[1]), lambda *_: (place, 0))


def dot(a, b, contract=((1,), (0,))):
    return lax.dot_general(a, b, (contract, ((), ())), preferred_element_type=F32)


def parts_of(x, count):
    parts = []
    for _ in range(count):
        part = x.astype(BF16)
        parts.append(part)
        x = x - part.astype(F32)
    return parts


def spread(x, expand, count=2):
    total = None
    for part in parts_of(x, count):
        term = dot(part, expand)
        total = term if total is None else total + term
    return total


def expander(heads, width):
    head = lax.broadcasted_iota(jnp.int32, (heads, heads * width), 0)
    lane = lax.broadcasted_iota(jnp.int32, (heads, heads * width), 1)
    inside = jnp.logical_and(lane >= head * width, lane < (head + 1) * width)
    return jnp.where(inside, 1.0, 0.0).astype(BF16)


def silu(v):
    return v * (1.0 / (1.0 + jnp.exp(-v)))


def conv_block(padded_ref, start, taps_ref, columns):
    summed = None
    for k in range(taps_ref.shape[0]):
        row = 8 + start - (taps_ref.shape[0] - 1) + k
        term = taps_ref[k : k + 1, columns].astype(F32) * padded_ref[row : row + SPAN, columns]
        summed = term if summed is None else summed + term
    return silu(summed).astype(BF16)


def project_first(pieces, index, gain, wide, narrow_weight, step_weight, inner, state):
    rows, width = pieces[0].shape
    model, heads = step_weight.shape[1], step_weight.shape[0]
    count = model // width
    wide_blocks = inner // state
    offsets = [(k + 1) // 2 * (-1) ** (k % 2) for k in range(len(pieces))]

    def body(index_ref, gain_ref, *refs):
        parts = refs[: len(offsets)]
        wide_refs, refs = refs[len(offsets) : len(offsets) + len(wide)], refs[-7:]
        narrow_ref, steps_ref, out_ref, step_ref, scaled_ref, scale_ref, square_ref = refs
        turn = pl.program_id(0)

        @pl.when(turn == 0)
        def _():
            square_ref[...] = jnp.zeros_like(square_ref)
            for part, offset in zip(parts, offsets):
                target = index_ref[0] + offset

                @pl.when(jnp.logical_and(target >= 0, target < count))
                def _():
                    def columns(k, carry):
                        here = pl.ds(pl.multiple_of(k * LANES, LANES), LANES)
                        there = pl.ds(pl.multiple_of(target * width + k * LANES, LANES), LANES)
                        value = part[:, here].astype(F32)
                        square_ref[...] += value * value
                        scaled_ref[:, there] = (value * gain_ref[:, there]).astype(BF16)
                        return carry

                    lax.fori_loop(0, width // LANES, columns, 0)

            moment = jnp.sum(square_ref[...], axis=-1, keepdims=True) * (1.0 / model)
            scale_ref[...] = jnp.broadcast_to(lax.rsqrt(moment + EPSILON), scale_ref.shape)
            raw = dot(scaled_ref[...], steps_ref[...], ((1,), (1,)))
            step_ref[...] = (raw * scale_ref[:, 0:heads]).astype(BF16)

        @pl.when(turn < wide_blocks)
        def _():
            raw = rows_dot(scaled_ref, wide_refs)
            out_ref[...] = (raw * scale_ref[:, 0:1]).astype(BF16)

        @pl.when(turn == wide_blocks)
        def _():
            raw = dot(scaled_ref[...], narrow_ref[...])
            out_ref[...] = (raw * scale_ref[:, 0:1]).astype(BF16)

    shape = jax.ShapeDtypeStruct
    return pl.pallas_call(
        body,
        grid=(wide_blocks + 1,),
        out_shape=[
            shape((rows, inner + state), BF16),
            shape((rows, heads), BF16),
            shape((rows, model), BF16),
            shape((rows, LANES), F32),
        ],
        in_specs=[pl.BlockSpec(memory_space=pltpu.SMEM), whole_spec(gain)]
        + [whole_spec(piece) for piece in pieces]
        + [
            pl.BlockSpec(
                (part.shape[0], state),
                lambda j: (0, wide_blocks + jnp.minimum(j, wide_blocks - 1)),
            )
            for part in wide
        ]
        + [
            pl.BlockSpec((model, state), lambda j: (0, 0)),
            whole_spec(step_weight),
        ],
        out_specs=[
            pl.BlockSpec((rows, state), lambda j: (0, j)),
            pl.BlockSpec((rows, heads), lambda j: (0, 0)),
            pl.BlockSpec((rows, model), lambda j: (0, 0)),
            pl.BlockSpec((rows, LANES), lambda j: (0, 0)),
        ],
        scratch_shapes=[pltpu.VMEM((rows, LANES), F32)],
        compiler_params=granted(48),
        name="project_first",
    )(index, gain, *pieces, *wide, narrow_weight, step_weight)


def rows_dot(left_ref, right_refs):
    summed, start = None, 0
    for right_ref in right_refs:
        stop = start + right_ref.shape[0]
        term = dot(left_ref[:, start:stop], right_ref[...])
        summed = term if summed is None else summed + term
        start = stop
    return summed


def project_second(scaled, scales, wide, narrow_weight, inner, state):
    model = scaled[0].shape[1]
    wide_blocks = inner // state
    parts = len(scaled)

    def body(*refs):
        scaled_refs, scale_refs, refs = refs[:parts], refs[parts : 2 * parts], refs[2 * parts :]
        *wide_refs, narrow_ref = refs[:-parts]
        turn = pl.program_id(0)

        def project(weight_refs):
            for scaled_ref, scale_ref, out_ref in zip(scaled_refs, scale_refs, refs[-parts:]):
                raw = rows_dot(scaled_ref, weight_refs)
                out_ref[...] = (raw * scale_ref[:, 0:1]).astype(BF16)

        @pl.when(turn < wide_blocks)
        def _():
            project(wide_refs)

        @pl.when(turn == wide_blocks)
        def _():
            project([narrow_ref])

    return pl.pallas_call(
        body,
        grid=(wide_blocks + 1,),
        out_shape=[jax.ShapeDtypeStruct((part.shape[0], inner + state), BF16) for part in scaled],
        in_specs=[whole_spec(part) for part in (*scaled, *scales)]
        + [
            pl.BlockSpec((part.shape[0], state), lambda j: (0, jnp.minimum(j, wide_blocks - 1)))
            for part in wide
        ]
        + [pl.BlockSpec((model, state), lambda j: (0, 1))],
        out_specs=[pl.BlockSpec((part.shape[0], state), lambda j: (0, j)) for part in scaled],
        compiler_params=granted(48),
        name="project_second",
    )(*scaled, *scales, *wide, narrow_weight)


def fill(padded_ref, raw_ref, rim_refs, lead, columns):
    if lead:
        padded_ref[0:8, :] = raw_ref[lead - 8 : lead, columns].astype(F32)
    else:
        padded_ref[0:8, :] = rim_refs[0][TAIL - 8 : TAIL, columns].astype(F32)
    padded_ref[8:, :] = raw_ref[lead:, columns].astype(F32)


def state_body(inner, state, heads, groups, lead, last_part):
    size = state // groups
    width = inner // heads

    def body(raw_ref, raw_step_ref, taps_ref, bias_ref, decay_ref, *refs):
        earlier, refs = (refs[:3], refs[3:]) if last_part else ((), refs)
        conv_ref, step_ref, cum_ref, update_ref, block_log_ref, *sums, padded_ref = refs
        rows = raw_ref.shape[0] - lead
        fill(padded_ref, raw_ref, earlier, lead, slice(0, inner + state))
        expand = expander(heads, width)
        row = lax.broadcasted_iota(jnp.int32, (SPAN, SPAN), 0)
        col = lax.broadcasted_iota(jnp.int32, (SPAN, SPAN), 1)
        lower = jnp.where(row >= col, 1.0, 0.0).astype(BF16)
        rate = jnp.exp(decay_ref[...])
        block_log_ref[...] = jnp.zeros_like(block_log_ref)
        total = earlier[1][...] if last_part else None
        total_log = earlier[2][0:1, :] if last_part else jnp.zeros((1, heads), F32)
        for b in range(rows // SPAN):
            start = b * SPAN
            raw = raw_step_ref[lead + start : lead + start + SPAN, :]
            pre = raw.astype(F32) + bias_ref[...]
            step = jnp.maximum(pre, 0.0) + jnp.log1p(jnp.exp(-jnp.abs(pre)))
            log_decay = -step * rate
            cum = None
            for part in parts_of(log_decay, 3):
                term = dot(lower, part)
                cum = term if cum is None else cum + term
            last = cum[SPAN - 1 : SPAN, :]
            step_ref[start : start + SPAN, :] = step
            cum_ref[start : start + SPAN, :] = cum
            block_log_ref[b : b + 1, :] = last
            factor = spread(step * jnp.exp(last - cum), expand)
            final = spread(jnp.broadcast_to(last, (8, heads)), expand, 3)[0:1, :]
            keep = jnp.exp(final)
            updates = []
            for g in range(groups):
                x_cols = slice(g * inner // groups, (g + 1) * inner // groups)
                b_cols = slice(inner + g * size, inner + (g + 1) * size)
                x = conv_block(padded_ref, start, taps_ref, x_cols)
                maps = conv_block(padded_ref, start, taps_ref, b_cols)
                conv_ref[start : start + SPAN, x_cols] = x
                conv_ref[start : start + SPAN, b_cols] = maps
                scaled = (x.astype(F32) * factor[:, x_cols]).astype(BF16)
                update = dot(maps, scaled, ((0,), (0,)))
                update_ref[b, :, x_cols] = update
                updates.append(update)
            update = jnp.concatenate(updates, axis=1)
            total = update if total is None else keep * total + update
            total_log = total_log + last
        if last_part:
            sums[0][0:size, :] = total.astype(BF16)
            sums[0][size : size + TAIL, :] = log_rows(
                spread(jnp.broadcast_to(total_log, (8, heads)), expand, 3)[0:1, :]
            )
        else:
            sums[0][...] = total
            sums[1][...] = jnp.broadcast_to(total_log, (8, heads))

    return body


def log_rows(log):
    row = lax.broadcasted_iota(jnp.int32, (TAIL, log.shape[1]), 0)
    block = jnp.zeros((TAIL, log.shape[1]), F32)
    for k, part in enumerate(parts_of(log, 3)):
        block = jnp.where(row == k, part.astype(F32), block)
    return block.astype(BF16)


def log_of(message_ref, size):
    rows = message_ref[size : size + TAIL, :].astype(F32)
    return rows[0:1, :] + rows[1:2, :] + rows[2:3, :]


def combine_body(size, first):
    def body(later_ref, mine_ref, came_ref, *refs):
        if first:
            out_ref, before_ref, before_log_ref = refs
        else:
            prior_ref, prior_log_ref, out_ref, before_ref, before_log_ref = refs
        mine = mine_ref[0:size, :].astype(F32)
        came = came_ref[0:size, :].astype(F32)
        my_log, came_log = log_of(mine_ref, size), log_of(came_ref, size)

        @pl.when(later_ref[0] == 1)
        def _():
            out_ref[0:size, :] = (jnp.exp(my_log) * came + mine).astype(BF16)
            if first:
                before_ref[...] = came
                before_log_ref[0:1, :] = came_log
            else:
                before_ref[...] = jnp.exp(prior_log_ref[0:1, :]) * came + prior_ref[...]
                before_log_ref[0:1, :] = prior_log_ref[0:1, :] + came_log

        @pl.when(later_ref[0] == 0)
        def _():
            out_ref[0:size, :] = (jnp.exp(came_log) * mine + came).astype(BF16)
            if first:
                before_ref[...] = jnp.zeros_like(before_ref)
                before_log_ref[0:1, :] = jnp.zeros_like(came_log)
            else:
                before_ref[...] = prior_ref[...]
                before_log_ref[0:1, :] = prior_log_ref[0:1, :]

        out_ref[size : size + TAIL, :] = log_rows(my_log + came_log)

    return body


def within_body(inner, state, heads, groups, lead):
    size = state // groups
    width = inner // heads
    per_group = heads // groups

    def body(conv_ref, step_ref, cum_ref, raw_ref, taps_ref, skip_ref, *refs):
        *rim, out_ref, maps_ref, padded_ref = refs
        rows = raw_ref.shape[0] - lead
        fill(padded_ref, raw_ref, rim, lead, slice(inner, inner + state))
        expand = expander(heads, width)
        row = lax.broadcasted_iota(jnp.int32, (SPAN, SPAN), 0)
        col = lax.broadcasted_iota(jnp.int32, (SPAN, SPAN), 1)
        causal = row >= col
        lane = lax.broadcasted_iota(jnp.int32, (SPAN, 2 * width), 1)
        skip = spread(jnp.broadcast_to(skip_ref[...], (8, heads)), expand, 3)[0:1, :]
        for b in range(rows // SPAN):
            here = slice(b * SPAN, (b + 1) * SPAN)
            cum = cum_ref[here, :]
            padded_cum = jnp.concatenate([cum, jnp.zeros((SPAN, SPAN - heads), F32)], axis=1)
            cum_rows = padded_cum.T
            step = spread(step_ref[here, :], expand)
            for g in range(groups):
                maps = conv_block(
                    padded_ref, b * SPAN, taps_ref, slice(g * size, (g + 1) * size)
                )
                maps_ref[here, g * size : (g + 1) * size] = maps
                in_map = conv_ref[here, inner + g * size : inner + (g + 1) * size]
                scores = dot(maps, in_map, ((1,), (1,)))
                for pair in range(per_group // 2):
                    head = g * per_group + 2 * pair
                    cols = slice(head * width, (head + 2) * width)
                    x = conv_ref[here, cols].astype(F32)
                    scaled = x * step[:, cols]
                    weighted = []
                    for h in (head, head + 1):
                        gap = cum[:, h : h + 1] - cum_rows[h : h + 1, :]
                        decay = jnp.exp(jnp.where(causal, gap, -1e30))
                        weighted.append((scores * decay).astype(BF16))
                    stacked = jnp.concatenate(
                        [
                            jnp.where(lane < width, scaled, 0.0).astype(BF16),
                            jnp.where(lane < width, 0.0, scaled).astype(BF16),
                        ],
                        axis=0,
                    )
                    out = dot(jnp.concatenate(weighted, axis=1), stacked)
                    out_ref[here, cols] = out + skip[:, cols] * x

    return body


def finish(
    last_part, lead, index, later, entering, update, block_log, cum, maps, within, second, gain,
    out_weight, inner, state, heads, groups, count,
):
    size = state // groups
    width = inner // heads
    rows = second.shape[0] - lead
    blocks = rows // SPAN
    model = out_weight.shape[1]
    turn_width = model // count
    first = len(entering) > 1

    def body(index_ref, later_ref, *refs):
        entering_refs, refs = refs[: len(entering)], refs[len(entering) :]
        (
            update_ref, block_log_ref, cum_ref, maps_ref, within_ref, second_ref, gain_ref,
            weight_ref, out_ref, top_ref, bottom_ref, *memory_out, mixed_ref,
        ) = refs

        @pl.when(pl.program_id(0) == 0)
        def _():
            expand = expander(heads, width)
            if first:
                came_ref, before_ref, before_log_ref, start_ref = entering_refs
                is_later = later_ref[0] == 1
                prior_log = before_log_ref[0:1, :]
                prior = before_ref[...]
                came = came_ref[0:size, :].astype(F32)
                came_log = log_of(came_ref, size)
                memory = jnp.where(is_later, jnp.exp(prior_log) * came + prior, prior)
                memory_log = jnp.where(is_later, prior_log + came_log, prior_log)
                memory = jnp.exp(memory_log) * start_ref[...] + memory
            else:
                memory = entering_refs[0][...]
            keep = jnp.exp(spread(block_log_ref[...], expand, 3))
            for b in range(blocks):
                here = slice(b * SPAN, (b + 1) * SPAN)
                reach = spread(jnp.exp(cum_ref[here, :]), expand)
                for g in range(groups):
                    cols = slice(g * inner // groups, (g + 1) * inner // groups)
                    carried = dot(
                        maps_ref[here, g * size : (g + 1) * size], memory[:, cols].astype(BF16)
                    )
                    scan = within_ref[here, cols] + reach[:, cols] * carried
                    gate = second_ref[lead + b * SPAN : lead + (b + 1) * SPAN, cols]
                    gated = scan * silu(gate.astype(F32))
                    moment = jnp.mean(gated * gated, axis=-1, keepdims=True)
                    mixed_ref[here, cols] = (
                        gated * lax.rsqrt(moment + EPSILON) * gain_ref[:, cols].astype(F32)
                    ).astype(BF16)
                if not last_part or b < blocks - 1:
                    memory = keep[b : b + 1, :] * memory + update_ref[b]
            if memory_out:
                memory_out[0][...] = memory

        sent = dot(mixed_ref[...], weight_ref[...]).astype(BF16)
        out_ref[...] = sent
        target = farthest(pl.program_id(0), index_ref)

        @pl.when(target == count - 1)
        def _():
            top_ref[...] = sent

        @pl.when(target == 0)
        def _():
            bottom_ref[...] = sent

    def farthest(j, index_ref):
        index = index_ref[0]
        low, high = jnp.int32(0), jnp.int32(count - 1)
        chosen = low
        for k in range(count):
            up = high - index >= index - low
            pick = jnp.where(up, high, low)
            chosen = jnp.where(j == k, pick, chosen)
            high = jnp.where(up, high - 1, high)
            low = jnp.where(up, low, low + 1)
        return chosen

    shape = jax.ShapeDtypeStruct
    extra = [shape((rows, turn_width), BF16)] * 2
    extra += [] if last_part else [shape((size, inner), F32)]

    def fixed(array):
        rank = len(array.shape)
        return pl.BlockSpec(array.shape, lambda *_: (0,) * rank)

    return pl.pallas_call(
        body,
        out_shape=[shape((rows, model), BF16)] + extra,
        grid_spec=pltpu.PrefetchScalarGridSpec(
            num_scalar_prefetch=2,
            grid=(count,),
            in_specs=[fixed(a) for a in entering]
            + [
                fixed(update),
                fixed(block_log),
                fixed(cum),
                fixed(maps),
                fixed(within),
                fixed(second),
                fixed(gain),
                pl.BlockSpec((inner, turn_width), lambda j, i, _: (0, farthest(j, i))),
            ],
            out_specs=[pl.BlockSpec((rows, turn_width), lambda j, i, _: (0, farthest(j, i)))]
            + [fixed(a) for a in extra],
            scratch_shapes=[pltpu.VMEM((rows, inner), BF16)],
        ),
        compiler_params=granted(24),
        name="finish",
    )(
        index, later, *entering, update, block_log, cum, maps, within, second, gain, out_weight
    )


def relay(index, distance, partial, received, count):
    rows, model = partial.shape
    width = model // count

    def body(index_ref, ahead_ref, behind_ref, *refs):
        for own, came, out in zip((ahead_ref, behind_ref), refs[:-2], refs[-2:]):
            out[...] = (own[...].astype(F32) + came[...].astype(F32)).astype(BF16)

    def place(sign):
        return lambda j, i: (j, jnp.clip(i[0] + sign * distance, 0, count - 1))

    turns = 4
    whole = pl.BlockSpec((rows // turns, width), lambda j, i: (j, 0))
    shape = jax.ShapeDtypeStruct((rows, width), BF16)
    return pl.pallas_call(
        body,
        out_shape=[shape, shape],
        grid_spec=pltpu.PrefetchScalarGridSpec(
            num_scalar_prefetch=1,
            grid=(turns,),
            in_specs=[
                pl.BlockSpec((rows // turns, width), place(1)),
                pl.BlockSpec((rows // turns, width), place(-1)),
                whole,
                whole,
            ],
            out_specs=[whole, whole],
        ),
        compiler_params=granted(8),
        name="relay",
    )(index, partial, partial, *received)


def send_on(ahead, behind, distance, axis):
    count = lax.axis_size(axis)
    return (
        lax.ppermute(ahead, axis, [(i, i + 1) for i in range(count - distance)]),
        lax.ppermute(behind, axis, [(i, i - 1) for i in range(distance, count)]),
    )


def total(index, partial, received, hidden, row_block, count, filled):
    rows, model = partial.shape
    width = model // count
    turns = 4

    def body(index_ref, own_ref, ahead_ref, behind_ref, hidden_ref, *refs):
        summed = own_ref[...].astype(F32) + ahead_ref[...].astype(F32)
        summed = summed + behind_ref[...].astype(F32)
        refs[-1][...] = (summed + hidden_ref[...].astype(F32)).astype(BF16)

    block = (rows // turns, width)
    whole = pl.BlockSpec(block, lambda j, i: (j, 0))
    placed = pl.BlockSpec(block, lambda j, i: (row_block * turns + j, 0))
    return pl.pallas_call(
        body,
        out_shape=jax.ShapeDtypeStruct(hidden.shape, BF16),
        grid_spec=pltpu.PrefetchScalarGridSpec(
            num_scalar_prefetch=1,
            grid=(turns,),
            in_specs=[pl.BlockSpec(block, lambda j, i: (j, i[0])), whole, whole, placed]
            + [pl.BlockSpec(memory_space=pl.ANY)] * len(filled),
            out_specs=placed,
        ),
        input_output_aliases={5: 0} if filled else {},
        compiler_params=granted(8),
        name="total",
    )(index, partial, *received, hidden, *filled)


def on_device(
    hidden, norm_gain, gate_x_weight, state_weight, step_weight, conv_inner, conv_state,
    step_bias, decay_log, skip_gain, inner_gain, out_weight, initial_state,
):
    rows = hidden.shape[0]
    half = rows // 2
    inner = gate_x_weight.shape[2]
    state = state_weight.shape[2]
    heads = step_weight.shape[1]
    size = initial_state.shape[2]
    groups = state // size
    blocks = rows // SPAN
    feature_index = lax.axis_index("tp").reshape(1)
    range_index = lax.axis_index("seq")
    ranges = lax.axis_size("seq")

    model = step_weight.shape[0]
    parts_count = lax.axis_size("tp")
    wide = [gate_x_weight.reshape(model, 2 * inner)]
    narrow_weight = state_weight.reshape(model, 2 * state)
    step_rows = step_weight.T
    taps = jnp.concatenate([conv_inner, conv_state[:, 0]], axis=1)
    out_taps = conv_state[:, 1]
    start_state = initial_state.transpose(2, 0, 1).reshape(size, inner)
    gain = norm_gain.astype(F32)[None, :]
    out_gain = inner_gain[None, :]
    bias, rate, skip = step_bias[None, :], decay_log[None, :], skip_gain[None, :]

    late_pieces = [hidden[half:]]
    halo = shifted(hidden[rows - TAIL :], "seq", 1)
    early_pieces = [jnp.concatenate([halo, hidden[:half]], axis=0)]
    late_pieces = line_step(late_pieces * 2, 1, "tp")[1:]
    early_pieces = line_step(early_pieces * 2, 1, "tp")[1:]
    small = (wide, narrow_weight, step_rows, taps, start_state, gain, out_gain)
    for step in range(2, parts_count):
        early_pieces = line_step(early_pieces, step, "tp")
        late_pieces = line_step(late_pieces, step, "tp")
        if step == 2:
            held = lax.optimization_barrier((early_pieces[1:], late_pieces[1:], small))
            early_pieces[1:], late_pieces[1:], small = held
    wide, narrow_weight, step_rows, taps, start_state, gain, out_gain = small

    shape = jax.ShapeDtypeStruct
    weights = (wide, narrow_weight)

    def states(raw, steps, lead, earlier):
        part_rows = raw.shape[0] - lead
        sums = (
            [shape((size + TAIL, inner), BF16)]
            if earlier
            else [shape((size, inner), F32), shape((8, heads), F32)]
        )
        return call(
            state_body(inner, state, heads, groups, lead, bool(earlier)),
            [
                shape((part_rows, inner + state), BF16),
                shape((part_rows, heads), F32),
                shape((part_rows, heads), F32),
                shape((part_rows // SPAN, size, inner), F32),
                shape((8, heads), F32),
            ]
            + sums,
            raw,
            steps,
            taps,
            bias,
            rate,
            *earlier,
            scratch=[pltpu.VMEM((part_rows + 8, inner + state), F32)],
            name="states",
        )

    def within(conv, step, cum, raw, lead, rim):
        part_rows = raw.shape[0] - lead
        return call(
            within_body(inner, state, heads, groups, lead),
            [shape((part_rows, inner), F32), shape((part_rows, state), BF16)],
            conv,
            step,
            cum,
            raw,
            out_taps,
            skip,
            *rim,
            scratch=[pltpu.VMEM((part_rows + 8, state), F32)],
            name="within",
        )

    early_first, early_step, early, early_scale = project_first(
        early_pieces, feature_index, gain, *weights, step_rows, inner, state
    )
    *early_states, early_sum, early_log = states(early_first, early_step, TAIL, ())
    held = lax.optimization_barrier(
        (late_pieces[-2:], early, early_states, early_sum, early_log)
    )
    late_pieces[-2:], early, early_states, early_sum, early_log = held
    late_first, late_step, late, late_scale = project_first(
        late_pieces, feature_index, gain, *weights, step_rows, inner, state
    )
    *late_states, message = states(
        late_first, late_step, 0, (rim_of(early_first), early_sum, early_log)
    )
    early_second, late_second = project_second(
        (early, late), (early_scale, late_scale), *weights, inner, state
    )
    before = ()
    bit = 1
    while True:
        came = swapped(message, "seq", bit)
        if bit == 2:
            held = lax.optimization_barrier((came, early_second, late_second))
            came, early_second, late_second = held
            inside = [
                within(*early_states[:3], early_second, TAIL, ()),
                within(*late_states[:3], late_second, 0, (rim_of(early_second),)),
            ]
        later = ((range_index // bit) % 2).astype(jnp.int32).reshape(1)
        bit *= 2
        if bit == ranges:
            break
        message, *before = call(
            combine_body(size, not before),
            [
                shape((size + TAIL, inner), BF16),
                shape((size, inner), F32),
                shape((8, inner), F32),
            ],
            later,
            message,
            came,
            *before,
            scalars=1,
            name="combine",
        )
    entering = (came, *before, start_state)
    partials, received = [], []
    for k, (second, lead) in enumerate(((early_second, TAIL), (late_second, 0))):
        _, _, cum, update, block_log = (early_states, late_states)[k]
        out, maps = inside[k]
        partial, top, bottom, *entering = finish(
            k == 1, lead, feature_index, later, entering, update, block_log, cum, maps, out,
            second, out_gain, out_weight, inner, state, heads, groups, parts_count,
        )
        partials.append(partial)
        received.append(send_on(top, bottom, parts_count - 1, "tp"))
    for distance in range(parts_count - 2, 0, -1):
        for k, partial in enumerate(partials):
            onward = relay(feature_index, distance, partial, received[k], parts_count)
            received[k] = send_on(*onward, distance, "tp")
    filled = ()
    for k, partial in enumerate(partials):
        filled = (
            total(feature_index, partial, received[k], hidden, k, parts_count, filled),
        )
    return filled[0]


def solution(mesh):
    return jax.shard_map(
        on_device,
        mesh=mesh,
        in_specs=(
            P("seq", "tp"),
            P(),
            P(None, None, "tp"),
            P(None, None, "tp"),
            P(None, "tp"),
            P(None, "tp"),
            P(None, None, "tp"),
            P("tp"),
            P("tp"),
            P("tp"),
            P("tp"),
            P("tp", None),
            P("tp", None, None),
        ),
        out_specs=P("seq", "tp"),
        check_vma=False,
    )
```

```python
import jax
import jax.numpy as jnp
from jax import lax
from jax.experimental import pallas as pl
from jax.experimental.pallas import tpu as pltpu
from jax.sharding import PartitionSpec as P

SPAN = 128
EPSILON = 1e-05
TAIL = 16
LANES = 128
F32 = jnp.float32
BF16 = jnp.bfloat16


def shifted(block, axis, distance):
    count = lax.axis_size(axis)
    route = [(i, i + distance) for i in range(count) if 0 <= i + distance < count]
    return lax.ppermute(block, axis, route)


def swapped(block, axis, bit):
    return lax.ppermute(block, axis, [(i, i ^ bit) for i in range(lax.axis_size(axis))])


def line_step(pieces, step, axis):
    count = lax.axis_size(axis)
    behind, ahead = pieces[-2], pieces[-1]
    behind = lax.ppermute(behind, axis, [(i, i + 1) for i in range(step - 1, count - 1)])
    ahead = lax.ppermute(ahead, axis, [(i, i - 1) for i in range(1, count - step + 1)])
    return pieces + [behind, ahead]


def whole_spec(array):
    rank = len(array.shape)
    return pl.BlockSpec(array.shape, lambda *_: (0,) * rank)


def once_spec(array):
    rank = len(array.shape)
    once = pl.Buffered(1)
    return pl.BlockSpec(array.shape, lambda *_: (0,) * rank, pipeline_mode=once)


def call(body, outs, *arrays, scratch=(), scalars=0, name=None, limit=60):
    pairs = [a if isinstance(a, tuple) else (a, whole_spec(a)) for a in arrays[scalars:]]
    return pl.pallas_call(
        body,
        out_shape=outs,
        grid=(1,),
        in_specs=[pl.BlockSpec(memory_space=pltpu.SMEM)] * scalars + [spec for _, spec in pairs],
        out_specs=jax.tree.map(whole_spec, outs),
        scratch_shapes=list(scratch),
        compiler_params=granted(limit),
        name=name,
    )(*arrays[:scalars], *[a for a, _ in pairs])


def granted(mebibytes):
    return pltpu.CompilerParams(vmem_limit_bytes=mebibytes * 2**20)


def dot(a, b, contract=((1,), (0,))):
    return lax.dot_general(a, b, (contract, ((), ())), preferred_element_type=F32)


def parts_of(x, count):
    parts = []
    for _ in range(count):
        part = x.astype(BF16)
        parts.append(part)
        x = x - part.astype(F32)
    return parts


def spread(x, expand, count=2):
    total = None
    for part in parts_of(x, count):
        term = dot(part, expand)
        total = term if total is None else total + term
    return total


def expander(heads, width, first=0, count=None):
    lanes = (count or heads) * width
    head = lax.broadcasted_iota(jnp.int32, (heads, lanes), 0) - first
    lane = lax.broadcasted_iota(jnp.int32, (heads, lanes), 1)
    inside = jnp.logical_and(lane >= head * width, lane < (head + 1) * width)
    return jnp.where(inside, 1.0, 0.0).astype(BF16)


def silu(v):
    return v * (1.0 / (1.0 + jnp.exp(-v)))


def conv_block(padded_ref, start, taps_ref, columns):
    summed = None
    for k in range(taps_ref.shape[0]):
        row = 8 + start - (taps_ref.shape[0] - 1) + k
        term = taps_ref[k : k + 1, columns].astype(F32) * padded_ref[row : row + SPAN, columns]
        summed = term if summed is None else summed + term
    return silu(summed).astype(BF16)


def rows_in(ref, raw, rim_refs, lead):
    if lead:
        ref[0:8, :] = raw[lead - 8 : lead, :].astype(F32)
    else:
        ref[0:8, :] = rim_refs[0][TAIL - 8 : TAIL, :].astype(F32)
    ref[8:, :] = raw[lead:, :].astype(F32)


def enter(
    pieces, lead, index, gain, wide, narrow, steps, taps, bias, rate, earlier, inner, state, size
):
    total_rows, width = pieces[0].shape
    rows = total_rows - lead
    model, heads = steps.shape[1], steps.shape[0]
    count = model // width
    head_width = inner // heads
    groups = state // size
    turns = inner // state
    turn_heads = heads // turns
    blocks = rows // SPAN
    offsets = [(k + 1) // 2 * (-1) ** (k % 2) for k in range(len(pieces))]

    def body(index_ref, gain_ref, *refs):
        parts, refs = refs[: len(offsets)], refs[len(offsets) :]
        wide_ref, narrow_ref, steps_ref, taps_ref, bias_ref, rate_ref, *refs = refs
        rim_refs, refs = (refs[:3], refs[3:]) if earlier else ((), refs)
        conv_ref, step_ref, cum_ref, update_ref, block_log_ref, scaled_ref, scale_ref, *refs = refs
        *sums, square_ref, raw_ref, padded_ref, maps_ref, factor_ref, log_ref = refs
        turn = pl.program_id(0)

        @pl.when(turn == 0)
        def _():
            square_ref[...] = jnp.zeros_like(square_ref)
            for part, offset in zip(parts, offsets):
                target = index_ref[0] + offset

                @pl.when(jnp.logical_and(target >= 0, target < count))
                def _():
                    def columns(k, carry):
                        here = pl.ds(pl.multiple_of(k * LANES, LANES), LANES)
                        there = pl.ds(pl.multiple_of(target * width + k * LANES, LANES), LANES)
                        value = part[:, here].astype(F32)
                        square_ref[...] += value * value
                        scaled_ref[:, there] = (value * gain_ref[:, there]).astype(BF16)
                        return carry

                    lax.fori_loop(0, width // LANES, columns, 0)

            moment = jnp.sum(square_ref[...], axis=-1, keepdims=True) * (1.0 / model)
            scale_ref[...] = jnp.broadcast_to(lax.rsqrt(moment + EPSILON), scale_ref.shape)
            raw_ref[...] = (dot(scaled_ref[...], narrow_ref[...]) * scale_ref[:, 0:1]).astype(BF16)
            raw_step = dot(scaled_ref[...], steps_ref[...], ((1,), (1,)))
            raw_step = (raw_step * scale_ref[:, 0:heads]).astype(BF16)
            row = lax.broadcasted_iota(jnp.int32, (SPAN, SPAN), 0)
            col = lax.broadcasted_iota(jnp.int32, (SPAN, SPAN), 1)
            lower = jnp.where(row >= col, 1.0, 0.0).astype(BF16)
            block_log_ref[...] = jnp.zeros_like(block_log_ref)
            total_log = rim_refs[2][0:1, :] if earlier else jnp.zeros((1, heads), F32)
            for b in range(blocks):
                here = slice(b * SPAN, (b + 1) * SPAN)
                pre = raw_step[lead + b * SPAN : lead + (b + 1) * SPAN, :].astype(F32)
                pre = pre + bias_ref[...]
                step = jnp.maximum(pre, 0.0) + jnp.log1p(jnp.exp(-jnp.abs(pre)))
                log_decay = -step * jnp.exp(rate_ref[...])
                cum = None
                for part in parts_of(log_decay, 3):
                    term = dot(lower, part)
                    cum = term if cum is None else cum + term
                last = cum[SPAN - 1 : SPAN, :]
                step_ref[here, :] = step
                cum_ref[here, :] = cum
                block_log_ref[b : b + 1, :] = last
                factor_ref[here, :] = step * jnp.exp(last - cum)
                total_log = total_log + last
            log_ref[...] = jnp.broadcast_to(total_log, log_ref.shape)

        @pl.when(turn > 0)
        def _():
            raw_ref[...] = (dot(scaled_ref[...], wide_ref[...]) * scale_ref[:, 0:1]).astype(BF16)

        rows_in(padded_ref, raw_ref[...], rim_refs, lead)
        for b in range(blocks):
            conv_ref[b * SPAN : (b + 1) * SPAN, :] = conv_block(
                padded_ref, b * SPAN, taps_ref, slice(0, state)
            )
        if not earlier:
            sums[2][...] = raw_ref[total_rows - TAIL :, :]

        @pl.when(turn == 0)
        def _():
            maps_ref[...] = conv_ref[...]

        for k in range(turns):

            @pl.when(turn == 1 + k)
            def _():
                group = k * state * groups // inner
                expand = expander(heads, head_width, k * turn_heads, turn_heads)
                keep = jnp.exp(spread(block_log_ref[...], expand, 3))
                total = rim_refs[1][...] if earlier else None
                for b in range(blocks):
                    here = slice(b * SPAN, (b + 1) * SPAN)
                    factor = spread(factor_ref[here, :], expand)
                    scaled = (conv_ref[here, :].astype(F32) * factor).astype(BF16)
                    maps = maps_ref[here, group * size : (group + 1) * size]
                    update = dot(maps, scaled, ((0,), (0,)))
                    update_ref[b] = update
                    total = update if total is None else keep[b : b + 1, :] * total + update
                if earlier:
                    sums[0][0:size, :] = total.astype(BF16)
                    log = spread(log_ref[...], expand, 3)[0:1, :]
                    sums[0][size : size + TAIL, :] = log_rows(log)
                else:
                    sums[0][...] = total
                    sums[1][...] = log_ref[...]

    shape = jax.ShapeDtypeStruct

    def any_turn(j):
        return jnp.where(j == 0, turns, j - 1)

    def wide_turn(j):
        return jnp.maximum(j, 1) - 1

    ends = [pl.BlockSpec((TAIL, state), lambda j: (0, any_turn(j)))]
    ends += [pl.BlockSpec((size, state), lambda j: (0, wide_turn(j)))]
    ends += [pl.BlockSpec((8, heads), lambda j: (0, 0))]
    if earlier:
        sums = [shape((size + TAIL, inner), BF16)]
        sum_specs = [pl.BlockSpec((size + TAIL, state), lambda j: (0, wide_turn(j)))]
    else:
        sums = [shape((size, inner), F32), shape((8, heads), F32), shape((TAIL, inner + state), BF16)]
        sum_specs = [ends[1], ends[2], ends[0]]
    plain = [
        shape((rows, heads), F32),
        shape((rows, heads), F32),
        shape((blocks, size, inner), F32),
        shape((8, heads), F32),
        shape((total_rows, model), BF16),
        shape((total_rows, LANES), F32),
    ]
    plain_specs = [whole_spec(a) for a in plain]
    plain_specs[2] = pl.BlockSpec((blocks, size, state), lambda j: (0, 0, wide_turn(j)))
    return pl.pallas_call(
        body,
        grid=(1 + turns,),
        out_shape=[shape((rows, inner + state), BF16)] + plain + sums,
        in_specs=[pl.BlockSpec(memory_space=pltpu.SMEM), once_spec(gain)]
        + [once_spec(piece) for piece in pieces]
        + [
            pl.BlockSpec((model, state), lambda j: (0, turns + wide_turn(j))),
            pl.BlockSpec((model, state), lambda j: (0, 0), pipeline_mode=pl.Buffered(1)),
            once_spec(steps),
            pl.BlockSpec((taps.shape[0], state), lambda j: (0, any_turn(j))),
            once_spec(bias),
            once_spec(rate),
        ]
        + (ends if earlier else []),
        out_specs=[pl.BlockSpec((rows, state), lambda j: (0, any_turn(j)))]
        + plain_specs
        + sum_specs,
        scratch_shapes=[
            pltpu.VMEM((total_rows, LANES), F32),
            pltpu.VMEM((total_rows, state), BF16),
            pltpu.VMEM((rows + 8, state), F32),
            pltpu.VMEM((rows, state), BF16),
            pltpu.VMEM((rows, heads), F32),
            pltpu.VMEM((8, heads), F32),
        ],
        compiler_params=granted(60),
        name="enter",
    )(index, gain, *pieces, wide, narrow, steps, taps, bias, rate, *earlier)


def inside(
    scaled, scale, lead, wide, narrow, taps, skip, conv, step, cum, rim, inner, state, size
):
    total_rows, model = scaled.shape
    rows = total_rows - lead
    heads = step.shape[1]
    width = inner // heads
    groups = state // size
    turns = inner // state
    turn_heads = heads // turns
    blocks = rows // SPAN

    def body(
        scaled_ref, scale_ref, wide_ref, narrow_ref, taps_ref, skip_ref, conv_ref, step_ref,
        cum_ref, *refs,
    ):
        rim_refs, refs = refs[: len(rim)], refs[len(rim) :]
        out_ref, gate_ref, maps_ref, *tail, padded_ref, scores_ref, rows_ref = refs
        turn = pl.program_id(0)

        @pl.when(turn == 0)
        def _():
            raw = (dot(scaled_ref[...], narrow_ref[...]) * scale_ref[:, 0:1]).astype(BF16)
            rows_in(padded_ref, raw, rim_refs, lead)
            if tail:
                tail[0][...] = raw[total_rows - TAIL :, :]
            for b in range(blocks):
                here = slice(b * SPAN, (b + 1) * SPAN)
                maps_ref[here, :] = conv_block(padded_ref, b * SPAN, taps_ref, slice(0, state))
                for g in range(groups):
                    cols = slice(g * size, (g + 1) * size)
                    in_map = conv_ref[here, inner + g * size : inner + (g + 1) * size]
                    scores_ref[b, g] = dot(maps_ref[here, cols], in_map, ((1,), (1,)))
                padding = jnp.zeros((SPAN, SPAN - heads), F32)
                rows_ref[b] = jnp.concatenate([cum_ref[here, :], padding], axis=1).T

        row = lax.broadcasted_iota(jnp.int32, (SPAN, SPAN), 0)
        col = lax.broadcasted_iota(jnp.int32, (SPAN, SPAN), 1)
        causal = row >= col
        lane = lax.broadcasted_iota(jnp.int32, (SPAN, 2 * width), 1)
        for k in range(turns):

            @pl.when(turn == 1 + k)
            def _():
                raw = dot(scaled_ref[lead:, :], wide_ref[...]) * scale_ref[lead:, 0:1]
                gate_ref[...] = raw.astype(BF16)
                first = k * turn_heads
                expand = expander(heads, width, first, turn_heads)
                skips = spread(jnp.broadcast_to(skip_ref[...], (8, heads)), expand, 3)[0:1, :]
                for b in range(blocks):
                    here = slice(b * SPAN, (b + 1) * SPAN)
                    steps = spread(step_ref[here, :], expand)
                    cum = cum_ref[here, :]
                    for pair in range(turn_heads // 2):
                        head = first + 2 * pair
                        scores = scores_ref[b, head * groups // heads]
                        cols = slice(2 * pair * width, (2 * pair + 2) * width)
                        x = conv_ref[here, head * width : (head + 2) * width].astype(F32)
                        stepped = x * steps[:, cols]
                        weighted = []
                        for h in (head, head + 1):
                            gap = cum[:, h : h + 1] - rows_ref[b, h : h + 1, :]
                            decay = jnp.exp(jnp.where(causal, gap, -1e30))
                            weighted.append((scores * decay).astype(BF16))
                        stacked = jnp.concatenate(
                            [
                                jnp.where(lane < width, stepped, 0.0).astype(BF16),
                                jnp.where(lane < width, 0.0, stepped).astype(BF16),
                            ],
                            axis=0,
                        )
                        out = dot(jnp.concatenate(weighted, axis=1), stacked)
                        out_ref[here, cols] = out + skips[:, cols] * x

    def wide_turn(j):
        return jnp.maximum(j, 1) - 1

    shape = jax.ShapeDtypeStruct
    outs = [shape((rows, inner), F32), shape((rows, inner), BF16), shape((rows, state), BF16)]
    outs += [] if rim else [shape((TAIL, state), BF16)]
    turned = pl.BlockSpec((rows, state), lambda j: (0, wide_turn(j)))
    return pl.pallas_call(
        body,
        grid=(1 + turns,),
        out_shape=outs,
        in_specs=[
            once_spec(scaled),
            once_spec(scale),
            pl.BlockSpec((model, state), lambda j: (0, wide_turn(j))),
            pl.BlockSpec((model, state), lambda j: (0, 1), pipeline_mode=pl.Buffered(1)),
        ]
        + [once_spec(a) for a in (taps, skip, conv, step, cum, *rim)],
        out_specs=[turned, turned] + [whole_spec(a) for a in outs[2:]],
        scratch_shapes=[
            pltpu.VMEM((rows + 8, state), F32),
            pltpu.VMEM((blocks, groups, SPAN, SPAN), F32),
            pltpu.VMEM((blocks, SPAN, SPAN), F32),
        ],
        compiler_params=granted(60),
        name="inside",
    )(scaled, scale, wide, narrow, taps, skip, conv, step, cum, *rim)


def log_rows(log):
    row = lax.broadcasted_iota(jnp.int32, (TAIL, log.shape[1]), 0)
    block = jnp.zeros((TAIL, log.shape[1]), F32)
    for k, part in enumerate(parts_of(log, 3)):
        block = jnp.where(row == k, part.astype(F32), block)
    return block.astype(BF16)


def log_of(message_ref, size):
    rows = message_ref[size : size + TAIL, :].astype(F32)
    return rows[0:1, :] + rows[1:2, :] + rows[2:3, :]


def combine_body(size, first):
    def body(later_ref, mine_ref, came_ref, *refs):
        if first:
            out_ref, before_ref, before_log_ref = refs
        else:
            prior_ref, prior_log_ref, out_ref, before_ref, before_log_ref = refs
        mine = mine_ref[0:size, :].astype(F32)
        came = came_ref[0:size, :].astype(F32)
        my_log, came_log = log_of(mine_ref, size), log_of(came_ref, size)

        @pl.when(later_ref[0] == 1)
        def _():
            out_ref[0:size, :] = (jnp.exp(my_log) * came + mine).astype(BF16)
            if first:
                before_ref[...] = came
                before_log_ref[0:1, :] = came_log
            else:
                before_ref[...] = jnp.exp(prior_log_ref[0:1, :]) * came + prior_ref[...]
                before_log_ref[0:1, :] = prior_log_ref[0:1, :] + came_log

        @pl.when(later_ref[0] == 0)
        def _():
            out_ref[0:size, :] = (jnp.exp(came_log) * mine + came).astype(BF16)
            if first:
                before_ref[...] = jnp.zeros_like(before_ref)
                before_log_ref[0:1, :] = jnp.zeros_like(came_log)
            else:
                before_ref[...] = prior_ref[...]
                before_log_ref[0:1, :] = prior_log_ref[0:1, :]

        out_ref[size : size + TAIL, :] = log_rows(my_log + came_log)

    return body


def finish(
    last_part, lead, index, later, entering, update, block_log, cum, maps, within, second, gain,
    out_weight, inner, state, heads, groups, count,
):
    size = state // groups
    width = inner // heads
    rows = second.shape[0] - lead
    blocks = rows // SPAN
    model = out_weight.shape[1]
    turn_width = model // count
    first = len(entering) > 1

    def body(index_ref, later_ref, *refs):
        entering_refs, refs = refs[: len(entering)], refs[len(entering) :]
        (
            update_ref, block_log_ref, cum_ref, maps_ref, within_ref, second_ref, gain_ref,
            weight_ref, out_ref, top_ref, bottom_ref, *memory_out, mixed_ref,
        ) = refs

        @pl.when(pl.program_id(0) == 0)
        def _():
            expand = expander(heads, width)
            if first:
                came_ref, before_ref, before_log_ref, start_ref = entering_refs
                is_later = later_ref[0] == 1
                prior_log = before_log_ref[0:1, :]
                prior = before_ref[...]
                came = came_ref[0:size, :].astype(F32)
                came_log = log_of(came_ref, size)
                memory = jnp.where(is_later, jnp.exp(prior_log) * came + prior, prior)
                memory_log = jnp.where(is_later, prior_log + came_log, prior_log)
                memory = jnp.exp(memory_log) * start_ref[...] + memory
            else:
                memory = entering_refs[0][...]
            keep = jnp.exp(spread(block_log_ref[...], expand, 3))
            for b in range(blocks):
                here = slice(b * SPAN, (b + 1) * SPAN)
                reach = spread(jnp.exp(cum_ref[here, :]), expand)
                for g in range(groups):
                    cols = slice(g * inner // groups, (g + 1) * inner // groups)
                    carried = dot(
                        maps_ref[here, g * size : (g + 1) * size], memory[:, cols].astype(BF16)
                    )
                    scan = within_ref[here, cols] + reach[:, cols] * carried
                    gate = second_ref[lead + b * SPAN : lead + (b + 1) * SPAN, cols]
                    gated = scan * silu(gate.astype(F32))
                    moment = jnp.mean(gated * gated, axis=-1, keepdims=True)
                    mixed_ref[here, cols] = (
                        gated * lax.rsqrt(moment + EPSILON) * gain_ref[:, cols].astype(F32)
                    ).astype(BF16)
                if not last_part or b < blocks - 1:
                    memory = keep[b : b + 1, :] * memory + update_ref[b]
            if memory_out:
                memory_out[0][...] = memory

        sent = dot(mixed_ref[...], weight_ref[...]).astype(BF16)
        out_ref[...] = sent
        target = farthest(pl.program_id(0), index_ref)

        @pl.when(target == count - 1)
        def _():
            top_ref[...] = sent

        @pl.when(target == 0)
        def _():
            bottom_ref[...] = sent

    def farthest(j, index_ref):
        index = index_ref[0]
        low, high = jnp.int32(0), jnp.int32(count - 1)
        chosen = low
        for k in range(count):
            up = high - index >= index - low
            pick = jnp.where(up, high, low)
            chosen = jnp.where(j == k, pick, chosen)
            high = jnp.where(up, high - 1, high)
            low = jnp.where(up, low, low + 1)
        return chosen

    shape = jax.ShapeDtypeStruct
    extra = [shape((rows, turn_width), BF16)] * 2
    extra += [] if last_part else [shape((size, inner), F32)]

    return pl.pallas_call(
        body,
        out_shape=[shape((rows, model), BF16)] + extra,
        grid_spec=pltpu.PrefetchScalarGridSpec(
            num_scalar_prefetch=2,
            grid=(count,),
            in_specs=[once_spec(a) for a in entering]
            + [
                once_spec(update),
                once_spec(block_log),
                once_spec(cum),
                once_spec(maps),
                once_spec(within),
                once_spec(second),
                once_spec(gain),
                pl.BlockSpec((inner, turn_width), lambda j, i, _: (0, farthest(j, i))),
            ],
            out_specs=[pl.BlockSpec((rows, turn_width), lambda j, i, _: (0, farthest(j, i)))]
            + [whole_spec(a) for a in extra],
            scratch_shapes=[pltpu.VMEM((rows, inner), BF16)],
        ),
        compiler_params=granted(60),
        name="finish",
    )(
        index, later, *entering, update, block_log, cum, maps, within, second, gain, out_weight
    )


def relay(index, distance, partial, received, count):
    rows, model = partial.shape
    width = model // count

    def body(index_ref, ahead_ref, behind_ref, *refs):
        for own, came, out in zip((ahead_ref, behind_ref), refs[:-2], refs[-2:]):
            out[...] = (own[...].astype(F32) + came[...].astype(F32)).astype(BF16)

    def place(sign):
        return lambda j, i: (j, jnp.clip(i[0] + sign * distance, 0, count - 1))

    turns = 4
    whole = pl.BlockSpec((rows // turns, width), lambda j, i: (j, 0))
    shape = jax.ShapeDtypeStruct((rows, width), BF16)
    return pl.pallas_call(
        body,
        out_shape=[shape, shape],
        grid_spec=pltpu.PrefetchScalarGridSpec(
            num_scalar_prefetch=1,
            grid=(turns,),
            in_specs=[
                pl.BlockSpec((rows // turns, width), place(1)),
                pl.BlockSpec((rows // turns, width), place(-1)),
                whole,
                whole,
            ],
            out_specs=[whole, whole],
        ),
        compiler_params=granted(8),
        name="relay",
    )(index, partial, partial, *received)


def send_on(ahead, behind, distance, axis):
    count = lax.axis_size(axis)
    return (
        lax.ppermute(ahead, axis, [(i, i + 1) for i in range(count - distance)]),
        lax.ppermute(behind, axis, [(i, i - 1) for i in range(distance, count)]),
    )


def total(index, partial, received, hidden, row_block, count, filled):
    rows, model = partial.shape
    width = model // count
    turns = 4

    def body(index_ref, own_ref, ahead_ref, behind_ref, hidden_ref, *refs):
        summed = own_ref[...].astype(F32) + ahead_ref[...].astype(F32)
        summed = summed + behind_ref[...].astype(F32)
        refs[-1][...] = (summed + hidden_ref[...].astype(F32)).astype(BF16)

    block = (rows // turns, width)
    whole = pl.BlockSpec(block, lambda j, i: (j, 0))
    placed = pl.BlockSpec(block, lambda j, i: (row_block * turns + j, 0))
    return pl.pallas_call(
        body,
        out_shape=jax.ShapeDtypeStruct(hidden.shape, BF16),
        grid_spec=pltpu.PrefetchScalarGridSpec(
            num_scalar_prefetch=1,
            grid=(turns,),
            in_specs=[pl.BlockSpec(block, lambda j, i: (j, i[0])), whole, whole, placed]
            + [pl.BlockSpec(memory_space=pl.ANY)] * len(filled),
            out_specs=placed,
        ),
        input_output_aliases={5: 0} if filled else {},
        compiler_params=granted(8),
        name="total",
    )(index, partial, *received, hidden, *filled)


def on_device(
    hidden, norm_gain, gate_x_weight, state_weight, step_weight, conv_inner, conv_state,
    step_bias, decay_log, skip_gain, inner_gain, out_weight, initial_state,
):
    rows = hidden.shape[0]
    half = rows // 2
    inner = gate_x_weight.shape[2]
    state = state_weight.shape[2]
    heads = step_weight.shape[1]
    size = initial_state.shape[2]
    groups = state // size
    blocks = rows // SPAN
    feature_index = lax.axis_index("tp").reshape(1)
    range_index = lax.axis_index("seq")
    ranges = lax.axis_size("seq")

    model = step_weight.shape[0]
    parts_count = lax.axis_size("tp")
    narrow_weight = state_weight.reshape(model, 2 * state)
    step_rows = step_weight.T
    taps = jnp.concatenate([conv_inner, conv_state[:, 0]], axis=1)
    out_taps = conv_state[:, 1]
    start_state = initial_state.transpose(2, 0, 1).reshape(size, inner)
    gain = norm_gain.astype(F32)[None, :]
    out_gain = inner_gain[None, :]
    bias, rate, skip = step_bias[None, :], decay_log[None, :], skip_gain[None, :]

    late_pieces = [hidden[half:]]
    halo = shifted(hidden[rows - TAIL :], "seq", 1)
    early_pieces = [jnp.concatenate([halo, hidden[:half]], axis=0)]
    late_pieces = line_step(late_pieces * 2, 1, "tp")[1:]
    early_pieces = line_step(early_pieces * 2, 1, "tp")[1:]
    small = (narrow_weight, step_rows, taps, start_state, gain, out_gain)
    late_pieces[1:], small = lax.optimization_barrier((late_pieces[1:], small))
    narrow_weight, step_rows, taps, start_state, gain, out_gain = small
    for step in range(2, parts_count):
        early_pieces = line_step(early_pieces, step, "tp")
        if step == 2:
            held = lax.optimization_barrier((early_pieces[-2:], gate_x_weight))
            early_pieces[-2:], gate_x_weight = held
            wide = gate_x_weight.reshape(model, 2 * inner)
        late_pieces = line_step(late_pieces, step, "tp")
        if step == 2:
            late_pieces[1:], wide = lax.optimization_barrier((late_pieces[1:], wide))

    shape = jax.ShapeDtypeStruct

    def entered(pieces, lead, earlier):
        return enter(
            pieces, lead, feature_index, gain, wide, narrow_weight, step_rows, taps, bias, rate,
            earlier, inner, state, size,
        )

    early = entered(early_pieces, TAIL, ())
    late_pieces[-2:], early = lax.optimization_barrier((late_pieces[-2:], early))
    *early, early_sum, early_log, rim = early
    *late, message = entered(late_pieces, 0, (rim, early_sum, early_log))

    def within(part, lead, rim):
        conv, step, cum, _, _, scaled, scale = part
        return inside(
            scaled, scale, lead, wide, narrow_weight, out_taps, skip, conv, step, cum, rim,
            inner, state, size,
        )

    *early_out, rim = within(early, TAIL, ())
    late_out = within(late, 0, (rim,))
    before = ()
    bit = 1
    while True:
        came = swapped(message, "seq", bit)
        if bit == 2:
            came, early_out, rim = lax.optimization_barrier((came, early_out, rim))
            late_out = within(late, 0, (rim,))
        later = ((range_index // bit) % 2).astype(jnp.int32).reshape(1)
        bit *= 2
        if bit == ranges:
            break
        message, *before = call(
            combine_body(size, not before),
            [
                shape((size + TAIL, inner), BF16),
                shape((size, inner), F32),
                shape((8, inner), F32),
            ],
            later,
            message,
            came,
            *before,
            scalars=1,
            name="combine",
            limit=14,
        )
    entering = (came, *before, start_state)
    partials, received = [], []
    for k, (part, (out, gate, maps)) in enumerate(((early, early_out), (late, late_out))):
        _, _, cum, update, block_log, _, _ = part
        partial, top, bottom, *entering = finish(
            k == 1, 0, feature_index, later, entering, update, block_log, cum, maps, out,
            gate, out_gain, out_weight, inner, state, heads, groups, parts_count,
        )
        partials.append(partial)
        received.append(send_on(top, bottom, parts_count - 1, "tp"))
    for distance in range(parts_count - 2, 0, -1):
        for k, partial in enumerate(partials):
            onward = relay(feature_index, distance, partial, received[k], parts_count)
            received[k] = send_on(*onward, distance, "tp")
    filled = ()
    for k, partial in enumerate(partials):
        filled = (
            total(feature_index, partial, received[k], hidden, k, parts_count, filled),
        )
    return filled[0]


def solution(mesh):
    return jax.shard_map(
        on_device,
        mesh=mesh,
        in_specs=(
            P("seq", "tp"),
            P(),
            P(None, None, "tp"),
            P(None, None, "tp"),
            P(None, "tp"),
            P(None, "tp"),
            P(None, None, "tp"),
            P("tp"),
            P("tp"),
            P("tp"),
            P("tp"),
            P("tp", None),
            P("tp", None, None),
        ),
        out_specs=P("seq", "tp"),
        check_vma=False,
    )
```

```python
import jax
import jax.numpy as jnp
from jax import lax
from jax.experimental import pallas as pl
from jax.experimental.pallas import tpu as pltpu
from jax.sharding import PartitionSpec as P

SPAN = 128
EPSILON = 1e-05
TAIL = 16
LANES = 128
F32 = jnp.float32
BF16 = jnp.bfloat16


def shifted(block, axis, distance):
    count = lax.axis_size(axis)
    route = [(i, i + distance) for i in range(count) if 0 <= i + distance < count]
    return lax.ppermute(block, axis, route)


def swapped(block, axis, bit):
    return lax.ppermute(block, axis, [(i, i ^ bit) for i in range(lax.axis_size(axis))])


def line_step(pieces, step, axis):
    count = lax.axis_size(axis)
    behind, ahead = pieces[-2], pieces[-1]
    behind = lax.ppermute(behind, axis, [(i, i + 1) for i in range(step - 1, count - 1)])
    ahead = lax.ppermute(ahead, axis, [(i, i - 1) for i in range(1, count - step + 1)])
    return pieces + [behind, ahead]


def whole_spec(array):
    rank = len(array.shape)
    return pl.BlockSpec(array.shape, lambda *_: (0,) * rank)


def once_spec(array):
    rank = len(array.shape)
    once = pl.Buffered(1)
    return pl.BlockSpec(array.shape, lambda *_: (0,) * rank, pipeline_mode=once)


def call(body, outs, *arrays, scratch=(), scalars=0, name=None, limit=60):
    pairs = [a if isinstance(a, tuple) else (a, whole_spec(a)) for a in arrays[scalars:]]
    return pl.pallas_call(
        body,
        out_shape=outs,
        grid=(1,),
        in_specs=[pl.BlockSpec(memory_space=pltpu.SMEM)] * scalars + [spec for _, spec in pairs],
        out_specs=jax.tree.map(whole_spec, outs),
        scratch_shapes=list(scratch),
        compiler_params=granted(limit),
        name=name,
    )(*arrays[:scalars], *[a for a, _ in pairs])


def granted(mebibytes):
    return pltpu.CompilerParams(vmem_limit_bytes=mebibytes * 2**20)


def dot(a, b, contract=((1,), (0,))):
    return lax.dot_general(a, b, (contract, ((), ())), preferred_element_type=F32)


def parts_of(x, count):
    parts = []
    for _ in range(count):
        part = x.astype(BF16)
        parts.append(part)
        x = x - part.astype(F32)
    return parts


def spread(x, expand, count=2):
    parts = [part.astype(F32) for part in parts_of(x, count)]
    return dot(
        jnp.concatenate(parts, axis=1).astype(BF16), jnp.concatenate([expand] * count, axis=0)
    )


def expander(heads, width, first=0, count=None):
    lanes = (count or heads) * width
    head = lax.broadcasted_iota(jnp.int32, (heads, lanes), 0) - first
    lane = lax.broadcasted_iota(jnp.int32, (heads, lanes), 1)
    inside = jnp.logical_and(lane >= head * width, lane < (head + 1) * width)
    return jnp.where(inside, 1.0, 0.0).astype(BF16)


def silu(v):
    return v * (1.0 / (1.0 + jnp.exp(-v)))


def conv_block(padded_ref, start, taps_ref, columns):
    summed = None
    for k in range(taps_ref.shape[0]):
        row = 8 + start - (taps_ref.shape[0] - 1) + k
        term = taps_ref[k : k + 1, columns].astype(F32) * padded_ref[row : row + SPAN, columns]
        summed = term if summed is None else summed + term
    return silu(summed).astype(BF16)


def rows_in(ref, raw, lead):
    ref[0:8, :] = raw[lead - 8 : lead, :].astype(F32)
    ref[8:, :] = raw[lead:, :].astype(F32)


def scale_in(piece, gain_ref, square_ref, scaled_ref, gain_start, start, width):
    def columns(k, carry):
        here = pl.ds(pl.multiple_of(k * LANES, LANES), LANES)
        there = pl.ds(pl.multiple_of(start + k * LANES, LANES), LANES)
        gain = gain_ref[:, pl.ds(pl.multiple_of(gain_start + k * LANES, LANES), LANES)]
        value = piece(here)
        square_ref[...] += value * value
        scaled_ref[:, there] = (value * gain).astype(BF16)
        return carry

    lax.fori_loop(0, width // LANES, columns, 0)


def row_starts(pieces):
    starts = [0]
    for piece in pieces:
        starts.append(starts[-1] + piece.shape[0])
    return starts


def begin(row_parts, index, gain, wide, narrow, steps, inner, state):
    starts = row_starts([part[0] for part in row_parts])
    rows, width = starts[-1], row_parts[0][0].shape[1]
    per_part = len(row_parts[0])
    pieces = [piece for part in row_parts for piece in part]
    model, heads = steps.shape[1], steps.shape[0]
    count = model // width
    turns = inner // state
    offsets = [(k + 1) // 2 * (-1) ** (k % 2) for k in range(per_part)] * len(row_parts)

    def body(index_ref, gain_ref, *refs):
        parts, refs = refs[: len(offsets)], refs[len(offsets) :]
        wide_ref, narrow_ref, steps_ref, out_ref, out_step_ref, square_ref, scaled_ref = refs
        turn = pl.program_id(0)

        @pl.when(turn == 0)
        def _():
            square_ref[...] = jnp.zeros_like(square_ref)
            scaled_ref[...] = jnp.zeros_like(scaled_ref)
            for at, (part, offset) in enumerate(zip(parts, offsets)):
                target = index_ref[0] + offset
                here_rows = pl.ds(starts[at // per_part], part.shape[0])

                @pl.when(jnp.logical_and(target >= 0, target < count))
                def _():
                    scale_in(
                        lambda here: part[:, here].astype(F32),
                        gain_ref, square_ref.at[here_rows], scaled_ref.at[here_rows],
                        target * width, target * width, width,
                    )

            out_ref[...] = dot(scaled_ref[...], narrow_ref[...])
            out_step_ref[...] = dot(scaled_ref[...], steps_ref[...], ((1,), (1,)))

        @pl.when(turn > 0)
        def _():
            out_ref[...] = dot(scaled_ref[...], wide_ref[...])

    shape = jax.ShapeDtypeStruct
    outs = [shape((rows, heads), F32), shape((rows, LANES), F32), shape((rows, model), BF16)]
    return pl.pallas_call(
        body,
        grid=(1 + turns,),
        out_shape=[shape((rows, inner + state), F32)] + outs,
        in_specs=[pl.BlockSpec(memory_space=pltpu.SMEM), once_spec(gain)]
        + [once_spec(piece) for piece in pieces]
        + [
            pl.BlockSpec((model, state), lambda j: (0, turns + jnp.maximum(j, 1) - 1)),
            pl.BlockSpec((model, state), lambda j: (0, 0), pipeline_mode=pl.Buffered(1)),
            once_spec(steps),
        ],
        out_specs=[pl.BlockSpec((rows, state), lambda j: (0, jnp.where(j == 0, turns, j - 1)))]
        + [whole_spec(a) for a in outs],
        compiler_params=granted(60),
        name="begin",
    )(index, gain, *pieces, wide, narrow, steps)


def enter(
    begun, pieces, lead, index, gain, wide, narrow, steps, taps, bias, rate, inner, state, size
):
    sums, step_sums, squares, scaled = begun
    starts = row_starts(pieces[::2])
    total_rows, width = starts[-1], pieces[0].shape[1]
    rows = total_rows - lead
    model, heads = steps.shape[1], steps.shape[0]
    count = model // width
    head_width = inner // heads
    groups = state // size
    turns = inner // state
    turn_heads = heads // turns
    blocks = rows // SPAN

    def body(
        index_ref, gain_ref, *refs,
    ):
        piece_refs, refs = refs[: len(pieces)], refs[len(pieces) :]
        enter_body(index_ref, gain_ref, piece_refs, *refs)

    def enter_body(
        index_ref, gain_ref, piece_refs, old_ref, squares_ref, sums_ref, step_sums_ref,
        wide_ref, narrow_ref, steps_ref, taps_ref, bias_ref, rate_ref,
        scaled_ref, scale_ref, conv_ref, step_ref, cum_ref, update_ref, block_log_ref,
        message_ref, square_ref, piece_ref, raw_ref, padded_ref, maps_ref, factor_ref, log_ref,
    ):
        turn = pl.program_id(0)

        @pl.when(turn == 0)
        def _():
            at_end = jnp.logical_or(index_ref[0] == 0, index_ref[0] == count - 1)
            square_ref[...] = squares_ref[...]
            for k, (behind, ahead) in enumerate(zip(piece_refs[::2], piece_refs[1::2])):
                here_rows = pl.ds(starts[k], behind.shape[0])
                scale_in(
                    lambda here: behind[:, here].astype(F32) + ahead[:, here].astype(F32),
                    gain_ref, square_ref.at[here_rows], piece_ref.at[here_rows], 0, 0, width,
                )

            @pl.when(at_end)
            def _():
                scaled_ref[...] = piece_ref[...]

            @pl.when(jnp.logical_not(at_end))
            def _():
                scaled_ref[...] = old_ref[...]

            moment = jnp.sum(square_ref[...], axis=-1, keepdims=True) * (1.0 / model)
            scale_ref[...] = jnp.broadcast_to(lax.rsqrt(moment + EPSILON), scale_ref.shape)
            raw = sums_ref[...] + dot(piece_ref[...], narrow_ref[...])
            raw_ref[...] = (raw * scale_ref[:, 0:1]).astype(BF16)
            raw_step = step_sums_ref[...] + dot(piece_ref[...], steps_ref[...], ((1,), (1,)))
            raw_step = (raw_step * scale_ref[:, 0:heads]).astype(BF16)
            row = lax.broadcasted_iota(jnp.int32, (SPAN, SPAN), 0)
            col = lax.broadcasted_iota(jnp.int32, (SPAN, SPAN), 1)
            lower = jnp.where(row >= col, 1.0, 0.0).astype(BF16)
            block_log_ref[...] = jnp.zeros_like(block_log_ref)
            total_log = jnp.zeros((1, heads), F32)
            for b in range(blocks):
                here = slice(b * SPAN, (b + 1) * SPAN)
                pre = raw_step[lead + b * SPAN : lead + (b + 1) * SPAN, :].astype(F32)
                pre = pre + bias_ref[...]
                step = jnp.maximum(pre, 0.0) + jnp.log1p(jnp.exp(-jnp.abs(pre)))
                log_decay = -step * jnp.exp(rate_ref[...])
                cum = None
                for part in parts_of(log_decay, 3):
                    term = dot(lower, part)
                    cum = term if cum is None else cum + term
                last = cum[SPAN - 1 : SPAN, :]
                step_ref[here, :] = step
                cum_ref[here, :] = cum
                block_log_ref[b : b + 1, :] = last
                factor_ref[here, :] = step * jnp.exp(last - cum)
                total_log = total_log + last
            log_ref[...] = jnp.broadcast_to(total_log, log_ref.shape)

        @pl.when(turn > 0)
        def _():
            raw = sums_ref[...] + dot(piece_ref[...], wide_ref[...])
            raw_ref[...] = (raw * scale_ref[:, 0:1]).astype(BF16)

        rows_in(padded_ref, raw_ref[...], lead)
        for b in range(blocks):
            conv_ref[b * SPAN : (b + 1) * SPAN, :] = conv_block(
                padded_ref, b * SPAN, taps_ref, slice(0, state)
            )

        @pl.when(turn == 0)
        def _():
            maps_ref[...] = conv_ref[...]

        for k in range(turns):

            @pl.when(turn == 1 + k)
            def _():
                group = k * state * groups // inner
                expand = expander(heads, head_width, k * turn_heads, turn_heads)
                keep = jnp.exp(spread(block_log_ref[...], expand, 3))
                total = None
                for b in range(blocks):
                    here = slice(b * SPAN, (b + 1) * SPAN)
                    factor = spread(factor_ref[here, :], expand)
                    stepped = (conv_ref[here, :].astype(F32) * factor).astype(BF16)
                    maps = maps_ref[here, group * size : (group + 1) * size]
                    update = dot(maps, stepped, ((0,), (0,)))
                    update_ref[b] = update
                    total = update if total is None else keep[b : b + 1, :] * total + update
                message_ref[0:size, :] = total.astype(BF16)
                log = spread(log_ref[...], expand, 3)[0:1, :]
                message_ref[size : size + TAIL, :] = log_rows(log)

    def any_turn(j):
        return jnp.where(j == 0, turns, j - 1)

    def wide_turn(j):
        return jnp.maximum(j, 1) - 1

    def target(i):
        return jnp.where(i[0] == 0, count - 1, 0)

    shape = jax.ShapeDtypeStruct
    once = pl.Buffered(1)
    turned = pl.BlockSpec((total_rows, state), lambda j, i: (0, any_turn(j)))
    placed = pl.BlockSpec((total_rows, width), lambda j, i: (0, target(i)), pipeline_mode=once)
    outs = [
        shape(scaled.shape, BF16),
        shape((total_rows, LANES), F32),
        shape((rows, inner + state), BF16),
        shape((rows, heads), F32),
        shape((rows, heads), F32),
        shape((blocks, size, inner), F32),
        shape((8, heads), F32),
        shape((size + TAIL, inner), BF16),
    ]
    out_specs = [whole_spec(a) for a in outs]
    out_specs[0] = pl.BlockSpec((total_rows, width), lambda j, i: (0, target(i)))
    out_specs[2] = pl.BlockSpec((rows, state), lambda j, i: (0, any_turn(j)))
    out_specs[5] = pl.BlockSpec((blocks, size, state), lambda j, i: (0, 0, wide_turn(j)))
    out_specs[7] = pl.BlockSpec((size + TAIL, state), lambda j, i: (0, wide_turn(j)))
    return pl.pallas_call(
        body,
        out_shape=outs,
        grid_spec=pltpu.PrefetchScalarGridSpec(
            num_scalar_prefetch=1,
            grid=(1 + turns,),
            in_specs=[
                pl.BlockSpec((1, width), lambda j, i: (0, target(i))),
                *[once_spec(piece) for piece in pieces],
                placed,
                once_spec(squares),
                turned,
                once_spec(step_sums),
                pl.BlockSpec((width, state), lambda j, i: (target(i), turns + wide_turn(j))),
                pl.BlockSpec((width, state), lambda j, i: (target(i), 0)),
                pl.BlockSpec((heads, width), lambda j, i: (0, target(i))),
                pl.BlockSpec((taps.shape[0], state), lambda j, i: (0, any_turn(j))),
                once_spec(bias),
                once_spec(rate),
            ],
            out_specs=out_specs,
            scratch_shapes=[
                pltpu.VMEM((total_rows, LANES), F32),
                pltpu.VMEM((total_rows, width), BF16),
                pltpu.VMEM((total_rows, state), BF16),
                pltpu.VMEM((rows + 8, state), F32),
                pltpu.VMEM((rows, state), BF16),
                pltpu.VMEM((rows, heads), F32),
                pltpu.VMEM((8, heads), F32),
            ],
        ),
        input_output_aliases={2 + len(pieces): 0},
        compiler_params=granted(60),
        name="enter",
    )(
        index, gain, *pieces, scaled, squares, sums, step_sums, wide, narrow, steps, taps, bias,
        rate,
    )


def inside(
    half, scaled, scale, lead, wide, narrow, taps, skip, conv, step, cum, scores, inner, state,
    size,
):
    total_rows, model = scaled.shape
    rows = total_rows - lead
    heads = step.shape[1]
    width = inner // heads
    groups = state // size
    turns = inner // state // 2
    turn_heads = heads // turns // 2
    blocks = rows // SPAN
    lone = 1 if scores is None else 0

    def body(scaled_ref, scale_ref, wide_ref, skip_ref, conv_ref, x_ref, step_ref, cum_ref, *refs):
        if lone:
            narrow_ref, taps_ref, out_ref, gate_ref, scores_ref, maps_ref, rows_ref, padded_ref = refs
        else:
            scores_ref, out_ref, gate_ref, rows_ref = refs
        turn = pl.program_id(0)

        @pl.when(turn == 0)
        def _():
            if lone:
                raw = (dot(scaled_ref[...], narrow_ref[...]) * scale_ref[:, 0:1]).astype(BF16)
                rows_in(padded_ref, raw, lead)
            for b in range(blocks):
                here = slice(b * SPAN, (b + 1) * SPAN)
                padding = jnp.zeros((SPAN, SPAN - heads), F32)
                rows_ref[b] = jnp.concatenate([cum_ref[here, :], padding], axis=1).T
                if not lone:
                    continue
                maps_ref[here, :] = conv_block(padded_ref, b * SPAN, taps_ref, slice(0, state))
                for g in range(groups):
                    cols = slice(g * size, (g + 1) * size)
                    scores_ref[b, g] = dot(maps_ref[here, cols], conv_ref[here, cols], ((1,), (1,)))

        row = lax.broadcasted_iota(jnp.int32, (SPAN, SPAN), 0)
        col = lax.broadcasted_iota(jnp.int32, (SPAN, SPAN), 1)
        causal = row >= col
        lane = lax.broadcasted_iota(jnp.int32, (SPAN, 2 * width), 1)
        for k in range(turns):

            @pl.when(turn == lone + k)
            def _():
                raw = dot(scaled_ref[lead:, :], wide_ref[...]) * scale_ref[lead:, 0:1]
                gate_ref[...] = raw.astype(BF16)
                first = (half * turns + k) * turn_heads
                expand = expander(heads, width, first, turn_heads)
                skips = spread(jnp.broadcast_to(skip_ref[...], (8, heads)), expand, 3)[0:1, :]
                for b in range(blocks):
                    here = slice(b * SPAN, (b + 1) * SPAN)
                    steps = spread(step_ref[here, :], expand)
                    cum = cum_ref[here, :]
                    for pair in range(turn_heads // 2):
                        head = first + 2 * pair
                        scores_here = scores_ref[b, head * groups // heads]
                        cols = slice(2 * pair * width, (2 * pair + 2) * width)
                        x = x_ref[here, cols].astype(F32)
                        stepped = x * steps[:, cols]
                        weighted = []
                        for h in (head, head + 1):
                            gap = cum[:, h : h + 1] - rows_ref[b, h : h + 1, :]
                            decay = jnp.exp(jnp.where(causal, gap, -1e30))
                            weighted.append((scores_here * decay).astype(BF16))
                        stacked = jnp.concatenate(
                            [
                                jnp.where(lane < width, stepped, 0.0).astype(BF16),
                                jnp.where(lane < width, 0.0, stepped).astype(BF16),
                            ],
                            axis=0,
                        )
                        out = dot(jnp.concatenate(weighted, axis=1), stacked)
                        out_ref[here, cols] = out + skips[:, cols] * x

    def own_turn(j):
        return jnp.maximum(j - lone, 0)

    def wide_turn(j):
        return half * turns + own_turn(j)

    shape = jax.ShapeDtypeStruct
    score_shape = shape((blocks, groups, SPAN, SPAN), F32)
    maps_shape = shape((rows, state), BF16)
    outs = [shape((rows, inner // 2), F32), shape((rows, inner // 2), BF16)]
    turned = pl.BlockSpec((rows, state), lambda j: (0, own_turn(j)))
    scratch = [pltpu.VMEM((blocks, SPAN, SPAN), F32)]
    if lone:
        outs += [score_shape, maps_shape]
        more = (narrow, taps)
        more_specs = [
            pl.BlockSpec((model, state), lambda j: (0, 1), pipeline_mode=pl.Buffered(1)),
            once_spec(taps),
        ]
        scratch.append(pltpu.VMEM((rows + 8, state), F32))
    else:
        more, more_specs = (scores,), [once_spec(scores)]
    maps_at = inner // state
    return pl.pallas_call(
        body,
        grid=(lone + turns,),
        out_shape=outs,
        in_specs=[
            once_spec(scaled),
            once_spec(scale),
            pl.BlockSpec((model, state), lambda j: (0, wide_turn(j))),
            once_spec(skip),
            pl.BlockSpec((rows, state), lambda j: (0, maps_at), pipeline_mode=pl.Buffered(1)),
            pl.BlockSpec((rows, state), lambda j: (0, wide_turn(j))),
            once_spec(step),
            once_spec(cum),
        ]
        + more_specs,
        out_specs=[turned, turned] + [whole_spec(a) for a in outs[2:]],
        scratch_shapes=scratch,
        compiler_params=granted(60),
        name="inside",
    )(scaled, scale, wide, skip, conv, conv, step, cum, *more)


def log_rows(log):
    row = lax.broadcasted_iota(jnp.int32, (TAIL, log.shape[1]), 0)
    block = jnp.zeros((TAIL, log.shape[1]), F32)
    for k, part in enumerate(parts_of(log, 3)):
        block = jnp.where(row == k, part.astype(F32), block)
    return block.astype(BF16)


def log_of(message_ref, size):
    rows = message_ref[size : size + TAIL, :].astype(F32)
    return rows[0:1, :] + rows[1:2, :] + rows[2:3, :]


def combine_body(size, first):
    def body(later_ref, mine_ref, came_ref, *refs):
        if first:
            out_ref, before_ref, before_log_ref = refs
        else:
            prior_ref, prior_log_ref, out_ref, before_ref, before_log_ref = refs
        mine = mine_ref[0:size, :].astype(F32)
        came = came_ref[0:size, :].astype(F32)
        my_log, came_log = log_of(mine_ref, size), log_of(came_ref, size)

        @pl.when(later_ref[0] == 1)
        def _():
            out_ref[0:size, :] = (jnp.exp(my_log) * came + mine).astype(BF16)
            if first:
                before_ref[...] = came
                before_log_ref[0:1, :] = came_log
            else:
                before_ref[...] = jnp.exp(prior_log_ref[0:1, :]) * came + prior_ref[...]
                before_log_ref[0:1, :] = prior_log_ref[0:1, :] + came_log

        @pl.when(later_ref[0] == 0)
        def _():
            out_ref[0:size, :] = (jnp.exp(came_log) * mine + came).astype(BF16)
            if first:
                before_ref[...] = jnp.zeros_like(before_ref)
                before_log_ref[0:1, :] = jnp.zeros_like(came_log)
            else:
                before_ref[...] = prior_ref[...]
                before_log_ref[0:1, :] = prior_log_ref[0:1, :]

        out_ref[size : size + TAIL, :] = log_rows(my_log + came_log)

    return body


def finish(
    part, parts, index, later, entering, update, block_log, cum, maps, halves, gain, out_weight,
    inner, state, heads, groups, count,
):
    size = state // groups
    width = inner // heads
    rows = cum.shape[0] // parts
    last_part = part == parts - 1
    blocks = rows // SPAN
    model = out_weight.shape[1]
    turn_width = model // count
    first = len(entering) > 1

    def body(index_ref, later_ref, *refs):
        entering_refs, refs = refs[: len(entering)], refs[len(entering) :]
        update_ref, block_log_ref, cum_ref, maps_ref, *refs = refs
        half_refs, refs = (refs[0:2], refs[2:4]), refs[4:]
        gain_ref, weight_ref, out_ref, top_ref, bottom_ref, *memory_out, mixed_ref = refs

        def both(k, here, cols):
            split = inner // 2
            pieces = []
            for h in range(2):
                low, high = max(cols.start, h * split), min(cols.stop, (h + 1) * split)
                if low < high:
                    pieces.append(half_refs[h][k][here, low - h * split : high - h * split])
            return pieces[0] if len(pieces) == 1 else jnp.concatenate(pieces, axis=1)

        @pl.when(pl.program_id(0) == 0)
        def _():
            expand = expander(heads, width)
            if first:
                came_ref, before_ref, before_log_ref, start_ref = entering_refs
                is_later = later_ref[0] == 1
                prior_log = before_log_ref[0:1, :]
                prior = before_ref[...]
                came = came_ref[0:size, :].astype(F32)
                came_log = log_of(came_ref, size)
                memory = jnp.where(is_later, jnp.exp(prior_log) * came + prior, prior)
                memory_log = jnp.where(is_later, prior_log + came_log, prior_log)
                memory = jnp.exp(memory_log) * start_ref[...] + memory
            else:
                memory = entering_refs[0][...]
            keep = jnp.exp(spread(block_log_ref[...], expand, 3))
            for b in range(blocks):
                here = slice(b * SPAN, (b + 1) * SPAN)
                reach = spread(jnp.exp(cum_ref[here, :]), expand)
                for g in range(groups):
                    cols = slice(g * inner // groups, (g + 1) * inner // groups)
                    carried = dot(
                        maps_ref[here, g * size : (g + 1) * size], memory[:, cols].astype(BF16)
                    )
                    scan = both(0, here, cols) + reach[:, cols] * carried
                    gate = both(1, here, cols)
                    gated = scan * silu(gate.astype(F32))
                    moment = jnp.mean(gated * gated, axis=-1, keepdims=True)
                    mixed_ref[here, cols] = (
                        gated * lax.rsqrt(moment + EPSILON) * gain_ref[:, cols].astype(F32)
                    ).astype(BF16)
                if not last_part or b < blocks - 1:
                    at = part * blocks + b
                    memory = keep[at : at + 1, :] * memory + update_ref[b]
            if memory_out:
                memory_out[0][...] = memory

        sent = dot(mixed_ref[...], weight_ref[...]).astype(BF16)
        out_ref[...] = sent
        target = farthest(pl.program_id(0), index_ref)

        @pl.when(target == count - 1)
        def _():
            top_ref[...] = sent

        @pl.when(target == 0)
        def _():
            bottom_ref[...] = sent

    def rows_of(array):
        once = pl.Buffered(1)
        return pl.BlockSpec((rows, array.shape[1]), lambda *_: (part, 0), pipeline_mode=once)

    def farthest(j, index_ref):
        index = index_ref[0]
        low, high = jnp.int32(0), jnp.int32(count - 1)
        chosen = low
        for k in range(count):
            up = high - index >= index - low
            pick = jnp.where(up, high, low)
            chosen = jnp.where(j == k, pick, chosen)
            high = jnp.where(up, high - 1, high)
            low = jnp.where(up, low, low + 1)
        return chosen

    shape = jax.ShapeDtypeStruct
    extra = [shape((rows, turn_width), BF16)] * 2
    extra += [] if last_part else [shape((size, inner), F32)]

    return pl.pallas_call(
        body,
        out_shape=[shape((rows, model), BF16)] + extra,
        grid_spec=pltpu.PrefetchScalarGridSpec(
            num_scalar_prefetch=2,
            grid=(count,),
            in_specs=[once_spec(a) for a in entering]
            + [
                pl.BlockSpec((blocks, size, inner), lambda *_: (part, 0, 0)),
                once_spec(block_log),
                rows_of(cum),
                rows_of(maps),
            ]
            + [rows_of(a) for half in halves for a in half]
            + [
                once_spec(gain),
                pl.BlockSpec((inner, turn_width), lambda j, i, _: (0, farthest(j, i))),
            ],
            out_specs=[pl.BlockSpec((rows, turn_width), lambda j, i, _: (0, farthest(j, i)))]
            + [whole_spec(a) for a in extra],
            scratch_shapes=[pltpu.VMEM((rows, inner), BF16)],
        ),
        compiler_params=granted(60),
        name="finish",
    )(
        index, later, *entering, update, block_log, cum, maps, *halves[0], *halves[1], gain,
        out_weight,
    )


def relay(index, distance, partial, received, count):
    rows, model = partial.shape
    width = model // count

    def body(index_ref, ahead_ref, behind_ref, *refs):
        for own, came, out in zip((ahead_ref, behind_ref), refs[:-2], refs[-2:]):
            out[...] = (own[...].astype(F32) + came[...].astype(F32)).astype(BF16)

    def place(sign):
        return lambda j, i: (j, jnp.clip(i[0] + sign * distance, 0, count - 1))

    turns = 4
    whole = pl.BlockSpec((rows // turns, width), lambda j, i: (j, 0))
    shape = jax.ShapeDtypeStruct((rows, width), BF16)
    return pl.pallas_call(
        body,
        out_shape=[shape, shape],
        grid_spec=pltpu.PrefetchScalarGridSpec(
            num_scalar_prefetch=1,
            grid=(turns,),
            in_specs=[
                pl.BlockSpec((rows // turns, width), place(1)),
                pl.BlockSpec((rows // turns, width), place(-1)),
                whole,
                whole,
            ],
            out_specs=[whole, whole],
        ),
        compiler_params=granted(8),
        name="relay",
    )(index, partial, partial, *received)


def send_on(ahead, behind, distance, axis):
    count = lax.axis_size(axis)
    return (
        lax.ppermute(ahead, axis, [(i, i + 1) for i in range(count - distance)]),
        lax.ppermute(behind, axis, [(i, i - 1) for i in range(distance, count)]),
    )


def total(index, partial, received, hidden, row_block, count, filled):
    rows, model = partial.shape
    width = model // count
    turns = 4

    def body(index_ref, own_ref, ahead_ref, behind_ref, hidden_ref, *refs):
        summed = own_ref[...].astype(F32) + ahead_ref[...].astype(F32)
        summed = summed + behind_ref[...].astype(F32)
        refs[-1][...] = (summed + hidden_ref[...].astype(F32)).astype(BF16)

    block = (rows // turns, width)
    whole = pl.BlockSpec(block, lambda j, i: (j, 0))
    placed = pl.BlockSpec(block, lambda j, i: (row_block * turns + j, 0))
    return pl.pallas_call(
        body,
        out_shape=jax.ShapeDtypeStruct(hidden.shape, BF16),
        grid_spec=pltpu.PrefetchScalarGridSpec(
            num_scalar_prefetch=1,
            grid=(turns,),
            in_specs=[pl.BlockSpec(block, lambda j, i: (j, i[0])), whole, whole, placed]
            + [pl.BlockSpec(memory_space=pl.ANY)] * len(filled),
            out_specs=placed,
        ),
        input_output_aliases={5: 0} if filled else {},
        compiler_params=granted(8),
        name="total",
    )(index, partial, *received, hidden, *filled)


def on_device(
    hidden, norm_gain, gate_x_weight, state_weight, step_weight, conv_inner, conv_state,
    step_bias, decay_log, skip_gain, inner_gain, out_weight, initial_state,
):
    rows = hidden.shape[0]
    half = rows // 2
    inner = gate_x_weight.shape[2]
    state = state_weight.shape[2]
    heads = step_weight.shape[1]
    size = initial_state.shape[2]
    groups = state // size
    blocks = rows // SPAN
    feature_index = lax.axis_index("tp").reshape(1)
    range_index = lax.axis_index("seq")
    ranges = lax.axis_size("seq")

    model = step_weight.shape[0]
    parts_count = lax.axis_size("tp")
    narrow_weight = state_weight.reshape(model, 2 * state)
    step_rows = step_weight.T
    taps = jnp.concatenate([conv_inner, conv_state[:, 0]], axis=1)
    out_taps = conv_state[:, 1]
    start_state = initial_state.transpose(2, 0, 1).reshape(size, inner)
    gain = norm_gain.astype(F32)[None, :]
    out_gain = inner_gain[None, :]
    bias, rate, skip = step_bias[None, :], decay_log[None, :], skip_gain[None, :]

    halo = shifted(hidden[rows - TAIL :], "seq", 1)
    early = line_step([jnp.concatenate([halo, hidden[:half]], axis=0)] * 2, 1, "tp")[1:]
    late = line_step([hidden[half:]] * 2, 1, "tp")[1:]
    small = (narrow_weight, step_rows, taps, start_state, gain, out_gain)
    late[1:], small = lax.optimization_barrier((late[1:], small))
    narrow_weight, step_rows, taps, start_state, gain, out_gain = small
    wide = gate_x_weight.reshape(model, 2 * inner)
    for step in range(2, parts_count):
        early, late = line_step(early, step, "tp"), line_step(late, step, "tp")
        if step == 2:
            early[1:], late[1:], wide = lax.optimization_barrier((early[1:], late[1:], wide))

    shape = jax.ShapeDtypeStruct
    weights = (feature_index, gain, wide, narrow_weight, step_rows)
    begun = begin((early[:-2], late[:-2]), *weights, inner, state)
    last, begun = lax.optimization_barrier((early[-2:] + late[-2:], begun))
    scaled, scale, conv, step, cum, update, block_log, message = enter(
        begun, last, TAIL, *weights, taps, bias, rate, inner, state, size
    )

    def within(half, scores):
        return inside(
            half, scaled, scale, TAIL, wide, narrow_weight, out_taps, skip, conv, step, cum, scores,
            inner, state, size,
        )

    *first_half, scores, maps = within(0, None)
    second_half = within(1, scores)
    before = ()
    bit = 1
    while True:
        came = swapped(message, "seq", bit)
        if bit == 2:
            held = lax.optimization_barrier((came, first_half, scores, maps))
            came, first_half, scores, maps = held
            second_half = within(1, scores)
        later = ((range_index // bit) % 2).astype(jnp.int32).reshape(1)
        bit *= 2
        if bit == ranges:
            break
        message, *before = call(
            combine_body(size, not before),
            [
                shape((size + TAIL, inner), BF16),
                shape((size, inner), F32),
                shape((8, inner), F32),
            ],
            later,
            message,
            came,
            *before,
            scalars=1,
            name="combine",
            limit=14,
        )
    entering = (came, *before, start_state)
    partials, received = [], []
    halves = (first_half, second_half)
    for part in range(2):
        partial, top, bottom, *entering = finish(
            part, 2, feature_index, later, entering, update, block_log, cum, maps, halves,
            out_gain, out_weight, inner, state, heads, groups, parts_count,
        )
        partials.append(partial)
        received.append(send_on(top, bottom, parts_count - 1, "tp"))
    for distance in range(parts_count - 2, 0, -1):
        for k, partial in enumerate(partials):
            onward = relay(feature_index, distance, partial, received[k], parts_count)
            received[k] = send_on(*onward, distance, "tp")
    filled = ()
    for k, partial in enumerate(partials):
        filled = (
            total(feature_index, partial, received[k], hidden, k, parts_count, filled),
        )
    return filled[0]


def solution(mesh):
    return jax.shard_map(
        on_device,
        mesh=mesh,
        in_specs=(
            P("seq", "tp"),
            P(),
            P(None, None, "tp"),
            P(None, None, "tp"),
            P(None, "tp"),
            P(None, "tp"),
            P(None, None, "tp"),
            P("tp"),
            P("tp"),
            P("tp"),
            P("tp"),
            P("tp", None),
            P("tp", None, None),
        ),
        out_specs=P("seq", "tp"),
        check_vma=False,
    )
```

```python
import jax
import jax.numpy as jnp
from jax import lax
from jax.experimental import pallas as pl
from jax.experimental.pallas import tpu as pltpu
from jax.sharding import PartitionSpec as P

SPAN = 128
EPSILON = 1e-05
TAIL = 16
LANES = 128
F32 = jnp.float32
BF16 = jnp.bfloat16


def shifted(block, axis, distance):
    count = lax.axis_size(axis)
    route = [(i, i + distance) for i in range(count) if 0 <= i + distance < count]
    return lax.ppermute(block, axis, route)


def swapped(block, axis, bit):
    return lax.ppermute(block, axis, [(i, i ^ bit) for i in range(lax.axis_size(axis))])


def line_step(pieces, step, axis):
    count = lax.axis_size(axis)
    behind, ahead = pieces[-2], pieces[-1]
    behind = lax.ppermute(behind, axis, [(i, i + 1) for i in range(step - 1, count - 1)])
    ahead = lax.ppermute(ahead, axis, [(i, i - 1) for i in range(1, count - step + 1)])
    return pieces + [behind, ahead]


def whole_spec(array):
    rank = len(array.shape)
    return pl.BlockSpec(array.shape, lambda *_: (0,) * rank)


def once_spec(array):
    rank = len(array.shape)
    once = pl.Buffered(1)
    return pl.BlockSpec(array.shape, lambda *_: (0,) * rank, pipeline_mode=once)


def call(body, outs, *arrays, scratch=(), scalars=0, name=None, limit=60):
    pairs = [a if isinstance(a, tuple) else (a, whole_spec(a)) for a in arrays[scalars:]]
    return pl.pallas_call(
        body,
        out_shape=outs,
        grid=(1,),
        in_specs=[pl.BlockSpec(memory_space=pltpu.SMEM)] * scalars + [spec for _, spec in pairs],
        out_specs=jax.tree.map(whole_spec, outs),
        scratch_shapes=list(scratch),
        compiler_params=granted(limit),
        name=name,
    )(*arrays[:scalars], *[a for a, _ in pairs])


def granted(mebibytes):
    return pltpu.CompilerParams(vmem_limit_bytes=mebibytes * 2**20)


def dot(a, b, contract=((1,), (0,))):
    return lax.dot_general(a, b, (contract, ((), ())), preferred_element_type=F32)


def parts_of(x, count):
    parts = []
    for _ in range(count):
        part = x.astype(BF16)
        parts.append(part)
        x = x - part.astype(F32)
    return parts


def spread(x, expand, count=2):
    parts = [part.astype(F32) for part in parts_of(x, count)]
    return dot(
        jnp.concatenate(parts, axis=1).astype(BF16), jnp.concatenate([expand] * count, axis=0)
    )


def expander(heads, width, first=0, count=None):
    lanes = (count or heads) * width
    head = lax.broadcasted_iota(jnp.int32, (heads, lanes), 0) - first
    lane = lax.broadcasted_iota(jnp.int32, (heads, lanes), 1)
    inside = jnp.logical_and(lane >= head * width, lane < (head + 1) * width)
    return jnp.where(inside, 1.0, 0.0).astype(BF16)


def silu(v):
    return v * (1.0 / (1.0 + jnp.exp(-v)))


def conv_block(padded_ref, start, taps_ref, columns):
    summed = None
    for k in range(taps_ref.shape[0]):
        row = 8 + start - (taps_ref.shape[0] - 1) + k
        term = taps_ref[k : k + 1, columns].astype(F32) * padded_ref[row : row + SPAN, columns]
        summed = term if summed is None else summed + term
    return silu(summed).astype(BF16)


def rows_in(ref, raw, lead):
    ref[0:8, :] = raw[lead - 8 : lead, :].astype(F32)
    ref[8:, :] = raw[lead:, :].astype(F32)


def scale_in(piece, gain_ref, square_ref, scaled_ref, gain_start, start, width):
    def columns(k, carry):
        here = pl.ds(pl.multiple_of(k * LANES, LANES), LANES)
        there = pl.ds(pl.multiple_of(start + k * LANES, LANES), LANES)
        gain = gain_ref[:, pl.ds(pl.multiple_of(gain_start + k * LANES, LANES), LANES)]
        value = piece(here)
        square_ref[...] += value * value
        scaled_ref[:, there] = (value * gain).astype(BF16)
        return carry

    lax.fori_loop(0, width // LANES, columns, 0)


def row_starts(pieces):
    starts = [0]
    for piece in pieces:
        starts.append(starts[-1] + piece.shape[0])
    return starts


def begin(row_parts, index, gain, wide, narrow, steps, inner, state):
    starts = row_starts([part[0] for part in row_parts])
    rows, width = starts[-1], row_parts[0][0].shape[1]
    per_part = len(row_parts[0])
    pieces = [piece for part in row_parts for piece in part]
    model, heads = steps.shape[1], steps.shape[0]
    count = model // width
    turns = inner // state
    offsets = [(k + 1) // 2 * (-1) ** (k % 2) for k in range(per_part)] * len(row_parts)

    def body(index_ref, gain_ref, *refs):
        parts, refs = refs[: len(offsets)], refs[len(offsets) :]
        wide_ref, narrow_ref, steps_ref, out_ref, out_step_ref, square_ref, scaled_ref = refs
        turn = pl.program_id(0)

        @pl.when(turn == 0)
        def _():
            square_ref[...] = jnp.zeros_like(square_ref)
            scaled_ref[...] = jnp.zeros_like(scaled_ref)
            for at, (part, offset) in enumerate(zip(parts, offsets)):
                target = index_ref[0] + offset
                here_rows = pl.ds(starts[at // per_part], part.shape[0])

                @pl.when(jnp.logical_and(target >= 0, target < count))
                def _():
                    scale_in(
                        lambda here: part[:, here].astype(F32),
                        gain_ref, square_ref.at[here_rows], scaled_ref.at[here_rows],
                        target * width, target * width, width,
                    )

            out_ref[...] = dot(scaled_ref[...], narrow_ref[...])
            out_step_ref[...] = dot(scaled_ref[...], steps_ref[...], ((1,), (1,)))

        @pl.when(turn > 0)
        def _():
            out_ref[...] = dot(scaled_ref[...], wide_ref[...])

    shape = jax.ShapeDtypeStruct
    outs = [shape((rows, heads), F32), shape((rows, LANES), F32), shape((rows, model), BF16)]
    return pl.pallas_call(
        body,
        grid=(1 + turns,),
        out_shape=[shape((rows, inner + state), F32)] + outs,
        in_specs=[pl.BlockSpec(memory_space=pltpu.SMEM), once_spec(gain)]
        + [once_spec(piece) for piece in pieces]
        + [
            pl.BlockSpec((model, state), lambda j: (0, turns + jnp.maximum(j, 1) - 1)),
            pl.BlockSpec((model, state), lambda j: (0, 0), pipeline_mode=pl.Buffered(1)),
            once_spec(steps),
        ],
        out_specs=[pl.BlockSpec((rows, state), lambda j: (0, jnp.where(j == 0, turns, j - 1)))]
        + [whole_spec(a) for a in outs],
        compiler_params=granted(60),
        name="begin",
    )(index, gain, *pieces, wide, narrow, steps)


def enter(
    begun, pieces, lead, index, gain, wide, narrow, steps, taps, bias, rate, inner, state, size
):
    sums, step_sums, squares, scaled = begun
    starts = row_starts(pieces[::2])
    total_rows, width = starts[-1], pieces[0].shape[1]
    rows = total_rows - lead
    model, heads = steps.shape[1], steps.shape[0]
    count = model // width
    head_width = inner // heads
    groups = state // size
    turns = inner // state
    turn_heads = heads // turns
    blocks = rows // SPAN

    def body(
        index_ref, gain_ref, *refs,
    ):
        piece_refs, refs = refs[: len(pieces)], refs[len(pieces) :]
        enter_body(index_ref, gain_ref, piece_refs, *refs)

    def enter_body(
        index_ref, gain_ref, piece_refs, old_ref, squares_ref, sums_ref, step_sums_ref,
        wide_ref, narrow_ref, steps_ref, taps_ref, bias_ref, rate_ref,
        scaled_ref, scale_ref, conv_ref, step_ref, cum_ref, update_ref, block_log_ref,
        message_ref, square_ref, piece_ref, raw_ref, padded_ref, maps_ref, factor_ref, log_ref,
    ):
        turn = pl.program_id(0)

        @pl.when(turn == 0)
        def _():
            at_end = jnp.logical_or(index_ref[0] == 0, index_ref[0] == count - 1)
            square_ref[...] = squares_ref[...]
            for k, (behind, ahead) in enumerate(zip(piece_refs[::2], piece_refs[1::2])):
                here_rows = pl.ds(starts[k], behind.shape[0])
                scale_in(
                    lambda here: behind[:, here].astype(F32) + ahead[:, here].astype(F32),
                    gain_ref, square_ref.at[here_rows], piece_ref.at[here_rows], 0, 0, width,
                )

            @pl.when(at_end)
            def _():
                scaled_ref[...] = piece_ref[...]

            @pl.when(jnp.logical_not(at_end))
            def _():
                scaled_ref[...] = old_ref[...]

            moment = jnp.sum(square_ref[...], axis=-1, keepdims=True) * (1.0 / model)
            scale_ref[...] = jnp.broadcast_to(lax.rsqrt(moment + EPSILON), scale_ref.shape)
            raw = sums_ref[...] + dot(piece_ref[...], narrow_ref[...])
            raw_ref[...] = (raw * scale_ref[:, 0:1]).astype(BF16)
            raw_step = step_sums_ref[...] + dot(piece_ref[...], steps_ref[...], ((1,), (1,)))
            raw_step = (raw_step * scale_ref[:, 0:heads]).astype(BF16)
            row = lax.broadcasted_iota(jnp.int32, (SPAN, SPAN), 0)
            col = lax.broadcasted_iota(jnp.int32, (SPAN, SPAN), 1)
            lower = jnp.where(row >= col, 1.0, 0.0).astype(BF16)
            block_log_ref[...] = jnp.zeros_like(block_log_ref)
            total_log = jnp.zeros((1, heads), F32)
            for b in range(blocks):
                here = slice(b * SPAN, (b + 1) * SPAN)
                pre = raw_step[lead + b * SPAN : lead + (b + 1) * SPAN, :].astype(F32)
                pre = pre + bias_ref[...]
                step = jnp.maximum(pre, 0.0) + jnp.log1p(jnp.exp(-jnp.abs(pre)))
                log_decay = -step * jnp.exp(rate_ref[...])
                cum = None
                for part in parts_of(log_decay, 3):
                    term = dot(lower, part)
                    cum = term if cum is None else cum + term
                last = cum[SPAN - 1 : SPAN, :]
                step_ref[here, :] = step
                cum_ref[here, :] = cum
                block_log_ref[b : b + 1, :] = last
                factor_ref[here, :] = step * jnp.exp(last - cum)
                total_log = total_log + last
            log_ref[...] = jnp.broadcast_to(total_log, log_ref.shape)

        @pl.when(turn > 0)
        def _():
            raw = sums_ref[...] + dot(piece_ref[...], wide_ref[...])
            raw_ref[...] = (raw * scale_ref[:, 0:1]).astype(BF16)

        rows_in(padded_ref, raw_ref[...], lead)
        for b in range(blocks):
            conv_ref[b * SPAN : (b + 1) * SPAN, :] = conv_block(
                padded_ref, b * SPAN, taps_ref, slice(0, state)
            )

        @pl.when(turn == 0)
        def _():
            maps_ref[...] = conv_ref[...]

        for k in range(turns):

            @pl.when(turn == 1 + k)
            def _():
                group = k * state * groups // inner
                expand = expander(heads, head_width, k * turn_heads, turn_heads)
                keep = jnp.exp(spread(block_log_ref[...], expand, 3))
                total = None
                for b in range(blocks):
                    here = slice(b * SPAN, (b + 1) * SPAN)
                    factor = spread(factor_ref[here, :], expand)
                    stepped = (conv_ref[here, :].astype(F32) * factor).astype(BF16)
                    maps = maps_ref[here, group * size : (group + 1) * size]
                    update = dot(maps, stepped, ((0,), (0,)))
                    update_ref[b] = update
                    total = update if total is None else keep[b : b + 1, :] * total + update
                message_ref[0:size, :] = total.astype(BF16)
                log = spread(log_ref[...], expand, 3)[0:1, :]
                message_ref[size : size + TAIL, :] = log_rows(log)

    def any_turn(j):
        return jnp.where(j == 0, turns, j - 1)

    def wide_turn(j):
        return jnp.maximum(j, 1) - 1

    def target(i):
        return jnp.where(i[0] == 0, count - 1, 0)

    shape = jax.ShapeDtypeStruct
    once = pl.Buffered(1)
    turned = pl.BlockSpec((total_rows, state), lambda j, i: (0, any_turn(j)))
    placed = pl.BlockSpec((total_rows, width), lambda j, i: (0, target(i)), pipeline_mode=once)
    outs = [
        shape(scaled.shape, BF16),
        shape((total_rows, LANES), F32),
        shape((rows, inner + state), BF16),
        shape((rows, heads), F32),
        shape((rows, heads), F32),
        shape((blocks, size, inner), F32),
        shape((8, heads), F32),
        shape((size + TAIL, inner), BF16),
    ]
    out_specs = [whole_spec(a) for a in outs]
    out_specs[0] = pl.BlockSpec((total_rows, width), lambda j, i: (0, target(i)))
    out_specs[2] = pl.BlockSpec((rows, state), lambda j, i: (0, any_turn(j)))
    out_specs[5] = pl.BlockSpec((blocks, size, state), lambda j, i: (0, 0, wide_turn(j)))
    out_specs[7] = pl.BlockSpec((size + TAIL, state), lambda j, i: (0, wide_turn(j)))
    return pl.pallas_call(
        body,
        out_shape=outs,
        grid_spec=pltpu.PrefetchScalarGridSpec(
            num_scalar_prefetch=1,
            grid=(1 + turns,),
            in_specs=[
                pl.BlockSpec((1, width), lambda j, i: (0, target(i))),
                *[once_spec(piece) for piece in pieces],
                placed,
                once_spec(squares),
                turned,
                once_spec(step_sums),
                pl.BlockSpec((width, state), lambda j, i: (target(i), turns + wide_turn(j))),
                pl.BlockSpec((width, state), lambda j, i: (target(i), 0)),
                pl.BlockSpec((heads, width), lambda j, i: (0, target(i))),
                pl.BlockSpec((taps.shape[0], state), lambda j, i: (0, any_turn(j))),
                once_spec(bias),
                once_spec(rate),
            ],
            out_specs=out_specs,
            scratch_shapes=[
                pltpu.VMEM((total_rows, LANES), F32),
                pltpu.VMEM((total_rows, width), BF16),
                pltpu.VMEM((total_rows, state), BF16),
                pltpu.VMEM((rows + 8, state), F32),
                pltpu.VMEM((rows, state), BF16),
                pltpu.VMEM((rows, heads), F32),
                pltpu.VMEM((8, heads), F32),
            ],
        ),
        input_output_aliases={2 + len(pieces): 0},
        compiler_params=granted(60),
        name="enter",
    )(
        index, gain, *pieces, scaled, squares, sums, step_sums, wide, narrow, steps, taps, bias,
        rate,
    )


def inside(
    half, scaled, scale, lead, wide, narrow, taps, skip, conv, step, cum, scores, inner, state,
    size,
):
    total_rows, model = scaled.shape
    rows = total_rows - lead
    heads = step.shape[1]
    width = inner // heads
    groups = state // size
    turns = inner // state // 2
    turn_heads = heads // turns // 2
    blocks = rows // SPAN
    lone = 1 if scores is None else 0

    def body(scaled_ref, scale_ref, wide_ref, skip_ref, conv_ref, x_ref, step_ref, cum_ref, *refs):
        if lone:
            narrow_ref, taps_ref, out_ref, gate_ref, scores_ref, maps_ref, rows_ref, padded_ref = refs
        else:
            scores_ref, out_ref, gate_ref, rows_ref = refs
        turn = pl.program_id(0)

        @pl.when(turn == 0)
        def _():
            if lone:
                raw = (dot(scaled_ref[...], narrow_ref[...]) * scale_ref[:, 0:1]).astype(BF16)
                rows_in(padded_ref, raw, lead)
            for b in range(blocks):
                here = slice(b * SPAN, (b + 1) * SPAN)
                padding = jnp.zeros((SPAN, SPAN - heads), F32)
                rows_ref[b] = jnp.concatenate([cum_ref[here, :], padding], axis=1).T
                if not lone:
                    continue
                maps_ref[here, :] = conv_block(padded_ref, b * SPAN, taps_ref, slice(0, state))
                for g in range(groups):
                    cols = slice(g * size, (g + 1) * size)
                    scores_ref[b, g] = dot(maps_ref[here, cols], conv_ref[here, cols], ((1,), (1,)))

        row = lax.broadcasted_iota(jnp.int32, (SPAN, SPAN), 0)
        col = lax.broadcasted_iota(jnp.int32, (SPAN, SPAN), 1)
        causal = row >= col
        lane = lax.broadcasted_iota(jnp.int32, (SPAN, 2 * width), 1)
        for k in range(turns):

            @pl.when(turn == lone + k)
            def _():
                raw = dot(scaled_ref[lead:, :], wide_ref[...]) * scale_ref[lead:, 0:1]
                gate_ref[...] = raw.astype(BF16)
                first = (half * turns + k) * turn_heads
                expand = expander(heads, width, first, turn_heads)
                skips = spread(jnp.broadcast_to(skip_ref[...], (8, heads)), expand, 3)[0:1, :]
                for b in range(blocks):
                    here = slice(b * SPAN, (b + 1) * SPAN)
                    steps = spread(step_ref[here, :], expand)
                    cum = cum_ref[here, :]
                    for pair in range(turn_heads // 2):
                        head = first + 2 * pair
                        scores_here = scores_ref[b, head * groups // heads]
                        cols = slice(2 * pair * width, (2 * pair + 2) * width)
                        x = x_ref[here, cols].astype(F32)
                        stepped = x * steps[:, cols]
                        weighted = []
                        for h in (head, head + 1):
                            gap = cum[:, h : h + 1] - rows_ref[b, h : h + 1, :]
                            decay = jnp.exp(jnp.where(causal, gap, -1e30))
                            weighted.append((scores_here * decay).astype(BF16))
                        stacked = jnp.concatenate(
                            [
                                jnp.where(lane < width, stepped, 0.0).astype(BF16),
                                jnp.where(lane < width, 0.0, stepped).astype(BF16),
                            ],
                            axis=0,
                        )
                        out = dot(jnp.concatenate(weighted, axis=1), stacked)
                        out_ref[here, cols] = out + skips[:, cols] * x

    def own_turn(j):
        return jnp.maximum(j - lone, 0)

    def wide_turn(j):
        return half * turns + own_turn(j)

    shape = jax.ShapeDtypeStruct
    score_shape = shape((blocks, groups, SPAN, SPAN), F32)
    maps_shape = shape((rows, state), BF16)
    outs = [shape((rows, inner // 2), F32), shape((rows, inner // 2), BF16)]
    turned = pl.BlockSpec((rows, state), lambda j: (0, own_turn(j)))
    scratch = [pltpu.VMEM((blocks, SPAN, SPAN), F32)]
    if lone:
        outs += [score_shape, maps_shape]
        more = (narrow, taps)
        more_specs = [
            pl.BlockSpec((model, state), lambda j: (0, 1), pipeline_mode=pl.Buffered(1)),
            once_spec(taps),
        ]
        scratch.append(pltpu.VMEM((rows + 8, state), F32))
    else:
        more, more_specs = (scores,), [once_spec(scores)]
    maps_at = inner // state
    return pl.pallas_call(
        body,
        grid=(lone + turns,),
        out_shape=outs,
        in_specs=[
            once_spec(scaled),
            once_spec(scale),
            pl.BlockSpec((model, state), lambda j: (0, wide_turn(j))),
            once_spec(skip),
            pl.BlockSpec((rows, state), lambda j: (0, maps_at), pipeline_mode=pl.Buffered(1)),
            pl.BlockSpec((rows, state), lambda j: (0, wide_turn(j))),
            once_spec(step),
            once_spec(cum),
        ]
        + more_specs,
        out_specs=[turned, turned] + [whole_spec(a) for a in outs[2:]],
        scratch_shapes=scratch,
        compiler_params=granted(60),
        name="inside",
    )(scaled, scale, wide, skip, conv, conv, step, cum, *more)


def log_rows(log):
    row = lax.broadcasted_iota(jnp.int32, (TAIL, log.shape[1]), 0)
    block = jnp.zeros((TAIL, log.shape[1]), F32)
    for k, part in enumerate(parts_of(log, 3)):
        block = jnp.where(row == k, part.astype(F32), block)
    return block.astype(BF16)


def log_of(message_ref, size):
    rows = message_ref[size : size + TAIL, :].astype(F32)
    return rows[0:1, :] + rows[1:2, :] + rows[2:3, :]


def combine_body(size, first):
    def body(later_ref, mine_ref, came_ref, *refs):
        if first:
            out_ref, before_ref, before_log_ref = refs
        else:
            prior_ref, prior_log_ref, out_ref, before_ref, before_log_ref = refs
        mine = mine_ref[0:size, :].astype(F32)
        came = came_ref[0:size, :].astype(F32)
        my_log, came_log = log_of(mine_ref, size), log_of(came_ref, size)

        @pl.when(later_ref[0] == 1)
        def _():
            out_ref[0:size, :] = (jnp.exp(my_log) * came + mine).astype(BF16)
            if first:
                before_ref[...] = came
                before_log_ref[0:1, :] = came_log
            else:
                before_ref[...] = jnp.exp(prior_log_ref[0:1, :]) * came + prior_ref[...]
                before_log_ref[0:1, :] = prior_log_ref[0:1, :] + came_log

        @pl.when(later_ref[0] == 0)
        def _():
            out_ref[0:size, :] = (jnp.exp(came_log) * mine + came).astype(BF16)
            if first:
                before_ref[...] = jnp.zeros_like(before_ref)
                before_log_ref[0:1, :] = jnp.zeros_like(came_log)
            else:
                before_ref[...] = prior_ref[...]
                before_log_ref[0:1, :] = prior_log_ref[0:1, :]

        out_ref[size : size + TAIL, :] = log_rows(my_log + came_log)

    return body


def finish(
    part, parts, index, later, entering, update, block_log, cum, maps, halves, gain, out_weight,
    inner, state, heads, groups, count,
):
    size = state // groups
    width = inner // heads
    rows = cum.shape[0] // parts
    last_part = part == parts - 1
    blocks = rows // SPAN
    model = out_weight.shape[1]
    turn_width = model // count
    first = len(entering) > 1

    def body(index_ref, later_ref, *refs):
        entering_refs, refs = refs[: len(entering)], refs[len(entering) :]
        update_ref, block_log_ref, cum_ref, maps_ref, *refs = refs
        half_refs, refs = (refs[0:2], refs[2:4]), refs[4:]
        gain_ref, weight_ref, top_ref, bottom_ref, mixed_ref, *memory_out = refs

        def both(k, here, cols):
            split = inner // 2
            pieces = []
            for h in range(2):
                low, high = max(cols.start, h * split), min(cols.stop, (h + 1) * split)
                if low < high:
                    pieces.append(half_refs[h][k][here, low - h * split : high - h * split])
            return pieces[0] if len(pieces) == 1 else jnp.concatenate(pieces, axis=1)

        @pl.when(pl.program_id(0) == 0)
        def _():
            expand = expander(heads, width)
            if first:
                came_ref, before_ref, before_log_ref, start_ref = entering_refs
                is_later = later_ref[0] == 1
                prior_log = before_log_ref[0:1, :]
                prior = before_ref[...]
                came = came_ref[0:size, :].astype(F32)
                came_log = log_of(came_ref, size)
                memory = jnp.where(is_later, jnp.exp(prior_log) * came + prior, prior)
                memory_log = jnp.where(is_later, prior_log + came_log, prior_log)
                memory = jnp.exp(memory_log) * start_ref[...] + memory
            else:
                memory = entering_refs[0][...]
            keep = jnp.exp(spread(block_log_ref[...], expand, 3))
            for b in range(blocks):
                here = slice(b * SPAN, (b + 1) * SPAN)
                reach = spread(jnp.exp(cum_ref[here, :]), expand)
                for g in range(groups):
                    cols = slice(g * inner // groups, (g + 1) * inner // groups)
                    carried = dot(
                        maps_ref[here, g * size : (g + 1) * size], memory[:, cols].astype(BF16)
                    )
                    scan = both(0, here, cols) + reach[:, cols] * carried
                    gate = both(1, here, cols)
                    gated = scan * silu(gate.astype(F32))
                    moment = jnp.mean(gated * gated, axis=-1, keepdims=True)
                    mixed_ref[here, cols] = (
                        gated * lax.rsqrt(moment + EPSILON) * gain_ref[:, cols].astype(F32)
                    ).astype(BF16)
                if not last_part or b < blocks - 1:
                    at = part * blocks + b
                    memory = keep[at : at + 1, :] * memory + update_ref[b]
            if memory_out:
                memory_out[0][...] = memory

        sent = dot(mixed_ref[...], weight_ref[...]).astype(BF16)

        @pl.when(pl.program_id(0) == 0)
        def _():
            top_ref[...] = sent

        @pl.when(pl.program_id(0) == 1)
        def _():
            bottom_ref[...] = sent

    def rows_of(array):
        once = pl.Buffered(1)
        return pl.BlockSpec((rows, array.shape[1]), lambda *_: (part, 0), pipeline_mode=once)

    shape = jax.ShapeDtypeStruct
    extra = [shape((rows, turn_width), BF16)] * 2 + [shape((rows, inner), BF16)]
    extra += [] if last_part else [shape((size, inner), F32)]

    return pl.pallas_call(
        body,
        out_shape=extra,
        grid_spec=pltpu.PrefetchScalarGridSpec(
            num_scalar_prefetch=2,
            grid=(2,),
            in_specs=[once_spec(a) for a in entering]
            + [
                pl.BlockSpec((blocks, size, inner), lambda *_: (part, 0, 0)),
                once_spec(block_log),
                rows_of(cum),
                rows_of(maps),
            ]
            + [rows_of(a) for half in halves for a in half]
            + [
                once_spec(gain),
                pl.BlockSpec((inner, turn_width), lambda j, *_: (0, (1 - j) * (count - 1))),
            ],
            out_specs=[whole_spec(a) for a in extra],
        ),
        compiler_params=granted(60),
        name="finish",
    )(
        index, later, *entering, update, block_log, cum, maps, *halves[0], *halves[1], gain,
        out_weight,
    )


def project_out(mixed, out_weight, count):
    rows, inner = mixed.shape
    model = out_weight.shape[1]
    width = model // count

    def body(mixed_ref, weight_ref, out_ref):
        out_ref[...] = dot(mixed_ref[...], weight_ref[...]).astype(BF16)

    return pl.pallas_call(
        body,
        grid=(count,),
        out_shape=jax.ShapeDtypeStruct((rows, model), BF16),
        in_specs=[once_spec(mixed), pl.BlockSpec((inner, width), lambda j: (0, j))],
        out_specs=pl.BlockSpec((rows, width), lambda j: (0, j)),
        compiler_params=granted(12),
        name="project_out",
    )(mixed, out_weight)


def relay(index, distance, partial, received, count):
    rows, model = partial.shape
    width = model // count

    def body(index_ref, ahead_ref, behind_ref, *refs):
        for own, came, out in zip((ahead_ref, behind_ref), refs[:-2], refs[-2:]):
            out[...] = (own[...].astype(F32) + came[...].astype(F32)).astype(BF16)

    def place(sign):
        return lambda j, i: (j, jnp.clip(i[0] + sign * distance, 0, count - 1))

    turns = 4
    whole = pl.BlockSpec((rows // turns, width), lambda j, i: (j, 0))
    shape = jax.ShapeDtypeStruct((rows, width), BF16)
    return pl.pallas_call(
        body,
        out_shape=[shape, shape],
        grid_spec=pltpu.PrefetchScalarGridSpec(
            num_scalar_prefetch=1,
            grid=(turns,),
            in_specs=[
                pl.BlockSpec((rows // turns, width), place(1)),
                pl.BlockSpec((rows // turns, width), place(-1)),
                whole,
                whole,
            ],
            out_specs=[whole, whole],
        ),
        compiler_params=granted(8),
        name="relay",
    )(index, partial, partial, *received)


def send_on(ahead, behind, distance, axis):
    count = lax.axis_size(axis)
    return (
        lax.ppermute(ahead, axis, [(i, i + 1) for i in range(count - distance)]),
        lax.ppermute(behind, axis, [(i, i - 1) for i in range(distance, count)]),
    )


def total(index, partial, received, hidden, row_block, count, filled):
    rows, model = partial.shape
    width = model // count
    turns = 4

    def body(index_ref, own_ref, ahead_ref, behind_ref, hidden_ref, *refs):
        summed = own_ref[...].astype(F32) + ahead_ref[...].astype(F32)
        summed = summed + behind_ref[...].astype(F32)
        refs[-1][...] = (summed + hidden_ref[...].astype(F32)).astype(BF16)

    block = (rows // turns, width)
    whole = pl.BlockSpec(block, lambda j, i: (j, 0))
    placed = pl.BlockSpec(block, lambda j, i: (row_block * turns + j, 0))
    return pl.pallas_call(
        body,
        out_shape=jax.ShapeDtypeStruct(hidden.shape, BF16),
        grid_spec=pltpu.PrefetchScalarGridSpec(
            num_scalar_prefetch=1,
            grid=(turns,),
            in_specs=[pl.BlockSpec(block, lambda j, i: (j, i[0])), whole, whole, placed]
            + [pl.BlockSpec(memory_space=pl.ANY)] * len(filled),
            out_specs=placed,
        ),
        input_output_aliases={5: 0} if filled else {},
        compiler_params=granted(8),
        name="total",
    )(index, partial, *received, hidden, *filled)


def on_device(
    hidden, norm_gain, gate_x_weight, state_weight, step_weight, conv_inner, conv_state,
    step_bias, decay_log, skip_gain, inner_gain, out_weight, initial_state,
):
    rows = hidden.shape[0]
    half = rows // 2
    inner = gate_x_weight.shape[2]
    state = state_weight.shape[2]
    heads = step_weight.shape[1]
    size = initial_state.shape[2]
    groups = state // size
    blocks = rows // SPAN
    feature_index = lax.axis_index("tp").reshape(1)
    range_index = lax.axis_index("seq")
    ranges = lax.axis_size("seq")

    model = step_weight.shape[0]
    parts_count = lax.axis_size("tp")
    narrow_weight = state_weight.reshape(model, 2 * state)
    step_rows = step_weight.T
    taps = jnp.concatenate([conv_inner, conv_state[:, 0]], axis=1)
    out_taps = conv_state[:, 1]
    start_state = initial_state.transpose(2, 0, 1).reshape(size, inner)
    gain = norm_gain.astype(F32)[None, :]
    out_gain = inner_gain[None, :]
    bias, rate, skip = step_bias[None, :], decay_log[None, :], skip_gain[None, :]

    halo = shifted(hidden[rows - TAIL :], "seq", 1)
    early = line_step([jnp.concatenate([halo, hidden[:half]], axis=0)] * 2, 1, "tp")[1:]
    late = line_step([hidden[half:]] * 2, 1, "tp")[1:]
    small = (narrow_weight, step_rows, taps, start_state, gain, out_gain)
    late[1:], small = lax.optimization_barrier((late[1:], small))
    narrow_weight, step_rows, taps, start_state, gain, out_gain = small
    wide = gate_x_weight.reshape(model, 2 * inner)
    for step in range(2, parts_count):
        early, late = line_step(early, step, "tp"), line_step(late, step, "tp")
        if step == 2:
            early[1:], late[1:], wide = lax.optimization_barrier((early[1:], late[1:], wide))

    shape = jax.ShapeDtypeStruct
    weights = (feature_index, gain, wide, narrow_weight, step_rows)
    begun = begin((early[:-2], late[:-2]), *weights, inner, state)
    last, begun = lax.optimization_barrier((early[-2:] + late[-2:], begun))
    scaled, scale, conv, step, cum, update, block_log, message = enter(
        begun, last, TAIL, *weights, taps, bias, rate, inner, state, size
    )

    def within(half, scores):
        return inside(
            half, scaled, scale, TAIL, wide, narrow_weight, out_taps, skip, conv, step, cum, scores,
            inner, state, size,
        )

    *first_half, scores, maps = within(0, None)
    second_half = within(1, scores)
    before = ()
    bit = 1
    while True:
        came = swapped(message, "seq", bit)
        if bit == 2:
            held = lax.optimization_barrier((came, first_half, scores, maps))
            came, first_half, scores, maps = held
            second_half = within(1, scores)
        later = ((range_index // bit) % 2).astype(jnp.int32).reshape(1)
        bit *= 2
        if bit == ranges:
            break
        message, *before = call(
            combine_body(size, not before),
            [
                shape((size + TAIL, inner), BF16),
                shape((size, inner), F32),
                shape((8, inner), F32),
            ],
            later,
            message,
            came,
            *before,
            scalars=1,
            name="combine",
            limit=14,
        )
    entering = (came, *before, start_state)
    partials, received = [], []
    halves = (first_half, second_half)
    for part in range(2):
        top, bottom, mixed, *entering = finish(
            part, 2, feature_index, later, entering, update, block_log, cum, maps, halves,
            out_gain, out_weight, inner, state, heads, groups, parts_count,
        )
        partials.append(mixed)
        received.append(send_on(top, bottom, parts_count - 1, "tp"))
    onward = ()
    for distance in range(parts_count - 2, 0, -1):
        for k in range(2):
            if distance == parts_count - 2:
                mixed, _ = lax.optimization_barrier((partials[k], onward))
                partials[k] = project_out(mixed, out_weight, parts_count)
            onward = relay(feature_index, distance, partials[k], received[k], parts_count)
            received[k] = send_on(*onward, distance, "tp")
    filled = ()
    for k, partial in enumerate(partials):
        filled = (
            total(feature_index, partial, received[k], hidden, k, parts_count, filled),
        )
    return filled[0]


def solution(mesh):
    return jax.shard_map(
        on_device,
        mesh=mesh,
        in_specs=(
            P("seq", "tp"),
            P(),
            P(None, None, "tp"),
            P(None, None, "tp"),
            P(None, "tp"),
            P(None, "tp"),
            P(None, None, "tp"),
            P("tp"),
            P("tp"),
            P("tp"),
            P("tp"),
            P("tp", None),
            P("tp", None, None),
        ),
        out_specs=P("seq", "tp"),
        check_vma=False,
    )
```

```python
import jax
import jax.numpy as jnp
from jax import lax
from jax.experimental import pallas as pl
from jax.experimental.pallas import tpu as pltpu
from jax.sharding import PartitionSpec as P

SPAN = 128
EPSILON = 1e-05
TAIL = 16
LANES = 128
F32 = jnp.float32
BF16 = jnp.bfloat16


def shifted(block, axis, distance):
    count = lax.axis_size(axis)
    route = [(i, i + distance) for i in range(count) if 0 <= i + distance < count]
    return lax.ppermute(block, axis, route)


def swapped(block, axis, bit):
    return lax.ppermute(block, axis, [(i, i ^ bit) for i in range(lax.axis_size(axis))])


def line_step(pieces, step, axis):
    count = lax.axis_size(axis)
    behind, ahead = pieces[-2], pieces[-1]
    behind = lax.ppermute(behind, axis, [(i, i + 1) for i in range(step - 1, count - 1)])
    ahead = lax.ppermute(ahead, axis, [(i, i - 1) for i in range(1, count - step + 1)])
    return pieces + [behind, ahead]


def whole_spec(array):
    rank = len(array.shape)
    return pl.BlockSpec(array.shape, lambda *_: (0,) * rank)


def once_spec(array):
    rank = len(array.shape)
    once = pl.Buffered(1)
    return pl.BlockSpec(array.shape, lambda *_: (0,) * rank, pipeline_mode=once)


def call(body, outs, *arrays, scratch=(), scalars=0, name=None, limit=60, turns=1):
    def spec_of(array):
        rows, columns = array.shape
        return pl.BlockSpec((rows, columns // turns), lambda j: (0, j))

    pairs = [a if isinstance(a, tuple) else (a, spec_of(a)) for a in arrays[scalars:]]
    return pl.pallas_call(
        body,
        out_shape=outs,
        grid=(turns,),
        in_specs=[pl.BlockSpec(memory_space=pltpu.SMEM)] * scalars + [spec for _, spec in pairs],
        out_specs=jax.tree.map(spec_of, outs),
        scratch_shapes=list(scratch),
        compiler_params=granted(limit),
        name=name,
    )(*arrays[:scalars], *[a for a, _ in pairs])


def granted(mebibytes):
    return pltpu.CompilerParams(vmem_limit_bytes=mebibytes * 2**20)


def dot(a, b, contract=((1,), (0,))):
    return lax.dot_general(a, b, (contract, ((), ())), preferred_element_type=F32)


def parts_of(x, count):
    parts = []
    for _ in range(count):
        part = x.astype(BF16)
        parts.append(part)
        x = x - part.astype(F32)
    return parts


def spread(x, expand, count=2):
    parts = [part.astype(F32) for part in parts_of(x, count)]
    return dot(
        jnp.concatenate(parts, axis=1).astype(BF16), jnp.concatenate([expand] * count, axis=0)
    )


def expander(heads, width, first=0, count=None):
    lanes = (count or heads) * width
    head = lax.broadcasted_iota(jnp.int32, (heads, lanes), 0) - first
    lane = lax.broadcasted_iota(jnp.int32, (heads, lanes), 1)
    inside = jnp.logical_and(lane >= head * width, lane < (head + 1) * width)
    return jnp.where(inside, 1.0, 0.0).astype(BF16)


def silu(v):
    return v * (1.0 / (1.0 + jnp.exp(-v)))


def conv_block(padded_ref, start, taps_ref, columns):
    summed = None
    for k in range(taps_ref.shape[0]):
        row = 8 + start - (taps_ref.shape[0] - 1) + k
        term = taps_ref[k : k + 1, columns].astype(F32) * padded_ref[row : row + SPAN, columns]
        summed = term if summed is None else summed + term
    return silu(summed).astype(BF16)


def rows_in(ref, raw, lead):
    ref[0:8, :] = raw[lead - 8 : lead, :].astype(F32)
    ref[8:, :] = raw[lead:, :].astype(F32)


def scale_in(piece, gain_ref, square_ref, scaled_ref, gain_start, start, width):
    def columns(k, carry):
        here = pl.ds(pl.multiple_of(k * LANES, LANES), LANES)
        there = pl.ds(pl.multiple_of(start + k * LANES, LANES), LANES)
        gain = gain_ref[:, pl.ds(pl.multiple_of(gain_start + k * LANES, LANES), LANES)]
        value = piece(here)
        square_ref[...] += value * value
        scaled_ref[:, there] = (value * gain).astype(BF16)
        return carry

    lax.fori_loop(0, width // LANES, columns, 0)


def row_starts(pieces):
    starts = [0]
    for piece in pieces:
        starts.append(starts[-1] + piece.shape[0])
    return starts


def begin(row_parts, index, gain, wide, narrow, steps, inner, state):
    starts = row_starts([part[0] for part in row_parts])
    rows, width = starts[-1], row_parts[0][0].shape[1]
    per_part = len(row_parts[0])
    pieces = [piece for part in row_parts for piece in part]
    model, heads = steps.shape[1], steps.shape[0]
    count = model // width
    turns = inner // state
    offsets = [(k + 1) // 2 * (-1) ** (k % 2) for k in range(per_part)] * len(row_parts)

    def body(index_ref, gain_ref, *refs):
        parts, refs = refs[: len(offsets)], refs[len(offsets) :]
        wide_ref, narrow_ref, steps_ref, out_ref, out_step_ref, square_ref, scaled_ref = refs
        turn = pl.program_id(0)

        @pl.when(turn == 0)
        def _():
            square_ref[...] = jnp.zeros_like(square_ref)
            scaled_ref[...] = jnp.zeros_like(scaled_ref)
            for at, (part, offset) in enumerate(zip(parts, offsets)):
                target = index_ref[0] + offset
                here_rows = pl.ds(starts[at // per_part], part.shape[0])

                @pl.when(jnp.logical_and(target >= 0, target < count))
                def _():
                    scale_in(
                        lambda here: part[:, here].astype(F32),
                        gain_ref, square_ref.at[here_rows], scaled_ref.at[here_rows],
                        target * width, target * width, width,
                    )

            out_ref[...] = dot(scaled_ref[...], narrow_ref[...])
            out_step_ref[...] = dot(scaled_ref[...], steps_ref[...], ((1,), (1,)))

        @pl.when(turn > 0)
        def _():
            out_ref[...] = dot(scaled_ref[...], wide_ref[...])

    shape = jax.ShapeDtypeStruct
    outs = [shape((rows, heads), F32), shape((rows, LANES), F32), shape((rows, model), BF16)]
    return pl.pallas_call(
        body,
        grid=(1 + turns,),
        out_shape=[shape((rows, inner + state), F32)] + outs,
        in_specs=[pl.BlockSpec(memory_space=pltpu.SMEM), once_spec(gain)]
        + [once_spec(piece) for piece in pieces]
        + [
            pl.BlockSpec((model, state), lambda j: (0, turns + jnp.maximum(j, 1) - 1)),
            pl.BlockSpec((model, state), lambda j: (0, 0), pipeline_mode=pl.Buffered(1)),
            once_spec(steps),
        ],
        out_specs=[pl.BlockSpec((rows, state), lambda j: (0, jnp.where(j == 0, turns, j - 1)))]
        + [whole_spec(a) for a in outs],
        compiler_params=granted(60),
        name="begin",
    )(index, gain, *pieces, wide, narrow, steps)


def enter(
    begun, pieces, lead, index, gain, wide, narrow, steps, taps, bias, rate, inner, state, size
):
    sums, step_sums, squares, scaled = begun
    starts = row_starts(pieces[::2])
    total_rows, width = starts[-1], pieces[0].shape[1]
    rows = total_rows - lead
    model, heads = steps.shape[1], steps.shape[0]
    count = model // width
    head_width = inner // heads
    groups = state // size
    turns = inner // state
    turn_heads = heads // turns
    blocks = rows // SPAN

    def body(
        index_ref, gain_ref, *refs,
    ):
        piece_refs, refs = refs[: len(pieces)], refs[len(pieces) :]
        enter_body(index_ref, gain_ref, piece_refs, *refs)

    def enter_body(
        index_ref, gain_ref, piece_refs, old_ref, squares_ref, sums_ref, step_sums_ref,
        wide_ref, narrow_ref, steps_ref, taps_ref, bias_ref, rate_ref,
        scaled_ref, scale_ref, conv_ref, step_ref, cum_ref, update_ref, block_log_ref,
        message_ref, square_ref, piece_ref, raw_ref, padded_ref, maps_ref, factor_ref, log_ref,
    ):
        turn = pl.program_id(0)

        @pl.when(turn == 0)
        def _():
            at_end = jnp.logical_or(index_ref[0] == 0, index_ref[0] == count - 1)
            square_ref[...] = squares_ref[...]
            for k, (behind, ahead) in enumerate(zip(piece_refs[::2], piece_refs[1::2])):
                here_rows = pl.ds(starts[k], behind.shape[0])
                scale_in(
                    lambda here: behind[:, here].astype(F32) + ahead[:, here].astype(F32),
                    gain_ref, square_ref.at[here_rows], piece_ref.at[here_rows], 0, 0, width,
                )

            @pl.when(at_end)
            def _():
                scaled_ref[...] = piece_ref[...]

            @pl.when(jnp.logical_not(at_end))
            def _():
                scaled_ref[...] = old_ref[...]

            moment = jnp.sum(square_ref[...], axis=-1, keepdims=True) * (1.0 / model)
            scale_ref[...] = jnp.broadcast_to(lax.rsqrt(moment + EPSILON), scale_ref.shape)
            raw = sums_ref[...] + dot(piece_ref[...], narrow_ref[...])
            raw_ref[...] = (raw * scale_ref[:, 0:1]).astype(BF16)
            raw_step = step_sums_ref[...] + dot(piece_ref[...], steps_ref[...], ((1,), (1,)))
            raw_step = (raw_step * scale_ref[:, 0:heads]).astype(BF16)
            row = lax.broadcasted_iota(jnp.int32, (SPAN, SPAN), 0)
            col = lax.broadcasted_iota(jnp.int32, (SPAN, SPAN), 1)
            lower = jnp.where(row >= col, 1.0, 0.0).astype(BF16)
            block_log_ref[...] = jnp.zeros_like(block_log_ref)
            total_log = jnp.zeros((1, heads), F32)
            for b in range(blocks):
                here = slice(b * SPAN, (b + 1) * SPAN)
                pre = raw_step[lead + b * SPAN : lead + (b + 1) * SPAN, :].astype(F32)
                pre = pre + bias_ref[...]
                step = jnp.maximum(pre, 0.0) + jnp.log1p(jnp.exp(-jnp.abs(pre)))
                log_decay = -step * jnp.exp(rate_ref[...])
                cum = None
                for part in parts_of(log_decay, 3):
                    term = dot(lower, part)
                    cum = term if cum is None else cum + term
                last = cum[SPAN - 1 : SPAN, :]
                step_ref[here, :] = step
                cum_ref[here, :] = cum
                block_log_ref[b : b + 1, :] = last
                factor_ref[here, :] = step * jnp.exp(last - cum)
                total_log = total_log + last
            log_ref[...] = jnp.broadcast_to(total_log, log_ref.shape)

        @pl.when(turn > 0)
        def _():
            raw = sums_ref[...] + dot(piece_ref[...], wide_ref[...])
            raw_ref[...] = (raw * scale_ref[:, 0:1]).astype(BF16)

        rows_in(padded_ref, raw_ref[...], lead)
        for b in range(blocks):
            conv_ref[b * SPAN : (b + 1) * SPAN, :] = conv_block(
                padded_ref, b * SPAN, taps_ref, slice(0, state)
            )

        @pl.when(turn == 0)
        def _():
            maps_ref[...] = conv_ref[...]

        for k in range(turns):

            @pl.when(turn == 1 + k)
            def _():
                group = k * state * groups // inner
                expand = expander(heads, head_width, k * turn_heads, turn_heads)
                keep = jnp.exp(spread(block_log_ref[...], expand, 3))
                total = None
                for b in range(blocks):
                    here = slice(b * SPAN, (b + 1) * SPAN)
                    factor = spread(factor_ref[here, :], expand)
                    stepped = (conv_ref[here, :].astype(F32) * factor).astype(BF16)
                    maps = maps_ref[here, group * size : (group + 1) * size]
                    update = dot(maps, stepped, ((0,), (0,)))
                    update_ref[b] = update
                    total = update if total is None else keep[b : b + 1, :] * total + update
                message_ref[0:size, :] = total.astype(BF16)
                log = spread(log_ref[...], expand, 3)[0:1, :]
                message_ref[size : size + TAIL, :] = log_rows(log)

    def any_turn(j):
        return jnp.where(j == 0, turns, j - 1)

    def wide_turn(j):
        return jnp.maximum(j, 1) - 1

    def target(i):
        return jnp.where(i[0] == 0, count - 1, 0)

    shape = jax.ShapeDtypeStruct
    once = pl.Buffered(1)
    turned = pl.BlockSpec((total_rows, state), lambda j, i: (0, any_turn(j)))
    placed = pl.BlockSpec((total_rows, width), lambda j, i: (0, target(i)), pipeline_mode=once)
    outs = [
        shape(scaled.shape, BF16),
        shape((total_rows, LANES), F32),
        shape((rows, inner + state), BF16),
        shape((rows, heads), F32),
        shape((rows, heads), F32),
        shape((blocks, size, inner), F32),
        shape((8, heads), F32),
        shape((size + TAIL, inner), BF16),
    ]
    out_specs = [whole_spec(a) for a in outs]
    out_specs[0] = pl.BlockSpec((total_rows, width), lambda j, i: (0, target(i)))
    out_specs[2] = pl.BlockSpec((rows, state), lambda j, i: (0, any_turn(j)))
    out_specs[5] = pl.BlockSpec((blocks, size, state), lambda j, i: (0, 0, wide_turn(j)))
    out_specs[7] = pl.BlockSpec((size + TAIL, state), lambda j, i: (0, wide_turn(j)))
    return pl.pallas_call(
        body,
        out_shape=outs,
        grid_spec=pltpu.PrefetchScalarGridSpec(
            num_scalar_prefetch=1,
            grid=(1 + turns,),
            in_specs=[
                pl.BlockSpec((1, width), lambda j, i: (0, target(i))),
                *[once_spec(piece) for piece in pieces],
                placed,
                once_spec(squares),
                turned,
                once_spec(step_sums),
                pl.BlockSpec((width, state), lambda j, i: (target(i), turns + wide_turn(j))),
                pl.BlockSpec((width, state), lambda j, i: (target(i), 0)),
                pl.BlockSpec((heads, width), lambda j, i: (0, target(i))),
                pl.BlockSpec((taps.shape[0], state), lambda j, i: (0, any_turn(j))),
                once_spec(bias),
                once_spec(rate),
            ],
            out_specs=out_specs,
            scratch_shapes=[
                pltpu.VMEM((total_rows, LANES), F32),
                pltpu.VMEM((total_rows, width), BF16),
                pltpu.VMEM((total_rows, state), BF16),
                pltpu.VMEM((rows + 8, state), F32),
                pltpu.VMEM((rows, state), BF16),
                pltpu.VMEM((rows, heads), F32),
                pltpu.VMEM((8, heads), F32),
            ],
        ),
        input_output_aliases={2 + len(pieces): 0},
        compiler_params=granted(60),
        name="enter",
    )(
        index, gain, *pieces, scaled, squares, sums, step_sums, wide, narrow, steps, taps, bias,
        rate,
    )


def inside(
    half, scaled, scale, lead, wide, narrow, taps, skip, conv, step, cum, scores, inner, state,
    size,
):
    total_rows, model = scaled.shape
    rows = total_rows - lead
    heads = step.shape[1]
    width = inner // heads
    groups = state // size
    turns = inner // state // 2
    turn_heads = heads // turns // 2
    blocks = rows // SPAN
    lone = 1 if scores is None else 0

    def body(scaled_ref, scale_ref, wide_ref, skip_ref, conv_ref, x_ref, step_ref, cum_ref, *refs):
        if lone:
            narrow_ref, taps_ref, out_ref, gate_ref, scores_ref, maps_ref, rows_ref, padded_ref = refs
        else:
            scores_ref, out_ref, gate_ref, rows_ref = refs
        turn = pl.program_id(0)

        @pl.when(turn == 0)
        def _():
            if lone:
                raw = (dot(scaled_ref[...], narrow_ref[...]) * scale_ref[:, 0:1]).astype(BF16)
                rows_in(padded_ref, raw, lead)
            for b in range(blocks):
                here = slice(b * SPAN, (b + 1) * SPAN)
                padding = jnp.zeros((SPAN, SPAN - heads), F32)
                rows_ref[b] = jnp.concatenate([cum_ref[here, :], padding], axis=1).T
                if not lone:
                    continue
                maps_ref[here, :] = conv_block(padded_ref, b * SPAN, taps_ref, slice(0, state))
                for g in range(groups):
                    cols = slice(g * size, (g + 1) * size)
                    scores_ref[b, g] = dot(maps_ref[here, cols], conv_ref[here, cols], ((1,), (1,)))

        row = lax.broadcasted_iota(jnp.int32, (SPAN, SPAN), 0)
        col = lax.broadcasted_iota(jnp.int32, (SPAN, SPAN), 1)
        causal = row >= col
        lane = lax.broadcasted_iota(jnp.int32, (SPAN, 2 * width), 1)
        for k in range(turns):

            @pl.when(turn == lone + k)
            def _():
                raw = dot(scaled_ref[lead:, :], wide_ref[...]) * scale_ref[lead:, 0:1]
                gate_ref[...] = raw.astype(BF16)
                first = (half * turns + k) * turn_heads
                expand = expander(heads, width, first, turn_heads)
                skips = spread(jnp.broadcast_to(skip_ref[...], (8, heads)), expand, 3)[0:1, :]
                for b in range(blocks):
                    here = slice(b * SPAN, (b + 1) * SPAN)
                    steps = spread(step_ref[here, :], expand)
                    cum = cum_ref[here, :]
                    for pair in range(turn_heads // 2):
                        head = first + 2 * pair
                        scores_here = scores_ref[b, head * groups // heads]
                        cols = slice(2 * pair * width, (2 * pair + 2) * width)
                        x = x_ref[here, cols].astype(F32)
                        stepped = x * steps[:, cols]
                        weighted = []
                        for h in (head, head + 1):
                            gap = cum[:, h : h + 1] - rows_ref[b, h : h + 1, :]
                            decay = jnp.exp(jnp.where(causal, gap, -1e30))
                            weighted.append((scores_here * decay).astype(BF16))
                        stacked = jnp.concatenate(
                            [
                                jnp.where(lane < width, stepped, 0.0).astype(BF16),
                                jnp.where(lane < width, 0.0, stepped).astype(BF16),
                            ],
                            axis=0,
                        )
                        out = dot(jnp.concatenate(weighted, axis=1), stacked)
                        out_ref[here, cols] = out + skips[:, cols] * x

    def own_turn(j):
        return jnp.maximum(j - lone, 0)

    def wide_turn(j):
        return half * turns + own_turn(j)

    shape = jax.ShapeDtypeStruct
    score_shape = shape((blocks, groups, SPAN, SPAN), F32)
    maps_shape = shape((rows, state), BF16)
    outs = [shape((rows, inner // 2), F32), shape((rows, inner // 2), BF16)]
    turned = pl.BlockSpec((rows, state), lambda j: (0, own_turn(j)))
    scratch = [pltpu.VMEM((blocks, SPAN, SPAN), F32)]
    if lone:
        outs += [score_shape, maps_shape]
        more = (narrow, taps)
        more_specs = [
            pl.BlockSpec((model, state), lambda j: (0, 1), pipeline_mode=pl.Buffered(1)),
            once_spec(taps),
        ]
        scratch.append(pltpu.VMEM((rows + 8, state), F32))
    else:
        more, more_specs = (scores,), [once_spec(scores)]
    maps_at = inner // state
    return pl.pallas_call(
        body,
        grid=(lone + turns,),
        out_shape=outs,
        in_specs=[
            once_spec(scaled),
            once_spec(scale),
            pl.BlockSpec((model, state), lambda j: (0, wide_turn(j))),
            once_spec(skip),
            pl.BlockSpec((rows, state), lambda j: (0, maps_at), pipeline_mode=pl.Buffered(1)),
            pl.BlockSpec((rows, state), lambda j: (0, wide_turn(j))),
            once_spec(step),
            once_spec(cum),
        ]
        + more_specs,
        out_specs=[turned, turned] + [whole_spec(a) for a in outs[2:]],
        scratch_shapes=scratch,
        compiler_params=granted(60),
        name="inside",
    )(scaled, scale, wide, skip, conv, conv, step, cum, *more)


def log_rows(log):
    row = lax.broadcasted_iota(jnp.int32, (TAIL, log.shape[1]), 0)
    block = jnp.zeros((TAIL, log.shape[1]), F32)
    for k, part in enumerate(parts_of(log, 3)):
        block = jnp.where(row == k, part.astype(F32), block)
    return block.astype(BF16)


def log_of(message_ref, size):
    rows = message_ref[size : size + TAIL, :].astype(F32)
    return rows[0:1, :] + rows[1:2, :] + rows[2:3, :]


def combine_body(size, first):
    def body(later_ref, mine_ref, came_ref, *refs):
        if first:
            out_ref, before_ref, before_log_ref = refs
        else:
            prior_ref, prior_log_ref, out_ref, before_ref, before_log_ref = refs
        mine = mine_ref[0:size, :].astype(F32)
        came = came_ref[0:size, :].astype(F32)
        my_log, came_log = log_of(mine_ref, size), log_of(came_ref, size)

        @pl.when(later_ref[0] == 1)
        def _():
            out_ref[0:size, :] = (jnp.exp(my_log) * came + mine).astype(BF16)
            if first:
                before_ref[...] = came
                before_log_ref[0:1, :] = came_log
            else:
                before_ref[...] = jnp.exp(prior_log_ref[0:1, :]) * came + prior_ref[...]
                before_log_ref[0:1, :] = prior_log_ref[0:1, :] + came_log

        @pl.when(later_ref[0] == 0)
        def _():
            out_ref[0:size, :] = (jnp.exp(came_log) * mine + came).astype(BF16)
            if first:
                before_ref[...] = jnp.zeros_like(before_ref)
                before_log_ref[0:1, :] = jnp.zeros_like(came_log)
            else:
                before_ref[...] = prior_ref[...]
                before_log_ref[0:1, :] = prior_log_ref[0:1, :]

        out_ref[size : size + TAIL, :] = log_rows(my_log + came_log)

    return body


def finish(
    part, parts, index, later, entering, update, block_log, cum, maps, halves, gain, out_weight,
    inner, state, heads, groups, count,
):
    size = state // groups
    width = inner // heads
    rows = cum.shape[0] // parts
    last_part = part == parts - 1
    blocks = rows // SPAN
    model = out_weight.shape[1]
    turn_width = model // count
    first = len(entering) > 1

    def body(index_ref, later_ref, *refs):
        entering_refs, refs = refs[: len(entering)], refs[len(entering) :]
        update_ref, block_log_ref, cum_ref, maps_ref, *refs = refs
        half_refs, refs = (refs[0:2], refs[2:4]), refs[4:]
        gain_ref, weight_ref, top_ref, bottom_ref, mixed_ref, *memory_out = refs

        def both(k, here, cols):
            split = inner // 2
            pieces = []
            for h in range(2):
                low, high = max(cols.start, h * split), min(cols.stop, (h + 1) * split)
                if low < high:
                    pieces.append(half_refs[h][k][here, low - h * split : high - h * split])
            return pieces[0] if len(pieces) == 1 else jnp.concatenate(pieces, axis=1)

        @pl.when(pl.program_id(0) == 0)
        def _():
            expand = expander(heads, width)
            if first:
                came_ref, before_ref, before_log_ref, start_ref = entering_refs
                is_later = later_ref[0] == 1
                prior_log = before_log_ref[0:1, :]
                prior = before_ref[...]
                came = came_ref[0:size, :].astype(F32)
                came_log = log_of(came_ref, size)
                memory = jnp.where(is_later, jnp.exp(prior_log) * came + prior, prior)
                memory_log = jnp.where(is_later, prior_log + came_log, prior_log)
                memory = jnp.exp(memory_log) * start_ref[...].T + memory
            else:
                memory = entering_refs[0][...]
            keep = jnp.exp(spread(block_log_ref[...], expand, 3))
            for b in range(blocks):
                here = slice(b * SPAN, (b + 1) * SPAN)
                reach = spread(jnp.exp(cum_ref[here, :]), expand)
                for g in range(groups):
                    cols = slice(g * inner // groups, (g + 1) * inner // groups)
                    carried = dot(
                        maps_ref[here, g * size : (g + 1) * size], memory[:, cols].astype(BF16)
                    )
                    scan = both(0, here, cols) + reach[:, cols] * carried
                    gate = both(1, here, cols)
                    gated = scan * silu(gate.astype(F32))
                    moment = jnp.mean(gated * gated, axis=-1, keepdims=True)
                    mixed_ref[here, cols] = (
                        gated * lax.rsqrt(moment + EPSILON) * gain_ref[:, cols].astype(F32)
                    ).astype(BF16)
                if not last_part or b < blocks - 1:
                    at = part * blocks + b
                    memory = keep[at : at + 1, :] * memory + update_ref[b]
            if memory_out:
                memory_out[0][...] = memory

        sent = dot(mixed_ref[...], weight_ref[...]).astype(BF16)

        @pl.when(pl.program_id(0) == 0)
        def _():
            top_ref[...] = sent

        @pl.when(pl.program_id(0) == 1)
        def _():
            bottom_ref[...] = sent

    def rows_of(array):
        once = pl.Buffered(1)
        return pl.BlockSpec((rows, array.shape[1]), lambda *_: (part, 0), pipeline_mode=once)

    shape = jax.ShapeDtypeStruct
    extra = [shape((rows, turn_width), BF16)] * 2 + [shape((rows, inner), BF16)]
    extra += [] if last_part else [shape((size, inner), F32)]

    return pl.pallas_call(
        body,
        out_shape=extra,
        grid_spec=pltpu.PrefetchScalarGridSpec(
            num_scalar_prefetch=2,
            grid=(2,),
            in_specs=[once_spec(a) for a in entering]
            + [
                pl.BlockSpec((blocks, size, inner), lambda *_: (part, 0, 0)),
                once_spec(block_log),
                rows_of(cum),
                rows_of(maps),
            ]
            + [rows_of(a) for half in halves for a in half]
            + [
                once_spec(gain),
                pl.BlockSpec((inner, turn_width), lambda j, *_: (0, (1 - j) * (count - 1))),
            ],
            out_specs=[whole_spec(a) for a in extra],
        ),
        compiler_params=granted(60),
        name="finish",
    )(
        index, later, *entering, update, block_log, cum, maps, *halves[0], *halves[1], gain,
        out_weight,
    )


def project_out(mixed, out_weight, count):
    rows, inner = mixed.shape
    model = out_weight.shape[1]
    width = model // count

    def body(mixed_ref, weight_ref, out_ref):
        out_ref[...] = dot(mixed_ref[...], weight_ref[...]).astype(BF16)

    return pl.pallas_call(
        body,
        grid=(count,),
        out_shape=jax.ShapeDtypeStruct((rows, model), BF16),
        in_specs=[once_spec(mixed), pl.BlockSpec((inner, width), lambda j: (0, j))],
        out_specs=pl.BlockSpec((rows, width), lambda j: (0, j)),
        compiler_params=granted(12),
        name="project_out",
    )(mixed, out_weight)


def relay(index, distance, partial, received, count):
    rows, model = partial.shape
    width = model // count

    def body(index_ref, ahead_ref, behind_ref, *refs):
        for own, came, out in zip((ahead_ref, behind_ref), refs[:-2], refs[-2:]):
            out[...] = (own[...].astype(F32) + came[...].astype(F32)).astype(BF16)

    def place(sign):
        return lambda j, i: (j, jnp.clip(i[0] + sign * distance, 0, count - 1))

    turns = 4
    whole = pl.BlockSpec((rows // turns, width), lambda j, i: (j, 0))
    shape = jax.ShapeDtypeStruct((rows, width), BF16)
    return pl.pallas_call(
        body,
        out_shape=[shape, shape],
        grid_spec=pltpu.PrefetchScalarGridSpec(
            num_scalar_prefetch=1,
            grid=(turns,),
            in_specs=[
                pl.BlockSpec((rows // turns, width), place(1)),
                pl.BlockSpec((rows // turns, width), place(-1)),
                whole,
                whole,
            ],
            out_specs=[whole, whole],
        ),
        compiler_params=granted(8),
        name="relay",
    )(index, partial, partial, *received)


def send_on(ahead, behind, distance, axis):
    count = lax.axis_size(axis)
    return (
        lax.ppermute(ahead, axis, [(i, i + 1) for i in range(count - distance)]),
        lax.ppermute(behind, axis, [(i, i - 1) for i in range(distance, count)]),
    )


def total(index, partial, received, hidden, row_block, count, filled):
    rows, model = partial.shape
    width = model // count
    turns = 4

    def body(index_ref, own_ref, ahead_ref, behind_ref, hidden_ref, *refs):
        summed = own_ref[...].astype(F32) + ahead_ref[...].astype(F32)
        summed = summed + behind_ref[...].astype(F32)
        refs[-1][...] = (summed + hidden_ref[...].astype(F32)).astype(BF16)

    block = (rows // turns, width)
    whole = pl.BlockSpec(block, lambda j, i: (j, 0))
    placed = pl.BlockSpec(block, lambda j, i: (row_block * turns + j, 0))
    return pl.pallas_call(
        body,
        out_shape=jax.ShapeDtypeStruct(hidden.shape, BF16),
        grid_spec=pltpu.PrefetchScalarGridSpec(
            num_scalar_prefetch=1,
            grid=(turns,),
            in_specs=[pl.BlockSpec(block, lambda j, i: (j, i[0])), whole, whole, placed]
            + [pl.BlockSpec(memory_space=pl.ANY)] * len(filled),
            out_specs=placed,
        ),
        input_output_aliases={5: 0} if filled else {},
        compiler_params=granted(8),
        name="total",
    )(index, partial, *received, hidden, *filled)


def on_device(
    hidden, norm_gain, gate_x_weight, state_weight, step_weight, conv_inner, conv_state,
    step_bias, decay_log, skip_gain, inner_gain, out_weight, initial_state,
):
    rows = hidden.shape[0]
    half = rows // 2
    inner = gate_x_weight.shape[2]
    state = state_weight.shape[2]
    heads = step_weight.shape[1]
    size = initial_state.shape[2]
    groups = state // size
    blocks = rows // SPAN
    feature_index = lax.axis_index("tp").reshape(1)
    range_index = lax.axis_index("seq")
    ranges = lax.axis_size("seq")

    model = step_weight.shape[0]
    parts_count = lax.axis_size("tp")
    narrow_weight = state_weight.reshape(model, 2 * state)
    step_rows = step_weight.T
    taps = jnp.concatenate([conv_inner, conv_state[:, 0]], axis=1)
    out_taps = conv_state[:, 1]
    start_state = initial_state.reshape(inner, size)
    gain = norm_gain.astype(F32)[None, :]
    out_gain = inner_gain[None, :]
    bias, rate, skip = step_bias[None, :], decay_log[None, :], skip_gain[None, :]

    halo = shifted(hidden[rows - TAIL :], "seq", 1)
    early = line_step([jnp.concatenate([halo, hidden[:half]], axis=0)] * 2, 1, "tp")[1:]
    late = line_step([hidden[half:]] * 2, 1, "tp")[1:]
    small = (narrow_weight, step_rows, taps, start_state, gain, out_gain)
    late[1:], small = lax.optimization_barrier((late[1:], small))
    narrow_weight, step_rows, taps, start_state, gain, out_gain = small
    wide = gate_x_weight.reshape(model, 2 * inner)
    for step in range(2, parts_count):
        early, late = line_step(early, step, "tp"), line_step(late, step, "tp")
        if step == 2:
            early[1:], late[1:], wide = lax.optimization_barrier((early[1:], late[1:], wide))

    shape = jax.ShapeDtypeStruct
    weights = (feature_index, gain, wide, narrow_weight, step_rows)
    begun = begin((early[:-2], late[:-2]), *weights, inner, state)
    last, begun = lax.optimization_barrier((early[-2:] + late[-2:], begun))
    scaled, scale, conv, step, cum, update, block_log, message = enter(
        begun, last, TAIL, *weights, taps, bias, rate, inner, state, size
    )

    def within(half, scores):
        return inside(
            half, scaled, scale, TAIL, wide, narrow_weight, out_taps, skip, conv, step, cum, scores,
            inner, state, size,
        )

    *first_half, scores, maps = within(0, None)
    second_half = within(1, scores)
    before = ()
    bit = 1
    while True:
        came = swapped(message, "seq", bit)
        if bit == 2:
            held = lax.optimization_barrier((came, first_half, scores, maps))
            came, first_half, scores, maps = held
            second_half = within(1, scores)
        later = ((range_index // bit) % 2).astype(jnp.int32).reshape(1)
        bit *= 2
        if bit == ranges:
            break
        message, *before = call(
            combine_body(size, not before),
            [
                shape((size + TAIL, inner), BF16),
                shape((size, inner), F32),
                shape((8, inner), F32),
            ],
            later,
            message,
            came,
            *before,
            scalars=1,
            name="combine",
            limit=14,
        )
    entering = (came, *before, start_state)
    partials, received = [], []
    halves = (first_half, second_half)
    for part in range(2):
        top, bottom, mixed, *entering = finish(
            part, 2, feature_index, later, entering, update, block_log, cum, maps, halves,
            out_gain, out_weight, inner, state, heads, groups, parts_count,
        )
        partials.append(mixed)
        received.append(send_on(top, bottom, parts_count - 1, "tp"))
    onward = ()
    for distance in range(parts_count - 2, 0, -1):
        for k in range(2):
            if distance == parts_count - 2:
                mixed, _ = lax.optimization_barrier((partials[k], onward))
                partials[k] = project_out(mixed, out_weight, parts_count)
            onward = relay(feature_index, distance, partials[k], received[k], parts_count)
            received[k] = send_on(*onward, distance, "tp")
    filled = ()
    for k, partial in enumerate(partials):
        filled = (
            total(feature_index, partial, received[k], hidden, k, parts_count, filled),
        )
    return filled[0]


def solution(mesh):
    return jax.shard_map(
        on_device,
        mesh=mesh,
        in_specs=(
            P("seq", "tp"),
            P(),
            P(None, None, "tp"),
            P(None, None, "tp"),
            P(None, "tp"),
            P(None, "tp"),
            P(None, None, "tp"),
            P("tp"),
            P("tp"),
            P("tp"),
            P("tp"),
            P("tp", None),
            P("tp", None, None),
        ),
        out_specs=P("seq", "tp"),
        check_vma=False,
    )
```

```python
import jax
import jax.numpy as jnp
from jax import lax
from jax.experimental import pallas as pl
from jax.experimental.pallas import tpu as pltpu
from jax.sharding import PartitionSpec as P

SPAN = 128
EPSILON = 1e-05
TAIL = 16
LANES = 128
F32 = jnp.float32
BF16 = jnp.bfloat16


def shifted(block, axis, distance):
    count = lax.axis_size(axis)
    route = [(i, i + distance) for i in range(count) if 0 <= i + distance < count]
    return lax.ppermute(block, axis, route)


def swapped(block, axis, bit):
    return lax.ppermute(block, axis, [(i, i ^ bit) for i in range(lax.axis_size(axis))])


def line_step(pieces, step, axis):
    count = lax.axis_size(axis)
    behind, ahead = pieces[-2], pieces[-1]
    behind = lax.ppermute(behind, axis, [(i, i + 1) for i in range(step - 1, count - 1)])
    ahead = lax.ppermute(ahead, axis, [(i, i - 1) for i in range(1, count - step + 1)])
    return pieces + [behind, ahead]


def whole_spec(array):
    rank = len(array.shape)
    return pl.BlockSpec(array.shape, lambda *_: (0,) * rank)


def once_spec(array):
    rank = len(array.shape)
    once = pl.Buffered(1)
    return pl.BlockSpec(array.shape, lambda *_: (0,) * rank, pipeline_mode=once)


def call(body, outs, *arrays, scratch=(), scalars=0, name=None, limit=60, turns=1):
    def spec_of(array):
        rows, columns = array.shape
        return pl.BlockSpec((rows, columns // turns), lambda j: (0, j))

    pairs = [a if isinstance(a, tuple) else (a, spec_of(a)) for a in arrays[scalars:]]
    return pl.pallas_call(
        body,
        out_shape=outs,
        grid=(turns,),
        in_specs=[pl.BlockSpec(memory_space=pltpu.SMEM)] * scalars + [spec for _, spec in pairs],
        out_specs=jax.tree.map(spec_of, outs),
        scratch_shapes=list(scratch),
        compiler_params=granted(limit),
        name=name,
    )(*arrays[:scalars], *[a for a, _ in pairs])


def granted(mebibytes):
    return pltpu.CompilerParams(vmem_limit_bytes=mebibytes * 2**20)


def dot(a, b, contract=((1,), (0,))):
    return lax.dot_general(a, b, (contract, ((), ())), preferred_element_type=F32)


def parts_of(x, count):
    parts = []
    for _ in range(count):
        part = x.astype(BF16)
        parts.append(part)
        x = x - part.astype(F32)
    return parts


def spread(x, expand, count=2):
    parts = [part.astype(F32) for part in parts_of(x, count)]
    return dot(
        jnp.concatenate(parts, axis=1).astype(BF16), jnp.concatenate([expand] * count, axis=0)
    )


def expander(heads, width, first=0, count=None):
    lanes = (count or heads) * width
    head = lax.broadcasted_iota(jnp.int32, (heads, lanes), 0) - first
    lane = lax.broadcasted_iota(jnp.int32, (heads, lanes), 1)
    inside = jnp.logical_and(lane >= head * width, lane < (head + 1) * width)
    return jnp.where(inside, 1.0, 0.0).astype(BF16)


def silu(v):
    return v * (1.0 / (1.0 + jnp.exp(-v)))


def conv_block(padded_ref, start, taps_ref, columns):
    summed = None
    for k in range(taps_ref.shape[0]):
        row = 8 + start - (taps_ref.shape[0] - 1) + k
        term = taps_ref[k : k + 1, columns].astype(F32) * padded_ref[row : row + SPAN, columns]
        summed = term if summed is None else summed + term
    return silu(summed).astype(BF16)


def rows_in(ref, raw, lead):
    ref[0:8, :] = raw[lead - 8 : lead, :].astype(F32)
    ref[8:, :] = raw[lead:, :].astype(F32)


def scale_in(piece, gain_ref, square_ref, scaled_ref, gain_start, start, width):
    def columns(k, carry):
        here = pl.ds(pl.multiple_of(k * LANES, LANES), LANES)
        there = pl.ds(pl.multiple_of(start + k * LANES, LANES), LANES)
        gain = gain_ref[:, pl.ds(pl.multiple_of(gain_start + k * LANES, LANES), LANES)]
        value = piece(here)
        square_ref[...] += value * value
        scaled_ref[:, there] = (value * gain).astype(BF16)
        return carry

    lax.fori_loop(0, width // LANES, columns, 0)


def row_starts(pieces):
    starts = [0]
    for piece in pieces:
        starts.append(starts[-1] + piece.shape[0])
    return starts


def begin(row_parts, index, gain, wide, narrow, steps, inner, state):
    starts = row_starts([part[0] for part in row_parts])
    rows, width = starts[-1], row_parts[0][0].shape[1]
    per_part = len(row_parts[0])
    pieces = [piece for part in row_parts for piece in part]
    model, heads = steps.shape[1], steps.shape[0]
    count = model // width
    turns = inner // state
    offsets = [(k + 1) // 2 * (-1) ** (k % 2) for k in range(per_part)] * len(row_parts)

    def body(index_ref, gain_ref, *refs):
        parts, refs = refs[: len(offsets)], refs[len(offsets) :]
        wide_ref, narrow_ref, steps_ref, out_ref, out_step_ref, square_ref, scaled_ref = refs
        turn = pl.program_id(0)

        @pl.when(turn == 0)
        def _():
            square_ref[...] = jnp.zeros_like(square_ref)
            scaled_ref[...] = jnp.zeros_like(scaled_ref)
            for at, (part, offset) in enumerate(zip(parts, offsets)):
                target = index_ref[0] + offset
                here_rows = pl.ds(starts[at // per_part], part.shape[0])

                @pl.when(jnp.logical_and(target >= 0, target < count))
                def _():
                    scale_in(
                        lambda here: part[:, here].astype(F32),
                        gain_ref, square_ref.at[here_rows], scaled_ref.at[here_rows],
                        target * width, target * width, width,
                    )

            out_ref[...] = dot(scaled_ref[...], narrow_ref[...])
            out_step_ref[...] = dot(scaled_ref[...], steps_ref[...], ((1,), (1,)))

        @pl.when(turn > 0)
        def _():
            out_ref[...] = dot(scaled_ref[...], wide_ref[...])

    shape = jax.ShapeDtypeStruct
    outs = [shape((rows, heads), F32), shape((rows, LANES), F32), shape((rows, model), BF16)]
    return pl.pallas_call(
        body,
        grid=(1 + turns,),
        out_shape=[shape((rows, inner + state), F32)] + outs,
        in_specs=[pl.BlockSpec(memory_space=pltpu.SMEM), once_spec(gain)]
        + [once_spec(piece) for piece in pieces]
        + [
            pl.BlockSpec((model, state), lambda j: (0, turns + jnp.maximum(j, 1) - 1)),
            pl.BlockSpec((model, state), lambda j: (0, 0), pipeline_mode=pl.Buffered(1)),
            once_spec(steps),
        ],
        out_specs=[pl.BlockSpec((rows, state), lambda j: (0, jnp.where(j == 0, turns, j - 1)))]
        + [whole_spec(a) for a in outs],
        compiler_params=granted(60),
        name="begin",
    )(index, gain, *pieces, wide, narrow, steps)


def enter(
    begun, pieces, lead, index, gain, wide, narrow, steps, taps, bias, rate, inner, state, size
):
    sums, step_sums, squares, scaled = begun
    starts = row_starts(pieces[::2])
    total_rows, width = starts[-1], pieces[0].shape[1]
    rows = total_rows - lead
    model, heads = steps.shape[1], steps.shape[0]
    count = model // width
    head_width = inner // heads
    groups = state // size
    turns = inner // state
    turn_heads = heads // turns
    blocks = rows // SPAN

    def body(
        index_ref, gain_ref, *refs,
    ):
        piece_refs, refs = refs[: len(pieces)], refs[len(pieces) :]
        enter_body(index_ref, gain_ref, piece_refs, *refs)

    def enter_body(
        index_ref, gain_ref, piece_refs, old_ref, squares_ref, sums_ref, step_sums_ref,
        wide_ref, narrow_ref, steps_ref, taps_ref, bias_ref, rate_ref,
        scaled_ref, scale_ref, conv_ref, step_ref, cum_ref, update_ref, block_log_ref,
        message_ref, square_ref, piece_ref, raw_ref, padded_ref, maps_ref, factor_ref, log_ref,
    ):
        turn = pl.program_id(0)

        @pl.when(turn == 0)
        def _():
            at_end = jnp.logical_or(index_ref[0] == 0, index_ref[0] == count - 1)
            square_ref[...] = squares_ref[...]
            for k, (behind, ahead) in enumerate(zip(piece_refs[::2], piece_refs[1::2])):
                here_rows = pl.ds(starts[k], behind.shape[0])
                scale_in(
                    lambda here: behind[:, here].astype(F32) + ahead[:, here].astype(F32),
                    gain_ref, square_ref.at[here_rows], piece_ref.at[here_rows], 0, 0, width,
                )

            @pl.when(at_end)
            def _():
                scaled_ref[...] = piece_ref[...]

            @pl.when(jnp.logical_not(at_end))
            def _():
                scaled_ref[...] = old_ref[...]

            moment = jnp.sum(square_ref[...], axis=-1, keepdims=True) * (1.0 / model)
            scale_ref[...] = jnp.broadcast_to(lax.rsqrt(moment + EPSILON), scale_ref.shape)
            raw = sums_ref[...] + dot(piece_ref[...], narrow_ref[...])
            raw_ref[...] = (raw * scale_ref[:, 0:1]).astype(BF16)
            raw_step = step_sums_ref[...] + dot(piece_ref[...], steps_ref[...], ((1,), (1,)))
            raw_step = (raw_step * scale_ref[:, 0:heads]).astype(BF16)
            row = lax.broadcasted_iota(jnp.int32, (SPAN, SPAN), 0)
            col = lax.broadcasted_iota(jnp.int32, (SPAN, SPAN), 1)
            lower = jnp.where(row >= col, 1.0, 0.0).astype(BF16)
            block_log_ref[...] = jnp.zeros_like(block_log_ref)
            total_log = jnp.zeros((1, heads), F32)
            for b in range(blocks):
                here = slice(b * SPAN, (b + 1) * SPAN)
                pre = raw_step[lead + b * SPAN : lead + (b + 1) * SPAN, :].astype(F32)
                pre = pre + bias_ref[...]
                step = jnp.maximum(pre, 0.0) + jnp.log1p(jnp.exp(-jnp.abs(pre)))
                log_decay = -step * jnp.exp(rate_ref[...])
                cum = None
                for part in parts_of(log_decay, 3):
                    term = dot(lower, part)
                    cum = term if cum is None else cum + term
                last = cum[SPAN - 1 : SPAN, :]
                step_ref[here, :] = step
                cum_ref[here, :] = cum
                block_log_ref[b : b + 1, :] = last
                factor_ref[here, :] = step * jnp.exp(last - cum)
                total_log = total_log + last
            log_ref[...] = jnp.broadcast_to(total_log, log_ref.shape)

        @pl.when(turn > 0)
        def _():
            raw = sums_ref[...] + dot(piece_ref[...], wide_ref[...])
            raw_ref[...] = (raw * scale_ref[:, 0:1]).astype(BF16)

        rows_in(padded_ref, raw_ref[...], lead)
        for b in range(blocks):
            conv_ref[b * SPAN : (b + 1) * SPAN, :] = conv_block(
                padded_ref, b * SPAN, taps_ref, slice(0, state)
            )

        @pl.when(turn == 0)
        def _():
            maps_ref[...] = conv_ref[...]

        for k in range(turns):

            @pl.when(turn == 1 + k)
            def _():
                group = k * state * groups // inner
                expand = expander(heads, head_width, k * turn_heads, turn_heads)
                keep = jnp.exp(spread(block_log_ref[...], expand, 3))
                total = None
                for b in range(blocks):
                    here = slice(b * SPAN, (b + 1) * SPAN)
                    factor = spread(factor_ref[here, :], expand)
                    stepped = (conv_ref[here, :].astype(F32) * factor).astype(BF16)
                    maps = maps_ref[here, group * size : (group + 1) * size]
                    update = dot(maps, stepped, ((0,), (0,)))
                    update_ref[b] = update
                    total = update if total is None else keep[b : b + 1, :] * total + update
                message_ref[0:size, :] = total.astype(BF16)
                log = spread(log_ref[...], expand, 3)[0:1, :]
                message_ref[size : size + TAIL, :] = log_rows(log)

    def any_turn(j):
        return jnp.where(j == 0, turns, j - 1)

    def wide_turn(j):
        return jnp.maximum(j, 1) - 1

    def target(i):
        return jnp.where(i[0] == 0, count - 1, 0)

    shape = jax.ShapeDtypeStruct
    once = pl.Buffered(1)
    turned = pl.BlockSpec((total_rows, state), lambda j, i: (0, any_turn(j)))
    placed = pl.BlockSpec((total_rows, width), lambda j, i: (0, target(i)), pipeline_mode=once)
    outs = [
        shape(scaled.shape, BF16),
        shape((total_rows, LANES), F32),
        shape((rows, inner + state), BF16),
        shape((rows, heads), F32),
        shape((rows, heads), F32),
        shape((blocks, size, inner), F32),
        shape((8, heads), F32),
        shape((size + TAIL, inner), BF16),
    ]
    out_specs = [whole_spec(a) for a in outs]
    out_specs[0] = pl.BlockSpec((total_rows, width), lambda j, i: (0, target(i)))
    out_specs[2] = pl.BlockSpec((rows, state), lambda j, i: (0, any_turn(j)))
    out_specs[5] = pl.BlockSpec((blocks, size, state), lambda j, i: (0, 0, wide_turn(j)))
    out_specs[7] = pl.BlockSpec((size + TAIL, state), lambda j, i: (0, wide_turn(j)))
    return pl.pallas_call(
        body,
        out_shape=outs,
        grid_spec=pltpu.PrefetchScalarGridSpec(
            num_scalar_prefetch=1,
            grid=(1 + turns,),
            in_specs=[
                pl.BlockSpec((1, width), lambda j, i: (0, target(i))),
                *[once_spec(piece) for piece in pieces],
                placed,
                once_spec(squares),
                turned,
                once_spec(step_sums),
                pl.BlockSpec((width, state), lambda j, i: (target(i), turns + wide_turn(j))),
                pl.BlockSpec((width, state), lambda j, i: (target(i), 0)),
                pl.BlockSpec((heads, width), lambda j, i: (0, target(i))),
                pl.BlockSpec((taps.shape[0], state), lambda j, i: (0, any_turn(j))),
                once_spec(bias),
                once_spec(rate),
            ],
            out_specs=out_specs,
            scratch_shapes=[
                pltpu.VMEM((total_rows, LANES), F32),
                pltpu.VMEM((total_rows, width), BF16),
                pltpu.VMEM((total_rows, state), BF16),
                pltpu.VMEM((rows + 8, state), F32),
                pltpu.VMEM((rows, state), BF16),
                pltpu.VMEM((rows, heads), F32),
                pltpu.VMEM((8, heads), F32),
            ],
        ),
        input_output_aliases={2 + len(pieces): 0},
        compiler_params=granted(60),
        name="enter",
    )(
        index, gain, *pieces, scaled, squares, sums, step_sums, wide, narrow, steps, taps, bias,
        rate,
    )


def inside(
    half, scaled, scale, lead, wide, narrow, taps, skip, conv, step, cum, scores, inner, state,
    size,
):
    total_rows, model = scaled.shape
    rows = total_rows - lead
    heads = step.shape[1]
    width = inner // heads
    groups = state // size
    turns = inner // state // 2
    turn_heads = heads // turns // 2
    blocks = rows // SPAN
    lone = 1 if scores is None else 0

    def body(scaled_ref, scale_ref, wide_ref, skip_ref, conv_ref, x_ref, step_ref, cum_ref, *refs):
        if lone:
            narrow_ref, taps_ref, out_ref, gate_ref, scores_ref, maps_ref, rows_ref, padded_ref = refs
        else:
            scores_ref, out_ref, gate_ref, rows_ref = refs
        turn = pl.program_id(0)

        @pl.when(turn == 0)
        def _():
            if lone:
                raw = (dot(scaled_ref[...], narrow_ref[...]) * scale_ref[:, 0:1]).astype(BF16)
                rows_in(padded_ref, raw, lead)
            for b in range(blocks):
                here = slice(b * SPAN, (b + 1) * SPAN)
                padding = jnp.zeros((SPAN, SPAN - heads), F32)
                rows_ref[b] = jnp.concatenate([cum_ref[here, :], padding], axis=1).T
                if not lone:
                    continue
                maps_ref[here, :] = conv_block(padded_ref, b * SPAN, taps_ref, slice(0, state))
                for g in range(groups):
                    cols = slice(g * size, (g + 1) * size)
                    scores_ref[b, g] = dot(maps_ref[here, cols], conv_ref[here, cols], ((1,), (1,)))

        row = lax.broadcasted_iota(jnp.int32, (SPAN, SPAN), 0)
        col = lax.broadcasted_iota(jnp.int32, (SPAN, SPAN), 1)
        causal = row >= col
        lane = lax.broadcasted_iota(jnp.int32, (SPAN, 2 * width), 1)
        for k in range(turns):

            @pl.when(turn == lone + k)
            def _():
                raw = dot(scaled_ref[lead:, :], wide_ref[...]) * scale_ref[lead:, 0:1]
                gate_ref[...] = raw.astype(BF16)
                first = (half * turns + k) * turn_heads
                expand = expander(heads, width, first, turn_heads)
                skips = spread(jnp.broadcast_to(skip_ref[...], (8, heads)), expand, 3)[0:1, :]
                for b in range(blocks):
                    here = slice(b * SPAN, (b + 1) * SPAN)
                    steps = spread(step_ref[here, :], expand)
                    cum = cum_ref[here, :]
                    for pair in range(turn_heads // 2):
                        head = first + 2 * pair
                        scores_here = scores_ref[b, head * groups // heads]
                        cols = slice(2 * pair * width, (2 * pair + 2) * width)
                        x = x_ref[here, cols].astype(F32)
                        stepped = x * steps[:, cols]
                        weighted = []
                        for h in (head, head + 1):
                            gap = cum[:, h : h + 1] - rows_ref[b, h : h + 1, :]
                            decay = jnp.exp(jnp.where(causal, gap, -1e30))
                            weighted.append((scores_here * decay).astype(BF16))
                        stacked = jnp.concatenate(
                            [
                                jnp.where(lane < width, stepped, 0.0).astype(BF16),
                                jnp.where(lane < width, 0.0, stepped).astype(BF16),
                            ],
                            axis=0,
                        )
                        out = dot(jnp.concatenate(weighted, axis=1), stacked)
                        out_ref[here, cols] = out + skips[:, cols] * x

    def own_turn(j):
        return jnp.maximum(j - lone, 0)

    def wide_turn(j):
        return half * turns + own_turn(j)

    shape = jax.ShapeDtypeStruct
    score_shape = shape((blocks, groups, SPAN, SPAN), F32)
    maps_shape = shape((rows, state), BF16)
    outs = [shape((rows, inner // 2), F32), shape((rows, inner // 2), BF16)]
    turned = pl.BlockSpec((rows, state), lambda j: (0, own_turn(j)))
    scratch = [pltpu.VMEM((blocks, SPAN, SPAN), F32)]
    if lone:
        outs += [score_shape, maps_shape]
        more = (narrow, taps)
        more_specs = [
            pl.BlockSpec((model, state), lambda j: (0, 1), pipeline_mode=pl.Buffered(1)),
            once_spec(taps),
        ]
        scratch.append(pltpu.VMEM((rows + 8, state), F32))
    else:
        more, more_specs = (scores,), [once_spec(scores)]
    maps_at = inner // state
    return pl.pallas_call(
        body,
        grid=(lone + turns,),
        out_shape=outs,
        in_specs=[
            once_spec(scaled),
            once_spec(scale),
            pl.BlockSpec((model, state), lambda j: (0, wide_turn(j))),
            once_spec(skip),
            pl.BlockSpec((rows, state), lambda j: (0, maps_at), pipeline_mode=pl.Buffered(1)),
            pl.BlockSpec((rows, state), lambda j: (0, wide_turn(j))),
            once_spec(step),
            once_spec(cum),
        ]
        + more_specs,
        out_specs=[turned, turned] + [whole_spec(a) for a in outs[2:]],
        scratch_shapes=scratch,
        compiler_params=granted(60),
        name="inside",
    )(scaled, scale, wide, skip, conv, conv, step, cum, *more)


def log_rows(log):
    row = lax.broadcasted_iota(jnp.int32, (TAIL, log.shape[1]), 0)
    block = jnp.zeros((TAIL, log.shape[1]), F32)
    for k, part in enumerate(parts_of(log, 3)):
        block = jnp.where(row == k, part.astype(F32), block)
    return block.astype(BF16)


def log_of(message_ref, size):
    rows = message_ref[size : size + TAIL, :].astype(F32)
    return rows[0:1, :] + rows[1:2, :] + rows[2:3, :]


def combine_body(size, first):
    def body(later_ref, mine_ref, came_ref, *refs):
        if first:
            out_ref, before_ref, before_log_ref = refs
        else:
            prior_ref, prior_log_ref, out_ref, before_ref, before_log_ref = refs
        mine = mine_ref[0:size, :].astype(F32)
        came = came_ref[0:size, :].astype(F32)
        my_log, came_log = log_of(mine_ref, size), log_of(came_ref, size)

        @pl.when(later_ref[0] == 1)
        def _():
            out_ref[0:size, :] = (jnp.exp(my_log) * came + mine).astype(BF16)
            if first:
                before_ref[...] = came
                before_log_ref[0:1, :] = came_log
            else:
                before_ref[...] = jnp.exp(prior_log_ref[0:1, :]) * came + prior_ref[...]
                before_log_ref[0:1, :] = prior_log_ref[0:1, :] + came_log

        @pl.when(later_ref[0] == 0)
        def _():
            out_ref[0:size, :] = (jnp.exp(came_log) * mine + came).astype(BF16)
            if first:
                before_ref[...] = jnp.zeros_like(before_ref)
                before_log_ref[0:1, :] = jnp.zeros_like(came_log)
            else:
                before_ref[...] = prior_ref[...]
                before_log_ref[0:1, :] = prior_log_ref[0:1, :]

        out_ref[size : size + TAIL, :] = log_rows(my_log + came_log)

    return body


def finish(
    part, parts, index, later, entering, update, block_log, cum, maps, halves, gain, out_weight,
    inner, state, heads, groups, count,
):
    size = state // groups
    width = inner // heads
    rows = cum.shape[0] // parts
    last_part = part == parts - 1
    blocks = rows // SPAN
    model = out_weight.shape[1]
    turn_width = model // count
    first = len(entering) > 1

    def body(index_ref, later_ref, *refs):
        entering_refs, refs = refs[: len(entering)], refs[len(entering) :]
        update_ref, block_log_ref, cum_ref, maps_ref, *refs = refs
        half_refs, refs = (refs[0:2], refs[2:4]), refs[4:]
        gain_ref, weight_ref, top_ref, bottom_ref, mixed_ref, *memory_out = refs

        def both(k, here, cols):
            split = inner // 2
            pieces = []
            for h in range(2):
                low, high = max(cols.start, h * split), min(cols.stop, (h + 1) * split)
                if low < high:
                    pieces.append(half_refs[h][k][here, low - h * split : high - h * split])
            return pieces[0] if len(pieces) == 1 else jnp.concatenate(pieces, axis=1)

        @pl.when(pl.program_id(0) == 0)
        def _():
            expand = expander(heads, width)
            if first:
                came_ref, before_ref, before_log_ref, start_ref = entering_refs
                is_later = later_ref[0] == 1
                prior_log = before_log_ref[0:1, :]
                prior = before_ref[...]
                came = came_ref[0:size, :].astype(F32)
                came_log = log_of(came_ref, size)
                memory = jnp.where(is_later, jnp.exp(prior_log) * came + prior, prior)
                memory_log = jnp.where(is_later, prior_log + came_log, prior_log)
                memory = jnp.exp(memory_log) * start_ref[...].T + memory
            else:
                memory = entering_refs[0][...]
            keep = jnp.exp(spread(block_log_ref[...], expand, 3))
            for b in range(blocks):
                here = slice(b * SPAN, (b + 1) * SPAN)
                reach = spread(jnp.exp(cum_ref[here, :]), expand)
                for g in range(groups):
                    cols = slice(g * inner // groups, (g + 1) * inner // groups)
                    carried = dot(
                        maps_ref[here, g * size : (g + 1) * size], memory[:, cols].astype(BF16)
                    )
                    scan = both(0, here, cols) + reach[:, cols] * carried
                    gate = both(1, here, cols)
                    gated = scan * silu(gate.astype(F32))
                    moment = jnp.mean(gated * gated, axis=-1, keepdims=True)
                    mixed_ref[here, cols] = (
                        gated * lax.rsqrt(moment + EPSILON) * gain_ref[:, cols].astype(F32)
                    ).astype(BF16)
                if not last_part or b < blocks - 1:
                    at = part * blocks + b
                    memory = keep[at : at + 1, :] * memory + update_ref[b]
            if memory_out:
                memory_out[0][...] = memory

        sent = dot(mixed_ref[...], weight_ref[...]).astype(BF16)

        @pl.when(pl.program_id(0) == 0)
        def _():
            top_ref[...] = sent

        @pl.when(pl.program_id(0) == 1)
        def _():
            bottom_ref[...] = sent

    def rows_of(array):
        once = pl.Buffered(1)
        return pl.BlockSpec((rows, array.shape[1]), lambda *_: (part, 0), pipeline_mode=once)

    shape = jax.ShapeDtypeStruct
    extra = [shape((rows, turn_width), BF16)] * 2 + [shape((rows, inner), BF16)]
    extra += [] if last_part else [shape((size, inner), F32)]

    return pl.pallas_call(
        body,
        out_shape=extra,
        grid_spec=pltpu.PrefetchScalarGridSpec(
            num_scalar_prefetch=2,
            grid=(2,),
            in_specs=[once_spec(a) for a in entering]
            + [
                pl.BlockSpec((blocks, size, inner), lambda *_: (part, 0, 0)),
                once_spec(block_log),
                rows_of(cum),
                rows_of(maps),
            ]
            + [rows_of(a) for half in halves for a in half]
            + [
                once_spec(gain),
                pl.BlockSpec((inner, turn_width), lambda j, *_: (0, (1 - j) * (count - 1))),
            ],
            out_specs=[whole_spec(a) for a in extra],
        ),
        compiler_params=granted(60),
        name="finish",
    )(
        index, later, *entering, update, block_log, cum, maps, *halves[0], *halves[1], gain,
        out_weight,
    )


def project_out(mixed, out_weight, count):
    rows, inner = mixed.shape
    model = out_weight.shape[1]
    width = model // count

    def body(mixed_ref, weight_ref, out_ref):
        out_ref[...] = dot(mixed_ref[...], weight_ref[...]).astype(BF16)

    return pl.pallas_call(
        body,
        grid=(count,),
        out_shape=jax.ShapeDtypeStruct((rows, model), BF16),
        in_specs=[once_spec(mixed), pl.BlockSpec((inner, width), lambda j: (0, j))],
        out_specs=pl.BlockSpec((rows, width), lambda j: (0, j)),
        compiler_params=granted(12),
        name="project_out",
    )(mixed, out_weight)


def relay(index, distance, partial, received, count):
    rows, model = partial.shape
    width = model // count

    def body(index_ref, ahead_ref, behind_ref, *refs):
        for own, came, out in zip((ahead_ref, behind_ref), refs[:-2], refs[-2:]):
            out[...] = (own[...].astype(F32) + came[...].astype(F32)).astype(BF16)

    def place(sign):
        return lambda j, i: (j, jnp.clip(i[0] + sign * distance, 0, count - 1))

    turns = 4
    whole = pl.BlockSpec((rows // turns, width), lambda j, i: (j, 0))
    shape = jax.ShapeDtypeStruct((rows, width), BF16)
    return pl.pallas_call(
        body,
        out_shape=[shape, shape],
        grid_spec=pltpu.PrefetchScalarGridSpec(
            num_scalar_prefetch=1,
            grid=(turns,),
            in_specs=[
                pl.BlockSpec((rows // turns, width), place(1)),
                pl.BlockSpec((rows // turns, width), place(-1)),
                whole,
                whole,
            ],
            out_specs=[whole, whole],
        ),
        compiler_params=granted(8),
        name="relay",
    )(index, partial, partial, *received)


def send_on(ahead, behind, distance, axis):
    count = lax.axis_size(axis)
    return (
        lax.ppermute(ahead, axis, [(i, i + 1) for i in range(count - distance)]),
        lax.ppermute(behind, axis, [(i, i - 1) for i in range(distance, count)]),
    )


def total(index, partial, received, hidden, row_block, count, filled):
    rows, model = partial.shape
    width = model // count
    turns = 2

    def body(index_ref, own_ref, ahead_ref, behind_ref, hidden_ref, *refs):
        summed = own_ref[...].astype(F32) + ahead_ref[...].astype(F32)
        summed = summed + behind_ref[...].astype(F32)
        refs[-1][...] = (summed + hidden_ref[...].astype(F32)).astype(BF16)

    block = (rows // turns, width)
    whole = pl.BlockSpec(block, lambda j, i: (j, 0))
    placed = pl.BlockSpec(block, lambda j, i: (row_block * turns + j, 0))
    return pl.pallas_call(
        body,
        out_shape=jax.ShapeDtypeStruct(hidden.shape, BF16),
        grid_spec=pltpu.PrefetchScalarGridSpec(
            num_scalar_prefetch=1,
            grid=(turns,),
            in_specs=[pl.BlockSpec(block, lambda j, i: (j, i[0])), whole, whole, placed]
            + [pl.BlockSpec(memory_space=pl.ANY)] * len(filled),
            out_specs=placed,
        ),
        input_output_aliases={5: 0} if filled else {},
        compiler_params=granted(8),
        name="total",
    )(index, partial, *received, hidden, *filled)


def on_device(
    hidden, norm_gain, gate_x_weight, state_weight, step_weight, conv_inner, conv_state,
    step_bias, decay_log, skip_gain, inner_gain, out_weight, initial_state,
):
    rows = hidden.shape[0]
    half = rows // 2
    inner = gate_x_weight.shape[2]
    state = state_weight.shape[2]
    heads = step_weight.shape[1]
    size = initial_state.shape[2]
    groups = state // size
    blocks = rows // SPAN
    feature_index = lax.axis_index("tp").reshape(1)
    range_index = lax.axis_index("seq")
    ranges = lax.axis_size("seq")

    model = step_weight.shape[0]
    parts_count = lax.axis_size("tp")
    narrow_weight = state_weight.reshape(model, 2 * state)
    step_rows = step_weight.T
    taps = jnp.concatenate([conv_inner, conv_state[:, 0]], axis=1)
    out_taps = conv_state[:, 1]
    start_state = initial_state.reshape(inner, size)
    gain = norm_gain.astype(F32)[None, :]
    out_gain = inner_gain[None, :]
    bias, rate, skip = step_bias[None, :], decay_log[None, :], skip_gain[None, :]

    halo = shifted(hidden[rows - TAIL :], "seq", 1)
    early = line_step([jnp.concatenate([halo, hidden[:half]], axis=0)] * 2, 1, "tp")[1:]
    late = line_step([hidden[half:]] * 2, 1, "tp")[1:]
    small = (narrow_weight, step_rows, taps, start_state, gain, out_gain)
    late[1:], small = lax.optimization_barrier((late[1:], small))
    narrow_weight, step_rows, taps, start_state, gain, out_gain = small
    wide = gate_x_weight.reshape(model, 2 * inner)
    for step in range(2, parts_count):
        early, late = line_step(early, step, "tp"), line_step(late, step, "tp")
        if step == 2:
            early[1:], late[1:], wide = lax.optimization_barrier((early[1:], late[1:], wide))

    shape = jax.ShapeDtypeStruct
    weights = (feature_index, gain, wide, narrow_weight, step_rows)
    begun = begin((early[:-2], late[:-2]), *weights, inner, state)
    last, begun = lax.optimization_barrier((early[-2:] + late[-2:], begun))
    scaled, scale, conv, step, cum, update, block_log, message = enter(
        begun, last, TAIL, *weights, taps, bias, rate, inner, state, size
    )

    def within(half, scores):
        return inside(
            half, scaled, scale, TAIL, wide, narrow_weight, out_taps, skip, conv, step, cum, scores,
            inner, state, size,
        )

    *first_half, scores, maps = within(0, None)
    second_half = within(1, scores)
    before = ()
    bit = 1
    while True:
        came = swapped(message, "seq", bit)
        if bit == 2:
            held = lax.optimization_barrier((came, first_half, scores, maps))
            came, first_half, scores, maps = held
            second_half = within(1, scores)
        later = ((range_index // bit) % 2).astype(jnp.int32).reshape(1)
        bit *= 2
        if bit == ranges:
            break
        message, *before = call(
            combine_body(size, not before),
            [
                shape((size + TAIL, inner), BF16),
                shape((size, inner), F32),
                shape((8, inner), F32),
            ],
            later,
            message,
            came,
            *before,
            scalars=1,
            name="combine",
            limit=14,
        )
    entering = (came, *before, start_state)
    partials, received = [], []
    halves = (first_half, second_half)
    for part in range(2):
        top, bottom, mixed, *entering = finish(
            part, 2, feature_index, later, entering, update, block_log, cum, maps, halves,
            out_gain, out_weight, inner, state, heads, groups, parts_count,
        )
        partials.append(mixed)
        received.append(send_on(top, bottom, parts_count - 1, "tp"))
    onward = ()
    for distance in range(parts_count - 2, 0, -1):
        for k in range(2):
            if distance == parts_count - 2:
                mixed, _ = lax.optimization_barrier((partials[k], onward))
                partials[k] = project_out(mixed, out_weight, parts_count)
            onward = relay(feature_index, distance, partials[k], received[k], parts_count)
            received[k] = send_on(*onward, distance, "tp")
    filled = ()
    for k, partial in enumerate(partials):
        filled = (
            total(feature_index, partial, received[k], hidden, k, parts_count, filled),
        )
    return filled[0]


def solution(mesh):
    return jax.shard_map(
        on_device,
        mesh=mesh,
        in_specs=(
            P("seq", "tp"),
            P(),
            P(None, None, "tp"),
            P(None, None, "tp"),
            P(None, "tp"),
            P(None, "tp"),
            P(None, None, "tp"),
            P("tp"),
            P("tp"),
            P("tp"),
            P("tp"),
            P("tp", None),
            P("tp", None, None),
        ),
        out_specs=P("seq", "tp"),
        check_vma=False,
    )
```
